256 devices in a mesh: seq: 32 (over z, x), heads: 8 (over y, core).
Axes of the slice: x: 4, y: 4, z: 8, core: 2. Of those that a mesh axis runs over, the one named last changes fastest.
Arguments:
- lin_q: bfloat16 [8192, 8192], P('seq', 'heads'), may hold values from -4 to 4
- lin_k: bfloat16 [8192, 8192], P('seq', 'heads'), may hold values from -4 to 4
- lin_v: bfloat16 [8192, 8192], P('seq', 'heads'), may hold values from -6 to 6
- decay_rates: float32 [64], P('heads'), may hold values from 3.0517578e-05 to 0.03125
- norm_gain: float32 [8192], P('heads'), may hold values from 0.25 to 1.75
- soft_q: bfloat16 [8192, 8192], P('seq', 'heads'), may hold values from -8 to 8
- soft_k: bfloat16 [8192, 1024], P('seq', 'heads'), may hold values from -8 to 8
- soft_v: bfloat16 [8192, 1024], P('seq', 'heads'), may hold values from -6 to 6
- segment_ids: int32 [8192], P('seq'), may hold values from 0 to 3, never falling along the last dimension, each value on 1 to 6144 neighbouring positions
Outputs:
- lin_out: bfloat16 [8192, 8192], P('seq', 'heads')
- soft_out: bfloat16 [8192, 8192], P('seq', 'heads')
The draws below stay inside these ranges and needn't reach their ends.
Inputs may be any that keep to these rules, and one draw needn't show every extreme that they name: `segment_ids`: never falling along the sequence; each document has 1 to 6144 tokens, one exactly that many.
All inputs are finite; a program needn't handle non-finite values.
Results may differ from the reference program's by a relative error of at most 0.0049.
Values may be sent and summed in bfloat16 or wider, within the bound.
A program may use at most 128 MiB of HBM per device.

```python
import math
import jax
import jax.numpy as jnp
import numpy as np
from jax import lax

HD = 128
HEADS = 64
KV_HEADS = 8
TOKENS = 8192
BLOCK = 256


def drawn_pair(key):
    shape_q = (TOKENS, HEADS, HD)
    shape_k = (TOKENS, KV_HEADS, HD)
    key_q = jax.random.fold_in(key, 101)
    key_k = jax.random.fold_in(key, 202)
    soft_q = jnp.clip(jax.random.normal(key_q, shape_q, jnp.float32), -6.0, 6.0)
    soft_k = jnp.clip(jax.random.normal(key_k, shape_k, jnp.float32), -6.0, 6.0)
    return (soft_q.reshape(TOKENS, HEADS * HD), soft_k.reshape(TOKENS, KV_HEADS * HD))


def draw_soft_q(key, part):
    return drawn_pair(key)[0].astype(jnp.bfloat16)


def draw_soft_k(key, part):
    return drawn_pair(key)[1].astype(jnp.bfloat16)


def steps_of(rng, extent, cuts, low, top_value):
    gain = 1.0
    for dim, blocks in cuts:
        heights = jax.random.uniform(jax.random.fold_in(jax.random.fold_in(rng, 6), dim), (blocks,), jnp.float32, low / len(cuts), top_value / len(cuts))
        gain = gain * jnp.repeat(jnp.exp(heights), extent[dim] // blocks).reshape((-1,) + (1,) * (len(extent) - 1 - dim))
    return gain


def profile(amount, total, limit, lean):
    loads = [(1 << 20) // math.isqrt(grade ** lean) + 1 for grade in range(2, amount + 1)]
    spare, given = total - limit - (amount - 1), [1] * (amount - 1)
    while spare > 0:
        candidates = [i for i in range(amount - 1) if given[i] < limit]
        mass, remaining = sum([loads[i] for i in candidates]), spare
        for i in candidates:
            more = min(limit - given[i], max(1, remaining * loads[i] // mass), spare)
            given[i] = given[i] + more
            spare = spare - more
    return np.array([limit] + given)


def ragged(stream_key, count, total, bound, lean):
    if count == 2:
        one = jax.random.randint(stream_key, (), max(1, total - bound), min(bound, total - 1) + 1)
        return jnp.stack([one, total - one])
    lengths = jnp.asarray(profile(count, total, bound, lean), jnp.int32)
    pairs = (count - 1) // 2
    source_of, taker = lengths[1:1 + 2 * pairs:2], lengths[2:2 + 2 * pairs:2]
    slack = jnp.minimum(source_of - 1, bound - taker)
    shifted = jax.random.randint(jax.random.fold_in(stream_key, 1), (pairs,), 0, 1 << 20) % (slack + 1)
    lengths = lengths.at[1:1 + 2 * pairs:2].set(source_of - shifted).at[2:2 + 2 * pairs:2].set(taker + shifted)
    return lengths[jax.random.permutation(jax.random.fold_in(stream_key, 2), count)]


def bell_draw(stream_key, shape, scale, reach, pieces=(), kind=jnp.bfloat16):
    level = steps_of(stream_key, shape, pieces, -0.22, 0.18) if pieces else 1.0
    entries = jax.random.normal(stream_key, shape, jnp.float32) * scale * level
    return jnp.minimum(jnp.maximum(entries, -reach), reach).astype(kind)


def setup_inputs(seed: int = 0) -> dict:
    key_list = jax.random.split(jax.random.key(seed), 10)
    lin_q = bell_draw(key_list[0], (TOKENS, HEADS * HD), 0.3, 4.0, ((0, 32), (1, 8)))
    lin_k = bell_draw(key_list[1], (TOKENS, HEADS * HD), 0.3, 4.0, ((0, 32), (1, 8)))
    lin_v = bell_draw(key_list[2], (TOKENS, HEADS * HD), 1.0, 6.0, ((0, 32), (1, 8)))
    decay_rates = jnp.clip(jnp.exp(math.log(0.03125) - 6.931472 * jax.random.uniform(key_list[3], (HEADS,), jnp.float32) ** steps_of(key_list[3], (HEADS,), ((0, 8),), -0.2, 0.2)), 3.0517578125e-05, 0.03125)
    norm_gain = jnp.clip(1.0 + 0.15 * jax.random.normal(key_list[4], (HEADS * HD,), jnp.float32), 0.25, 1.75)
    soft_q = draw_soft_q(jax.random.fold_in(key_list[9], 71), 0)
    soft_k = draw_soft_k(jax.random.fold_in(key_list[9], 71), 0)
    soft_v = bell_draw(key_list[7], (TOKENS, KV_HEADS * HD), 1.0, 6.0, ((0, 32), (1, 8)))
    segment_ids = jnp.searchsorted(jnp.cumsum(ragged(key_list[8], 4, TOKENS, 3 * TOKENS // 4, 2)), jnp.arange(TOKENS), side="right").astype(jnp.int32)
    return dict(lin_q=lin_q, lin_k=lin_k, lin_v=lin_v, decay_rates=decay_rates, norm_gain=norm_gain, soft_q=soft_q, soft_k=soft_k, soft_v=soft_v, segment_ids=segment_ids)


def light_block(carry, inputs, rates):
    state, last_prev = carry
    q_blk, k_blk, v_blk, seg_blk = inputs
    size = q_blk.shape[0]
    seg_f = seg_blk.astype(jnp.float32)
    pos = jnp.arange(size).astype(jnp.float32)
    diff = pos[:, None] - pos[None, :]
    linked = (diff >= 0.0) & (seg_f[:, None] == seg_f[None, :])
    decay = jnp.exp(-rates[:, None, None] * jnp.maximum(diff, 0.0)[None])
    scores = jnp.einsum('thd,shd->hts', q_blk, k_blk, preferred_element_type=jnp.float32)
    weights = jnp.where(linked[None], scores * decay, 0.0).astype(jnp.bfloat16)
    intra = jnp.einsum('hts,shd->thd', weights, v_blk, preferred_element_type=jnp.float32)
    use = (seg_f == last_prev).astype(jnp.float32)
    coef = jnp.exp(-rates[None, :] * (pos[:, None] + 1.0)) * use[:, None]
    q_state = jnp.einsum('thd,hde->the', q_blk.astype(jnp.float32), state, precision=lax.Precision.HIGHEST)
    out = intra + coef[:, :, None] * q_state
    last = seg_f[-1]
    k_weight = jnp.exp(-rates[None, :] * (size - 1.0 - pos[:, None])) * (seg_f == last).astype(jnp.float32)[:, None]
    k_dec = (k_blk.astype(jnp.float32) * k_weight[:, :, None]).astype(jnp.bfloat16)
    local = jnp.einsum('shd,she->hde', k_dec, v_blk, preferred_element_type=jnp.float32)
    keep = jnp.where(last == last_prev, 1.0, 0.0) * jnp.exp(-rates * size)
    return ((keep[:, None, None] * state + local, last), out)

def soft_head(q_h, k_h, v_h, seg):
    total = q_h.shape[0]
    rows = math.gcd(total, 1024)
    kpos = jnp.arange(total)
    scale = 1.0 / math.sqrt(q_h.shape[1])

    def one(start):
        qb = lax.dynamic_slice_in_dim(q_h, start, rows, 0)
        sb = lax.dynamic_slice_in_dim(seg, start, rows, 0)
        qpos = start + jnp.arange(rows)
        s = jnp.dot(qb, k_h.T, preferred_element_type=jnp.float32) * scale
        mask = (kpos[None, :] <= qpos[:, None]) & (seg[None, :] == sb[:, None])
        mx = lax.optimization_barrier(jnp.max(jnp.where(mask, s, -1e+30), axis=1))
        p = jnp.where(mask, jnp.exp(s - mx[:, None]), 0.0)
        den = lax.optimization_barrier(jnp.sum(p, axis=1))
        pv = jnp.dot(p.astype(jnp.bfloat16), v_h, preferred_element_type=jnp.float32)
        return (pv / den[:, None]).astype(jnp.bfloat16)
    starts = (jnp.arange(total // rows) * rows).astype(jnp.int32)
    return lax.map(one, starts).reshape(total, -1)

def reference(lin_q, lin_k, lin_v, decay_rates, norm_gain, soft_q, soft_k, soft_v, segment_ids):
    total = lin_q.shape[0]
    heads = decay_rates.shape[0]
    width = lin_q.shape[1] // heads
    blocks = total // BLOCK
    shape4 = (blocks, BLOCK, heads, width)
    init = (jnp.zeros((heads, width, width), jnp.float32), jnp.float32(-1.0))
    fn = lambda c, x: light_block(c, x, decay_rates)
    _, outs = lax.scan(fn, init, (lin_q.reshape(shape4), lin_k.reshape(shape4), lin_v.reshape(shape4), segment_ids.reshape(blocks, BLOCK)))
    raw = outs.reshape(total, heads * width)
    mean_sq = lax.optimization_barrier(jnp.mean(raw * raw, axis=1))
    lin_out = (raw * lax.rsqrt(mean_sq + 1e-06)[:, None] * norm_gain[None, :]).astype(jnp.bfloat16)
    shared_heads = soft_k.shape[1] // width
    group = heads // shared_heads
    qh = soft_q.reshape(total, heads, width).transpose(1, 0, 2)
    kh = soft_k.reshape(total, shared_heads, width).transpose(1, 0, 2)
    vh = soft_v.reshape(total, shared_heads, width).transpose(1, 0, 2)

    def per_head(index):
        shared = index // group
        return soft_head(qh[index], kh[shared], vh[shared], segment_ids)
    outputs = lax.map(per_head, jnp.arange(heads).astype(jnp.int32))
    soft_out = outputs.transpose(1, 0, 2).reshape(total, heads * width)
    return (lin_out, soft_out)
```

```python
from functools import partial
import math

import jax
import jax.numpy as jnp
from jax import lax
from jax.sharding import PartitionSpec as P

BLOCK = 256


def carried_in(part, axis, combine, identity):
    place = lax.axis_index(axis)
    size = lax.axis_size(axis)
    ident = jax.tree.map(lambda a, e: jnp.zeros_like(a) + jnp.asarray(e, a.dtype), part, identity)
    shifted = jax.tree.map(
        lambda a: lax.ppermute(a, axis, [(i, i + 1) for i in range(size - 1)]), part
    )
    state = jax.tree.map(lambda s, e: jnp.where(place == 0, e, s), shifted, ident)
    step = 1
    while step < size:
        pairs = [(i, i + step) for i in range(size - step)]
        earlier = jax.tree.map(lambda a: lax.ppermute(a, axis, pairs), state)
        merged = combine(earlier, state)
        state = jax.tree.map(lambda m, s: jnp.where(place >= step, m, s), merged, state)
        step *= 2
    return state


def light_block(carry, inputs, rates):
    state, last_prev = carry
    q_blk, k_blk, v_blk, seg_blk = inputs
    size = q_blk.shape[0]
    seg_f = seg_blk.astype(jnp.float32)
    pos = jnp.arange(size).astype(jnp.float32)
    diff = pos[:, None] - pos[None, :]
    linked = (diff >= 0.0) & (seg_f[:, None] == seg_f[None, :])
    decay = jnp.exp(-rates[:, None, None] * jnp.maximum(diff, 0.0)[None])
    scores = jnp.einsum("thd,shd->hts", q_blk, k_blk, preferred_element_type=jnp.float32)
    weights = jnp.where(linked[None], scores * decay, 0.0).astype(jnp.bfloat16)
    intra = jnp.einsum("hts,shd->thd", weights, v_blk, preferred_element_type=jnp.float32)
    use = (seg_f == last_prev).astype(jnp.float32)
    coef = jnp.exp(-rates[None, :] * (pos[:, None] + 1.0)) * use[:, None]
    q_state = jnp.einsum(
        "thd,hde->the", q_blk.astype(jnp.float32), state, precision=lax.Precision.HIGHEST
    )
    out = intra + coef[:, :, None] * q_state
    last = seg_f[-1]
    k_weight = (
        jnp.exp(-rates[None, :] * (size - 1.0 - pos[:, None]))
        * (seg_f == last).astype(jnp.float32)[:, None]
    )
    k_dec = (k_blk.astype(jnp.float32) * k_weight[:, :, None]).astype(jnp.bfloat16)
    local = jnp.einsum("shd,she->hde", k_dec, v_blk, preferred_element_type=jnp.float32)
    keep = jnp.where(last == last_prev, 1.0, 0.0) * jnp.exp(-rates * size)
    return ((keep[:, None, None] * state + local, last), out)


def combine_states(earlier, later):
    state_e, dec_e, last_e = earlier
    state_l, dec_l, last_l = later
    match = (last_e == last_l) | (last_l < 0.0)
    factor = jnp.where(match, dec_l, 0.0)
    return (factor[:, None, None] * state_e + state_l, dec_e * dec_l, jnp.maximum(last_e, last_l))


def block_update(inner, queries, qpos, seg_rows, k_blk, v_blk, s_blk, kpos, scale):
    mx, den, acc = inner
    shared_heads = k_blk.shape[1]
    group = queries.shape[2]
    query_count = queries.shape[0]
    key_count = k_blk.shape[0]
    heads = shared_heads * group
    s = (
        jnp.einsum("tgjd,sgd->gjts", queries, k_blk, preferred_element_type=jnp.float32).reshape(
            heads, query_count, key_count
        )
        * scale
    )
    mask = (kpos[None, :] <= qpos[:, None]) & (s_blk[None, :] == seg_rows[:, None])
    top = jnp.max(jnp.where(mask[None], s, -1e30), axis=2)
    new_mx = jnp.maximum(mx, top)
    corr = jnp.exp(mx - new_mx)
    p = jnp.where(mask[None], jnp.exp(s - new_mx[:, :, None]), 0.0)
    den = den * corr + jnp.sum(p, axis=2)
    weights = p.astype(jnp.bfloat16).reshape(shared_heads, group, query_count, key_count)
    mixed = jnp.einsum(
        "gjts,sgd->gjtd", weights, v_blk, preferred_element_type=jnp.float32
    ).reshape(heads, query_count, -1)
    acc = acc * corr[:, :, None] + mixed
    return (new_mx, den, acc)


def body(lin_q, lin_k, lin_v, decay_rates, norm_gain, soft_q, soft_k, soft_v, segment_ids):
    tok = lin_q.shape[0]
    heads = decay_rates.shape[0]
    width = lin_q.shape[1] // heads
    blocks = tok // BLOCK
    shape4 = (blocks, BLOCK, heads, width)
    init = (jnp.zeros((heads, width, width), jnp.float32), jnp.float32(-1.0))
    step_fn = lambda c, x: light_block(c, x, decay_rates)
    (state_loc, last_loc), outs = lax.scan(
        step_fn,
        init,
        (
            lin_q.reshape(shape4),
            lin_k.reshape(shape4),
            lin_v.reshape(shape4),
            segment_ids.reshape(blocks, BLOCK),
        ),
    )
    local_out = outs.reshape(tok, heads, width)
    summary = (state_loc, jnp.exp(-decay_rates * tok), last_loc.reshape(1))
    identity = (
        jnp.zeros((heads, width, width), jnp.float32),
        jnp.ones((heads,), jnp.float32),
        jnp.full((1,), -1.0, jnp.float32),
    )
    state_in, dec_in, last_in = carried_in(summary, "seq", combine_states, identity)
    seg_f = segment_ids.astype(jnp.float32)
    pos = jnp.arange(tok).astype(jnp.float32)
    coef = (
        jnp.exp(-decay_rates[None, :] * (pos[:, None] + 1.0))
        * (seg_f == last_in[0]).astype(jnp.float32)[:, None]
    )
    q_three = lin_q.reshape(tok, heads, width)
    q_state = jnp.einsum(
        "thd,hde->the", q_three.astype(jnp.float32), state_in, precision=lax.Precision.HIGHEST
    )
    raw = (local_out + coef[:, :, None] * q_state).reshape(tok, heads * width)
    sums = jnp.sum(raw * raw, axis=1)
    total_sq = lax.psum(sums, "heads")
    count = lax.axis_size("heads") * heads * width
    lin_out = (raw * lax.rsqrt(total_sq / count + 1e-06)[:, None] * norm_gain[None, :]).astype(
        jnp.bfloat16
    )
    scale = 1.0 / math.sqrt(width)
    shared_heads = soft_k.shape[1] // width
    group = heads // shared_heads
    mine = lax.axis_index("seq")
    plans = (soft_q, segment_ids, mine * tok)
    query_sets = []
    query_rows, seg_rows, first = plans
    count_rows = query_rows.shape[0]
    query_sets.append(
        (
            query_rows.reshape(count_rows, shared_heads, group, width),
            first + jnp.arange(count_rows),
            seg_rows,
            first + count_rows - 1,
        )
    )
    start_carry = tuple(
        (
            (
                jnp.full((heads, qs[0].shape[0]), -1e30, jnp.float32),
                jnp.zeros((heads, qs[0].shape[0]), jnp.float32),
                jnp.zeros((heads, qs[0].shape[0], width), jnp.float32),
            )
            for qs in query_sets
        )
    )
    carry = start_carry
    keys = lax.all_gather(soft_k, "seq", axis=0, tiled=True)
    values = lax.all_gather(soft_v, "seq", axis=0, tiled=True)
    seg_keys = lax.all_gather(segment_ids, "seq", axis=0, tiled=True)
    length = keys.shape[0]
    rows = math.gcd(length, 1024)
    count_blk = length // rows
    k_blocks = keys.reshape(count_blk, rows, shared_heads, width)
    v_blocks = values.reshape(count_blk, rows, shared_heads, width)
    s_blocks = seg_keys.reshape(count_blk, rows)

    def attend_one(state, item):
        k_blk, v_blk, s_blk, index = item
        blk_start = index * rows
        kpos = blk_start + jnp.arange(rows)
        fresh = []
        for query_set, inner in zip(query_sets, state):
            queries, qpos, seg_rows, last_pos = query_set
            update = partial(
                block_update,
                queries=queries,
                qpos=qpos,
                seg_rows=seg_rows,
                k_blk=k_blk,
                v_blk=v_blk,
                s_blk=s_blk,
                kpos=kpos,
                scale=scale,
            )
            inner = update(inner)
            fresh.append(inner)
        return (tuple(fresh), None)

    carry, _ = lax.scan(attend_one, carry, (k_blocks, v_blocks, s_blocks, jnp.arange(count_blk)))
    outputs = []
    for mx, den, acc in carry:
        outputs.append(
            (acc / den[:, :, None])
            .transpose(1, 0, 2)
            .reshape(acc.shape[1], heads * width)
            .astype(jnp.bfloat16)
        )
    soft_out = outputs[0]
    return (lin_out, soft_out)


def solution(mesh):
    placed = (
        P("seq", "heads"),
        P("seq", "heads"),
        P("seq", "heads"),
        P("heads"),
        P("heads"),
        P("seq", "heads"),
        P("seq", "heads"),
        P("seq", "heads"),
        P("seq"),
    )
    return jax.shard_map(
        body,
        mesh=mesh,
        in_specs=placed,
        out_specs=(P("seq", "heads"), P("seq", "heads")),
        check_vma=False,
    )
```

```python
import math

import jax
import jax.numpy as jnp
from jax import lax
from jax.experimental import pallas as pl
from jax.experimental.pallas import tpu as pltpu
from jax.sharding import PartitionSpec as P

BLOCK = 256
KEY_BLOCK = 512


def flash_body(sref, q_ref, k_ref, v_ref, st_ref, o_ref, m_ref, l_ref, acc_ref, *, heads, width, scale):
    j = pl.program_id(0)
    lo, hi, flo, fhi, q0 = sref[0], sref[1], sref[2], sref[3], sref[4]
    rows = q_ref.shape[0]
    kb = k_ref.shape[0]

    @pl.when(j == 0)
    def _():
        m_ref[...] = jnp.full(m_ref.shape, -1e30, jnp.float32)
        l_ref[...] = jnp.zeros(l_ref.shape, jnp.float32)
        acc_ref[...] = jnp.zeros(acc_ref.shape, jnp.float32)

    def step(masked):
        k = k_ref[...]
        v = v_ref[...]
        if masked:
            kpos = j * kb + lax.broadcasted_iota(jnp.int32, (rows, kb), 1)
            qpos = q0 + lax.broadcasted_iota(jnp.int32, (rows, kb), 0)
            valid = (kpos <= qpos) & (kpos >= st_ref[...])
        for h in range(heads):
            q = q_ref[:, h * width:(h + 1) * width]
            s = lax.dot_general(q, k, (((1,), (1,)), ((), ())), preferred_element_type=jnp.float32) * scale
            m_prev = m_ref[h]
            if masked:
                top = jnp.max(jnp.where(valid, s, -1e30), axis=1, keepdims=True)
            else:
                top = jnp.max(s, axis=1, keepdims=True)
            m_new = jnp.maximum(m_prev, top)
            corr = jnp.exp(m_prev - m_new)
            e = jnp.exp(s - m_new)
            p = jnp.where(valid, e, 0.0) if masked else e
            l_ref[h] = l_ref[h] * corr + jnp.sum(p, axis=1, keepdims=True)
            pv = jnp.dot(p.astype(jnp.bfloat16), v, preferred_element_type=jnp.float32)
            acc_ref[h] = acc_ref[h] * corr + pv
            m_ref[h] = m_new

    inside = (j >= lo) & (j <= hi)
    full = (j >= flo) & (j <= fhi)

    @pl.when(inside & full)
    def _():
        step(False)

    @pl.when(inside & jnp.logical_not(full))
    def _():
        step(True)

    @pl.when(j == pl.num_programs(0) - 1)
    def _():
        for h in range(heads):
            o_ref[:, h * width:(h + 1) * width] = (acc_ref[h] / l_ref[h]).astype(o_ref.dtype)


def flash_attention(q, keys, values, starts, q0):
    rows, total = q.shape
    length, width = keys.shape
    heads = total // width
    kb = min(KEY_BLOCK, length)
    nk = length // kb
    scale = 1.0 / math.sqrt(width)
    first = starts[0]
    last_start = starts[rows - 1]
    lo = first // kb
    hi = (q0 + rows - 1) // kb
    flo = (last_start + kb - 1) // kb
    fhi = (q0 + 1) // kb - 1
    sref = jnp.stack([lo, hi, flo, fhi, q0]).astype(jnp.int32)

    def kv_map(j, s):
        return (jnp.minimum(jnp.maximum(j, s[0]), s[1]), 0)

    kernel = lambda *refs: flash_body(*refs, heads=heads, width=width, scale=scale)
    return pl.pallas_call(
        kernel,
        out_shape=jax.ShapeDtypeStruct((rows, total), jnp.bfloat16),
        grid_spec=pltpu.PrefetchScalarGridSpec(
            num_scalar_prefetch=1,
            grid=(nk,),
            in_specs=[
                pl.BlockSpec((rows, total), lambda j, s: (0, 0)),
                pl.BlockSpec((kb, width), kv_map),
                pl.BlockSpec((kb, width), kv_map),
                pl.BlockSpec((rows, 1), lambda j, s: (0, 0)),
            ],
            out_specs=pl.BlockSpec((rows, total), lambda j, s: (0, 0)),
            scratch_shapes=[
                pltpu.VMEM((heads, rows, 1), jnp.float32),
                pltpu.VMEM((heads, rows, 1), jnp.float32),
                pltpu.VMEM((heads, rows, width), jnp.float32),
            ],
        ),
        compiler_params=pltpu.CompilerParams(dimension_semantics=("arbitrary",)),
        cost_estimate=pl.CostEstimate(
            flops=4 * rows * heads * length * width // 2,
            transcendentals=rows * heads * length // 2,
            bytes_accessed=2 * length * width * 2 + 2 * rows * total * 2,
        ),
    )(sref, q, keys, values, starts.reshape(rows, 1))


def carried_in(part, axis, combine, identity):
    place = lax.axis_index(axis)
    size = lax.axis_size(axis)
    ident = jax.tree.map(lambda a, e: jnp.zeros_like(a) + jnp.asarray(e, a.dtype), part, identity)
    shifted = jax.tree.map(
        lambda a: lax.ppermute(a, axis, [(i, i + 1) for i in range(size - 1)]), part
    )
    state = jax.tree.map(lambda s, e: jnp.where(place == 0, e, s), shifted, ident)
    step = 1
    while step < size:
        pairs = [(i, i + step) for i in range(size - step)]
        earlier = jax.tree.map(lambda a: lax.ppermute(a, axis, pairs), state)
        merged = combine(earlier, state)
        state = jax.tree.map(lambda m, s: jnp.where(place >= step, m, s), merged, state)
        step *= 2
    return state


def light_block(carry, inputs, rates):
    state, last_prev = carry
    q_blk, k_blk, v_blk, seg_blk = inputs
    size = q_blk.shape[0]
    seg_f = seg_blk.astype(jnp.float32)
    pos = jnp.arange(size).astype(jnp.float32)
    diff = pos[:, None] - pos[None, :]
    linked = (diff >= 0.0) & (seg_f[:, None] == seg_f[None, :])
    decay = jnp.exp(-rates[:, None, None] * jnp.maximum(diff, 0.0)[None])
    scores = jnp.einsum("thd,shd->hts", q_blk, k_blk, preferred_element_type=jnp.float32)
    weights = jnp.where(linked[None], scores * decay, 0.0).astype(jnp.bfloat16)
    intra = jnp.einsum("hts,shd->thd", weights, v_blk, preferred_element_type=jnp.float32)
    use = (seg_f == last_prev).astype(jnp.float32)
    coef = jnp.exp(-rates[None, :] * (pos[:, None] + 1.0)) * use[:, None]
    q_state = jnp.einsum(
        "thd,hde->the", q_blk.astype(jnp.float32), state, precision=lax.Precision.HIGHEST
    )
    out = intra + coef[:, :, None] * q_state
    last = seg_f[-1]
    k_weight = (
        jnp.exp(-rates[None, :] * (size - 1.0 - pos[:, None]))
        * (seg_f == last).astype(jnp.float32)[:, None]
    )
    k_dec = (k_blk.astype(jnp.float32) * k_weight[:, :, None]).astype(jnp.bfloat16)
    local = jnp.einsum("shd,she->hde", k_dec, v_blk, preferred_element_type=jnp.float32)
    keep = jnp.where(last == last_prev, 1.0, 0.0) * jnp.exp(-rates * size)
    return ((keep[:, None, None] * state + local, last), out)


def combine_states(earlier, later):
    state_e, dec_e, last_e = earlier
    state_l, dec_l, last_l = later
    match = (last_e == last_l) | (last_l < 0.0)
    factor = jnp.where(match, dec_l, 0.0)
    return (factor[:, None, None] * state_e + state_l, dec_e * dec_l, jnp.maximum(last_e, last_l))


def body(lin_q, lin_k, lin_v, decay_rates, norm_gain, soft_q, soft_k, soft_v, segment_ids):
    tok = lin_q.shape[0]
    heads = decay_rates.shape[0]
    width = lin_q.shape[1] // heads
    blocks = tok // BLOCK
    shape4 = (blocks, BLOCK, heads, width)
    init = (jnp.zeros((heads, width, width), jnp.float32), jnp.float32(-1.0))
    step_fn = lambda c, x: light_block(c, x, decay_rates)
    (state_loc, last_loc), outs = lax.scan(
        step_fn,
        init,
        (
            lin_q.reshape(shape4),
            lin_k.reshape(shape4),
            lin_v.reshape(shape4),
            segment_ids.reshape(blocks, BLOCK),
        ),
    )
    local_out = outs.reshape(tok, heads, width)
    summary = (state_loc, jnp.exp(-decay_rates * tok), last_loc.reshape(1))
    identity = (
        jnp.zeros((heads, width, width), jnp.float32),
        jnp.ones((heads,), jnp.float32),
        jnp.full((1,), -1.0, jnp.float32),
    )
    state_in, dec_in, last_in = carried_in(summary, "seq", combine_states, identity)
    seg_f = segment_ids.astype(jnp.float32)
    pos = jnp.arange(tok).astype(jnp.float32)
    coef = (
        jnp.exp(-decay_rates[None, :] * (pos[:, None] + 1.0))
        * (seg_f == last_in[0]).astype(jnp.float32)[:, None]
    )
    q_three = lin_q.reshape(tok, heads, width)
    q_state = jnp.einsum(
        "thd,hde->the", q_three.astype(jnp.float32), state_in, precision=lax.Precision.HIGHEST
    )
    raw = (local_out + coef[:, :, None] * q_state).reshape(tok, heads * width)
    sums = jnp.sum(raw * raw, axis=1)
    total_sq = lax.psum(sums, "heads")
    count = lax.axis_size("heads") * heads * width
    lin_out = (raw * lax.rsqrt(total_sq / count + 1e-06)[:, None] * norm_gain[None, :]).astype(
        jnp.bfloat16
    )
    shared_heads = soft_k.shape[1] // width
    group = heads // shared_heads
    mine = lax.axis_index("seq")
    keys = lax.all_gather(soft_k, "seq", axis=0, tiled=True)
    values = lax.all_gather(soft_v, "seq", axis=0, tiled=True)
    seg_keys = lax.all_gather(segment_ids.astype(jnp.float32), "seq", axis=0, tiled=True)
    starts = jnp.sum(
        (seg_keys[None, :] < segment_ids.astype(jnp.float32)[:, None]).astype(jnp.int32), axis=1
    )
    q0 = (mine * tok).astype(jnp.int32)
    pieces = []
    for g in range(shared_heads):
        cols = slice(g * group * width, (g + 1) * group * width)
        pieces.append(
            flash_attention(
                soft_q[:, cols],
                keys[:, g * width:(g + 1) * width],
                values[:, g * width:(g + 1) * width],
                starts,
                q0,
            )
        )
    soft_out = pieces[0] if shared_heads == 1 else jnp.concatenate(pieces, axis=1)
    return (lin_out, soft_out)


def solution(mesh):
    placed = (
        P("seq", "heads"),
        P("seq", "heads"),
        P("seq", "heads"),
        P("heads"),
        P("heads"),
        P("seq", "heads"),
        P("seq", "heads"),
        P("seq", "heads"),
        P("seq"),
    )
    return jax.shard_map(
        body,
        mesh=mesh,
        in_specs=placed,
        out_specs=(P("seq", "heads"), P("seq", "heads")),
        check_vma=False,
    )
```

```python
import math

import jax
import jax.numpy as jnp
from jax import lax
from jax.experimental import pallas as pl
from jax.experimental.pallas import tpu as pltpu
from jax.sharding import PartitionSpec as P

BLOCK = 256
KEY_BLOCK = 512


def flash_body(sref, q_ref, k_ref, v_ref, st_ref, o_ref, m_ref, l_ref, acc_ref, *, heads, width, scale):
    j = pl.program_id(0)
    lo, hi, flo, fhi, q0 = sref[0], sref[1], sref[2], sref[3], sref[4]
    rows = q_ref.shape[0]
    kb = k_ref.shape[0]

    @pl.when(j == 0)
    def _():
        m_ref[...] = jnp.full(m_ref.shape, -1e30, jnp.float32)
        l_ref[...] = jnp.zeros(l_ref.shape, jnp.float32)
        acc_ref[...] = jnp.zeros(acc_ref.shape, jnp.float32)

    def step(masked):
        k = k_ref[...]
        v = v_ref[...]
        if masked:
            kpos = j * kb + lax.broadcasted_iota(jnp.int32, (rows, kb), 1)
            qpos = q0 + lax.broadcasted_iota(jnp.int32, (rows, kb), 0)
            valid = (kpos <= qpos) & (kpos >= st_ref[...])
        for h in range(heads):
            q = q_ref[:, h * width:(h + 1) * width]
            s = lax.dot_general(q, k, (((1,), (1,)), ((), ())), preferred_element_type=jnp.float32) * scale
            m_prev = m_ref[h]
            if masked:
                top = jnp.max(jnp.where(valid, s, -1e30), axis=1, keepdims=True)
            else:
                top = jnp.max(s, axis=1, keepdims=True)
            m_new = jnp.maximum(m_prev, top)
            corr = jnp.exp(m_prev - m_new)
            e = jnp.exp(s - m_new)
            p = jnp.where(valid, e, 0.0) if masked else e
            l_ref[h] = l_ref[h] * corr + jnp.sum(p, axis=1, keepdims=True)
            pv = jnp.dot(p.astype(jnp.bfloat16), v, preferred_element_type=jnp.float32)
            acc_ref[h] = acc_ref[h] * corr + pv
            m_ref[h] = m_new

    inside = (j >= lo) & (j <= hi)
    full = (j >= flo) & (j <= fhi)

    @pl.when(inside & full)
    def _():
        step(False)

    @pl.when(inside & jnp.logical_not(full))
    def _():
        step(True)

    @pl.when(j == pl.num_programs(0) - 1)
    def _():
        for h in range(heads):
            o_ref[:, h * width:(h + 1) * width] = (acc_ref[h] / l_ref[h]).astype(o_ref.dtype)


def flash_attention(q, keys, values, starts, q0):
    rows, total = q.shape
    length, width = keys.shape
    heads = total // width
    kb = min(KEY_BLOCK, length)
    nk = length // kb
    scale = 1.0 / math.sqrt(width)
    first = starts[0]
    last_start = starts[rows - 1]
    lo = first // kb
    hi = (q0 + rows - 1) // kb
    flo = (last_start + kb - 1) // kb
    fhi = (q0 + 1) // kb - 1
    sref = jnp.stack([lo, hi, flo, fhi, q0]).astype(jnp.int32)

    def kv_map(j, s):
        return (jnp.minimum(jnp.maximum(j, s[0]), s[1]), 0)

    kernel = lambda *refs: flash_body(*refs, heads=heads, width=width, scale=scale)
    return pl.pallas_call(
        kernel,
        out_shape=jax.ShapeDtypeStruct((rows, total), jnp.bfloat16),
        grid_spec=pltpu.PrefetchScalarGridSpec(
            num_scalar_prefetch=1,
            grid=(nk,),
            in_specs=[
                pl.BlockSpec((rows, total), lambda j, s: (0, 0)),
                pl.BlockSpec((kb, width), kv_map),
                pl.BlockSpec((kb, width), kv_map),
                pl.BlockSpec((rows, 1), lambda j, s: (0, 0)),
            ],
            out_specs=pl.BlockSpec((rows, total), lambda j, s: (0, 0)),
            scratch_shapes=[
                pltpu.VMEM((heads, rows, 1), jnp.float32),
                pltpu.VMEM((heads, rows, 1), jnp.float32),
                pltpu.VMEM((heads, rows, width), jnp.float32),
            ],
        ),
        compiler_params=pltpu.CompilerParams(dimension_semantics=("arbitrary",)),
        cost_estimate=pl.CostEstimate(
            flops=4 * rows * heads * length * width // 2,
            transcendentals=rows * heads * length // 2,
            bytes_accessed=2 * length * width * 2 + 2 * rows * total * 2,
        ),
    )(sref, q, keys, values, starts.reshape(rows, 1))


def carried_in(part, axis, combine, identity):
    place = lax.axis_index(axis)
    size = lax.axis_size(axis)
    ident = jax.tree.map(lambda a, e: jnp.zeros_like(a) + jnp.asarray(e, a.dtype), part, identity)
    shifted = jax.tree.map(
        lambda a: lax.ppermute(a, axis, [(i, i + 1) for i in range(size - 1)]), part
    )
    state = jax.tree.map(lambda s, e: jnp.where(place == 0, e, s), shifted, ident)
    step = 1
    while step < size:
        pairs = [(i, i + step) for i in range(size - step)]
        earlier = jax.tree.map(lambda a: lax.ppermute(a, axis, pairs), state)
        merged = combine(earlier, state)
        state = jax.tree.map(lambda m, s: jnp.where(place >= step, m, s), merged, state)
        step *= 2
    return state


def light_block(carry, inputs, rates):
    state, last_prev = carry
    q_blk, k_blk, v_blk, seg_blk = inputs
    size = q_blk.shape[0]
    seg_f = seg_blk.astype(jnp.float32)
    pos = jnp.arange(size).astype(jnp.float32)
    diff = pos[:, None] - pos[None, :]
    linked = (diff >= 0.0) & (seg_f[:, None] == seg_f[None, :])
    decay = jnp.exp(-rates[:, None, None] * jnp.maximum(diff, 0.0)[None])
    scores = jnp.einsum("thd,shd->hts", q_blk, k_blk, preferred_element_type=jnp.float32)
    weights = jnp.where(linked[None], scores * decay, 0.0).astype(jnp.bfloat16)
    intra = jnp.einsum("hts,shd->thd", weights, v_blk, preferred_element_type=jnp.float32)
    use = (seg_f == last_prev).astype(jnp.float32)
    coef = jnp.exp(-rates[None, :] * (pos[:, None] + 1.0)) * use[:, None]
    q_state = jnp.einsum(
        "thd,hde->the", q_blk.astype(jnp.float32), state, precision=lax.Precision.HIGHEST
    )
    out = intra + coef[:, :, None] * q_state
    last = seg_f[-1]
    k_weight = (
        jnp.exp(-rates[None, :] * (size - 1.0 - pos[:, None]))
        * (seg_f == last).astype(jnp.float32)[:, None]
    )
    k_dec = (k_blk.astype(jnp.float32) * k_weight[:, :, None]).astype(jnp.bfloat16)
    local = jnp.einsum("shd,she->hde", k_dec, v_blk, preferred_element_type=jnp.float32)
    keep = jnp.where(last == last_prev, 1.0, 0.0) * jnp.exp(-rates * size)
    return ((keep[:, None, None] * state + local, last), out)


def combine_bounds(earlier, later):
    last_e, first_e = earlier
    last_l, first_l = later
    keep = (last_e == last_l) | (last_l < 0.0)
    return (jnp.maximum(last_e, last_l), jnp.where(keep, first_e, first_l))


def combine_states(earlier, later):
    state_e, dec_e, last_e = earlier
    state_l, dec_l, last_l = later
    match = (last_e == last_l) | (last_l < 0.0)
    factor = jnp.where(match, dec_l, 0.0)
    return (factor[:, None, None] * state_e + state_l, dec_e * dec_l, jnp.maximum(last_e, last_l))


def body(lin_q, lin_k, lin_v, decay_rates, norm_gain, soft_q, soft_k, soft_v, segment_ids):
    tok = lin_q.shape[0]
    heads = decay_rates.shape[0]
    width = lin_q.shape[1] // heads
    blocks = tok // BLOCK
    shape4 = (blocks, BLOCK, heads, width)
    init = (jnp.zeros((heads, width, width), jnp.float32), jnp.float32(-1.0))
    step_fn = lambda c, x: light_block(c, x, decay_rates)
    (state_loc, last_loc), outs = lax.scan(
        step_fn,
        init,
        (
            lin_q.reshape(shape4),
            lin_k.reshape(shape4),
            lin_v.reshape(shape4),
            segment_ids.reshape(blocks, BLOCK),
        ),
    )
    local_out = outs.reshape(tok, heads, width)
    summary = (state_loc, jnp.exp(-decay_rates * tok), last_loc.reshape(1))
    identity = (
        jnp.zeros((heads, width, width), jnp.float32),
        jnp.ones((heads,), jnp.float32),
        jnp.full((1,), -1.0, jnp.float32),
    )
    state_in, dec_in, last_in = carried_in(summary, "seq", combine_states, identity)
    seg_f = segment_ids.astype(jnp.float32)
    pos = jnp.arange(tok).astype(jnp.float32)
    coef = (
        jnp.exp(-decay_rates[None, :] * (pos[:, None] + 1.0))
        * (seg_f == last_in[0]).astype(jnp.float32)[:, None]
    )
    q_three = lin_q.reshape(tok, heads, width)
    q_state = jnp.einsum(
        "thd,hde->the", q_three.astype(jnp.float32), state_in, precision=lax.Precision.HIGHEST
    )
    raw = (local_out + coef[:, :, None] * q_state).reshape(tok, heads * width)
    sums = jnp.sum(raw * raw, axis=1)
    total_sq = lax.psum(sums, "heads")
    count = lax.axis_size("heads") * heads * width
    lin_out = (raw * lax.rsqrt(total_sq / count + 1e-06)[:, None] * norm_gain[None, :]).astype(
        jnp.bfloat16
    )
    shared_heads = soft_k.shape[1] // width
    group = heads // shared_heads
    mine = lax.axis_index("seq")
    keys = lax.all_gather(soft_k, "seq", axis=0, tiled=True)
    values = lax.all_gather(soft_v, "seq", axis=0, tiled=True)
    q0 = (mine * tok).astype(jnp.int32)
    seg_i = segment_ids.astype(jnp.float32)
    below = jnp.sum((seg_i[None, :] < seg_i[:, None]).astype(jnp.int32), axis=1)
    last_here = seg_i[tok - 1]
    first_here = (q0 + jnp.sum((seg_i < last_here).astype(jnp.int32))).astype(jnp.float32)
    last_before, first_before = carried_in(
        (last_here.reshape(1), first_here.reshape(1)),
        "seq",
        combine_bounds,
        (jnp.full((1,), -1.0, jnp.float32), jnp.zeros((1,), jnp.float32)),
    )
    starts = jnp.where(
        seg_i == last_before[0], first_before[0].astype(jnp.int32), q0 + below
    )
    pieces = []
    for g in range(shared_heads):
        cols = slice(g * group * width, (g + 1) * group * width)
        pieces.append(
            flash_attention(
                soft_q[:, cols],
                keys[:, g * width:(g + 1) * width],
                values[:, g * width:(g + 1) * width],
                starts,
                q0,
            )
        )
    soft_out = pieces[0] if shared_heads == 1 else jnp.concatenate(pieces, axis=1)
    return (lin_out, soft_out)


def solution(mesh):
    placed = (
        P("seq", "heads"),
        P("seq", "heads"),
        P("seq", "heads"),
        P("heads"),
        P("heads"),
        P("seq", "heads"),
        P("seq", "heads"),
        P("seq", "heads"),
        P("seq"),
    )
    return jax.shard_map(
        body,
        mesh=mesh,
        in_specs=placed,
        out_specs=(P("seq", "heads"), P("seq", "heads")),
        check_vma=False,
    )
```

```python
import math

import jax
import jax.numpy as jnp
from jax import lax
from jax.experimental import pallas as pl
from jax.experimental.pallas import tpu as pltpu
from jax.sharding import PartitionSpec as P

BLOCK = 256
KEY_BLOCK = 512


def flash_body(sref, q_ref, k_ref, v_ref, st_ref, o_ref, m_ref, l_ref, acc_ref, *, heads, width, scale):
    j = pl.program_id(0)
    lo, hi, flo, fhi, q0 = sref[0], sref[1], sref[2], sref[3], sref[4]
    rows = q_ref.shape[0]
    kb = k_ref.shape[0]

    @pl.when(j == 0)
    def _():
        m_ref[...] = jnp.full(m_ref.shape, -1e30, jnp.float32)
        l_ref[...] = jnp.zeros(l_ref.shape, jnp.float32)
        acc_ref[...] = jnp.zeros(acc_ref.shape, jnp.float32)

    def step(masked):
        k = k_ref[...]
        v = v_ref[...]
        if masked:
            kpos = j * kb + lax.broadcasted_iota(jnp.int32, (rows, kb), 1)
            qpos = q0 + lax.broadcasted_iota(jnp.int32, (rows, kb), 0)
            valid = (kpos <= qpos) & (kpos >= st_ref[...])
        for h in range(heads):
            q = q_ref[:, h * width:(h + 1) * width]
            s = lax.dot_general(q, k, (((1,), (1,)), ((), ())), preferred_element_type=jnp.float32) * scale
            m_prev = m_ref[h]
            if masked:
                top = jnp.max(jnp.where(valid, s, -1e30), axis=1, keepdims=True)
            else:
                top = jnp.max(s, axis=1, keepdims=True)
            m_new = jnp.maximum(m_prev, top)
            corr = jnp.exp(m_prev - m_new)
            e = jnp.exp(s - m_new)
            p = jnp.where(valid, e, 0.0) if masked else e
            l_ref[h] = l_ref[h] * corr + jnp.sum(p, axis=1, keepdims=True)
            pv = jnp.dot(p.astype(jnp.bfloat16), v, preferred_element_type=jnp.float32)
            acc_ref[h] = acc_ref[h] * corr + pv
            m_ref[h] = m_new

    inside = (j >= lo) & (j <= hi)
    full = (j >= flo) & (j <= fhi)

    @pl.when(inside & full)
    def _():
        step(False)

    @pl.when(inside & jnp.logical_not(full))
    def _():
        step(True)

    @pl.when(j == pl.num_programs(0) - 1)
    def _():
        for h in range(heads):
            o_ref[:, h * width:(h + 1) * width] = (acc_ref[h] / l_ref[h]).astype(o_ref.dtype)


def flash_attention(q, keys, values, starts, q0):
    rows, total = q.shape
    length, width = keys.shape
    heads = total // width
    kb = min(KEY_BLOCK, length)
    nk = length // kb
    scale = 1.0 / math.sqrt(width)
    first = starts[0]
    last_start = starts[rows - 1]
    lo = first // kb
    hi = (q0 + rows - 1) // kb
    flo = (last_start + kb - 1) // kb
    fhi = (q0 + 1) // kb - 1
    sref = jnp.stack([lo, hi, flo, fhi, q0]).astype(jnp.int32)

    def kv_map(j, s):
        return (jnp.minimum(jnp.maximum(j, s[0]), s[1]), 0)

    kernel = lambda *refs: flash_body(*refs, heads=heads, width=width, scale=scale)
    return pl.pallas_call(
        kernel,
        out_shape=jax.ShapeDtypeStruct((rows, total), jnp.bfloat16),
        grid_spec=pltpu.PrefetchScalarGridSpec(
            num_scalar_prefetch=1,
            grid=(nk,),
            in_specs=[
                pl.BlockSpec((rows, total), lambda j, s: (0, 0)),
                pl.BlockSpec((kb, width), kv_map),
                pl.BlockSpec((kb, width), kv_map),
                pl.BlockSpec((rows, 1), lambda j, s: (0, 0)),
            ],
            out_specs=pl.BlockSpec((rows, total), lambda j, s: (0, 0)),
            scratch_shapes=[
                pltpu.VMEM((heads, rows, 1), jnp.float32),
                pltpu.VMEM((heads, rows, 1), jnp.float32),
                pltpu.VMEM((heads, rows, width), jnp.float32),
            ],
        ),
        compiler_params=pltpu.CompilerParams(dimension_semantics=("arbitrary",)),
        cost_estimate=pl.CostEstimate(
            flops=4 * rows * heads * length * width // 2,
            transcendentals=rows * heads * length // 2,
            bytes_accessed=2 * length * width * 2 + 2 * rows * total * 2,
        ),
    )(sref, q, keys, values, starts.reshape(rows, 1))


def light_block(carry, inputs, rates):
    state, last_prev = carry
    q_blk, k_blk, v_blk, seg_blk = inputs
    size = q_blk.shape[0]
    seg_f = seg_blk.astype(jnp.float32)
    pos = jnp.arange(size).astype(jnp.float32)
    diff = pos[:, None] - pos[None, :]
    linked = (diff >= 0.0) & (seg_f[:, None] == seg_f[None, :])
    decay = jnp.exp(-rates[:, None, None] * jnp.maximum(diff, 0.0)[None])
    scores = jnp.einsum("thd,shd->hts", q_blk, k_blk, preferred_element_type=jnp.float32)
    weights = jnp.where(linked[None], scores * decay, 0.0).astype(jnp.bfloat16)
    intra = jnp.einsum("hts,shd->thd", weights, v_blk, preferred_element_type=jnp.float32)
    use = (seg_f == last_prev).astype(jnp.float32)
    coef = jnp.exp(-rates[None, :] * (pos[:, None] + 1.0)) * use[:, None]
    q_state = jnp.einsum(
        "thd,hde->the", q_blk.astype(jnp.float32), state, precision=lax.Precision.HIGHEST
    )
    out = intra + coef[:, :, None] * q_state
    last = seg_f[-1]
    k_weight = (
        jnp.exp(-rates[None, :] * (size - 1.0 - pos[:, None]))
        * (seg_f == last).astype(jnp.float32)[:, None]
    )
    k_dec = (k_blk.astype(jnp.float32) * k_weight[:, :, None]).astype(jnp.bfloat16)
    local = jnp.einsum("shd,she->hde", k_dec, v_blk, preferred_element_type=jnp.float32)
    keep = jnp.where(last == last_prev, 1.0, 0.0) * jnp.exp(-rates * size)
    return ((keep[:, None, None] * state + local, last), out)


def body(lin_q, lin_k, lin_v, decay_rates, norm_gain, soft_q, soft_k, soft_v, segment_ids):
    tok = lin_q.shape[0]
    heads = decay_rates.shape[0]
    width = lin_q.shape[1] // heads
    blocks = tok // BLOCK
    shape4 = (blocks, BLOCK, heads, width)
    init = (jnp.zeros((heads, width, width), jnp.float32), jnp.float32(-1.0))
    step_fn = lambda c, x: light_block(c, x, decay_rates)
    (state_loc, last_loc), outs = lax.scan(
        step_fn,
        init,
        (
            lin_q.reshape(shape4),
            lin_k.reshape(shape4),
            lin_v.reshape(shape4),
            segment_ids.reshape(blocks, BLOCK),
        ),
    )
    local_out = outs.reshape(tok, heads, width)
    mine = lax.axis_index("seq")
    parts = lax.axis_size("seq")
    q0 = (mine * tok).astype(jnp.int32)
    seg_i = segment_ids.astype(jnp.float32)
    last_here = seg_i[tok - 1]
    first_here = (q0 + jnp.sum((seg_i < last_here).astype(jnp.int32))).astype(jnp.float32)
    rows_per = heads * width // parts
    chunks = state_loc.reshape(parts, rows_per, width)
    lane = jnp.arange(width)
    info = jnp.where(lane == 0, last_here, jnp.where(lane == 1, first_here, 0.0))
    info = jnp.broadcast_to(info[None, None, :], (parts, 8, width))
    sent = lax.all_to_all(jnp.concatenate([chunks, info], axis=1), "seq", 0, 0)
    lasts = sent[:, rows_per, 0]
    firsts = sent[:, rows_per, 1]
    idx = jnp.arange(parts)
    last_prev = jnp.where(idx >= 1, jnp.roll(lasts, 1), -1.0)
    rate = decay_rates[(mine * rows_per) // width]
    gap = jnp.maximum(idx[:, None] - 1 - idx[None, :], 0).astype(jnp.float32)
    linked = (idx[None, :] < idx[:, None]) & (lasts[None, :] == last_prev[:, None])
    weight = jnp.where(linked, jnp.exp(-rate * tok * gap), 0.0)
    mixed = jnp.einsum(
        "pj,jrc->prc", weight, sent[:, :rows_per, :], precision=lax.Precision.HIGHEST
    )
    state_in = lax.all_to_all(mixed, "seq", 0, 0).reshape(heads, width, width)
    last_before = last_prev[mine]
    same_doc = (idx < mine) & (lasts == last_before)
    first_before = jnp.min(jnp.where(same_doc, firsts, jnp.float32(tok * parts)))
    last_in = last_before.reshape(1)
    seg_f = segment_ids.astype(jnp.float32)
    pos = jnp.arange(tok).astype(jnp.float32)
    coef = (
        jnp.exp(-decay_rates[None, :] * (pos[:, None] + 1.0))
        * (seg_f == last_in[0]).astype(jnp.float32)[:, None]
    )
    q_three = lin_q.reshape(tok, heads, width)
    q_state = jnp.einsum(
        "thd,hde->the", q_three.astype(jnp.float32), state_in, precision=lax.Precision.HIGHEST
    )
    raw = (local_out + coef[:, :, None] * q_state).reshape(tok, heads * width)
    sums = jnp.sum(raw * raw, axis=1)
    total_sq = lax.psum(sums, "heads")
    count = lax.axis_size("heads") * heads * width
    lin_out = (raw * lax.rsqrt(total_sq / count + 1e-06)[:, None] * norm_gain[None, :]).astype(
        jnp.bfloat16
    )
    shared_heads = soft_k.shape[1] // width
    group = heads // shared_heads
    keys = lax.all_gather(soft_k, "seq", axis=0, tiled=True)
    values = lax.all_gather(soft_v, "seq", axis=0, tiled=True)
    below = jnp.sum((seg_i[None, :] < seg_i[:, None]).astype(jnp.int32), axis=1)
    starts = jnp.where(
        seg_i == last_before, first_before.astype(jnp.int32), q0 + below
    )
    pieces = []
    for g in range(shared_heads):
        cols = slice(g * group * width, (g + 1) * group * width)
        pieces.append(
            flash_attention(
                soft_q[:, cols],
                keys[:, g * width:(g + 1) * width],
                values[:, g * width:(g + 1) * width],
                starts,
                q0,
            )
        )
    soft_out = pieces[0] if shared_heads == 1 else jnp.concatenate(pieces, axis=1)
    return (lin_out, soft_out)


def solution(mesh):
    placed = (
        P("seq", "heads"),
        P("seq", "heads"),
        P("seq", "heads"),
        P("heads"),
        P("heads"),
        P("seq", "heads"),
        P("seq", "heads"),
        P("seq", "heads"),
        P("seq"),
    )
    return jax.shard_map(
        body,
        mesh=mesh,
        in_specs=placed,
        out_specs=(P("seq", "heads"), P("seq", "heads")),
        check_vma=False,
    )
```

```python
import math

import jax
import jax.numpy as jnp
from jax import lax
from jax.experimental import pallas as pl
from jax.experimental.pallas import tpu as pltpu
from jax.sharding import PartitionSpec as P

BLOCK = 256
KEY_BLOCK = 256


def flash_body(sref, q_ref, k_ref, v_ref, st_ref, o_ref, m_ref, l_ref, acc_ref, *, heads, width, scale):
    j = pl.program_id(0)
    lo, hi, flo, fhi, q0 = sref[0], sref[1], sref[2], sref[3], sref[4]
    rows = q_ref.shape[0]
    kb = k_ref.shape[0]

    @pl.when(j == 0)
    def _():
        m_ref[...] = jnp.full(m_ref.shape, -1e30, jnp.float32)
        l_ref[...] = jnp.zeros(l_ref.shape, jnp.float32)
        acc_ref[...] = jnp.zeros(acc_ref.shape, jnp.float32)

    def step(masked):
        k = k_ref[...]
        v = v_ref[...]
        if masked:
            kpos = j * kb + lax.broadcasted_iota(jnp.int32, (rows, kb), 1)
            qpos = q0 + lax.broadcasted_iota(jnp.int32, (rows, kb), 0)
            valid = (kpos <= qpos) & (kpos >= st_ref[...])
        for h in range(heads):
            q = q_ref[:, h * width:(h + 1) * width]
            s = lax.dot_general(q, k, (((1,), (1,)), ((), ())), preferred_element_type=jnp.float32) * scale
            m_prev = m_ref[h]
            if masked:
                top = jnp.max(jnp.where(valid, s, -1e30), axis=1, keepdims=True)
            else:
                top = jnp.max(s, axis=1, keepdims=True)
            m_new = jnp.maximum(m_prev, top)
            corr = jnp.exp(m_prev - m_new)
            e = jnp.exp(s - m_new)
            p = jnp.where(valid, e, 0.0) if masked else e
            l_ref[h] = l_ref[h] * corr + jnp.sum(p, axis=1, keepdims=True)
            pv = jnp.dot(p.astype(jnp.bfloat16), v, preferred_element_type=jnp.float32)
            acc_ref[h] = acc_ref[h] * corr + pv
            m_ref[h] = m_new

    inside = (j >= lo) & (j <= hi)
    full = (j >= flo) & (j <= fhi)

    @pl.when(inside & full)
    def _():
        step(False)

    @pl.when(inside & jnp.logical_not(full))
    def _():
        step(True)

    @pl.when(j == pl.num_programs(0) - 1)
    def _():
        for h in range(heads):
            o_ref[:, h * width:(h + 1) * width] = (acc_ref[h] / l_ref[h]).astype(o_ref.dtype)


def flash_attention(q, keys, values, starts, q0):
    rows, total = q.shape
    length, width = keys.shape
    heads = total // width
    kb = min(KEY_BLOCK, length)
    nk = length // kb
    scale = 1.0 / math.sqrt(width)
    first = starts[0]
    last_start = starts[rows - 1]
    lo = first // kb
    hi = (q0 + rows - 1) // kb
    flo = (last_start + kb - 1) // kb
    fhi = (q0 + 1) // kb - 1
    sref = jnp.stack([lo, hi, flo, fhi, q0]).astype(jnp.int32)

    def kv_map(j, s):
        return (jnp.minimum(jnp.maximum(j, s[0]), s[1]), 0)

    kernel = lambda *refs: flash_body(*refs, heads=heads, width=width, scale=scale)
    return pl.pallas_call(
        kernel,
        out_shape=jax.ShapeDtypeStruct((rows, total), jnp.bfloat16),
        grid_spec=pltpu.PrefetchScalarGridSpec(
            num_scalar_prefetch=1,
            grid=(nk,),
            in_specs=[
                pl.BlockSpec((rows, total), lambda j, s: (0, 0)),
                pl.BlockSpec((kb, width), kv_map),
                pl.BlockSpec((kb, width), kv_map),
                pl.BlockSpec((rows, 1), lambda j, s: (0, 0)),
            ],
            out_specs=pl.BlockSpec((rows, total), lambda j, s: (0, 0)),
            scratch_shapes=[
                pltpu.VMEM((heads, rows, 1), jnp.float32),
                pltpu.VMEM((heads, rows, 1), jnp.float32),
                pltpu.VMEM((heads, rows, width), jnp.float32),
            ],
        ),
        compiler_params=pltpu.CompilerParams(dimension_semantics=("arbitrary",)),
        cost_estimate=pl.CostEstimate(
            flops=4 * rows * heads * length * width // 2,
            transcendentals=rows * heads * length // 2,
            bytes_accessed=2 * length * width * 2 + 2 * rows * total * 2,
        ),
    )(sref, q, keys, values, starts.reshape(rows, 1))


def gather_body(k_ref, v_ref, ko_ref, vo_ref, send_sem, recv_sem, own_sem, *, parts, rows):
    me = lax.axis_index("seq")
    col = lax.axis_index("heads")
    mine = pl.ds(pl.multiple_of(me * rows, rows), rows)
    own = [
        pltpu.make_async_copy(k_ref, ko_ref.at[mine], own_sem.at[0]),
        pltpu.make_async_copy(v_ref, vo_ref.at[mine], own_sem.at[1]),
    ]
    for c in own:
        c.start()

    def remote(step, src, dst, which):
        return pltpu.make_async_remote_copy(
            src_ref=src,
            dst_ref=dst.at[mine],
            send_sem=send_sem.at[step, which],
            recv_sem=recv_sem.at[me, which],
            device_id=(me + step, col),
            device_id_type=pl.DeviceIdType.MESH,
        )

    for step in range(1, parts):
        @pl.when(me + step < parts)
        def _():
            remote(step, k_ref, ko_ref, 0).start()
            remote(step, v_ref, vo_ref, 1).start()

    for src_slot in range(parts - 1):
        @pl.when(src_slot < me)
        def _():
            slot = pl.ds(src_slot * rows, rows)
            for which, (src, dst) in enumerate(((k_ref, ko_ref), (v_ref, vo_ref))):
                pltpu.make_async_remote_copy(
                    src_ref=src,
                    dst_ref=dst.at[slot],
                    send_sem=send_sem.at[0, which],
                    recv_sem=recv_sem.at[src_slot, which],
                    device_id=(me, col),
                    device_id_type=pl.DeviceIdType.MESH,
                ).wait_recv()

    for step in range(1, parts):
        @pl.when(me + step < parts)
        def _():
            remote(step, k_ref, ko_ref, 0).wait_send()
            remote(step, v_ref, vo_ref, 1).wait_send()

    for c in own:
        c.wait()


def gather_earlier(keys, values, parts):
    rows, width = keys.shape
    body = lambda *refs: gather_body(*refs, parts=parts, rows=rows)
    full = jax.ShapeDtypeStruct((parts * rows, width), keys.dtype)
    return pl.pallas_call(
        body,
        out_shape=(full, full),
        in_specs=[pl.BlockSpec(memory_space=pl.ANY)] * 2,
        out_specs=(pl.BlockSpec(memory_space=pl.ANY), pl.BlockSpec(memory_space=pl.ANY)),
        scratch_shapes=[
            pltpu.SemaphoreType.DMA((parts, 2)),
            pltpu.SemaphoreType.DMA((parts, 2)),
            pltpu.SemaphoreType.DMA((2,)),
        ],
        compiler_params=pltpu.CompilerParams(has_side_effects=True),
    )(keys, values)


def light_block(carry, inputs, rates):
    state, last_prev = carry
    q_blk, k_blk, v_blk, seg_blk = inputs
    size = q_blk.shape[0]
    seg_f = seg_blk.astype(jnp.float32)
    pos = jnp.arange(size).astype(jnp.float32)
    diff = pos[:, None] - pos[None, :]
    linked = (diff >= 0.0) & (seg_f[:, None] == seg_f[None, :])
    decay = jnp.exp(-rates[:, None, None] * jnp.maximum(diff, 0.0)[None])
    scores = jnp.einsum("thd,shd->hts", q_blk, k_blk, preferred_element_type=jnp.float32)
    weights = jnp.where(linked[None], scores * decay, 0.0).astype(jnp.bfloat16)
    intra = jnp.einsum("hts,shd->thd", weights, v_blk, preferred_element_type=jnp.float32)
    use = (seg_f == last_prev).astype(jnp.float32)
    coef = jnp.exp(-rates[None, :] * (pos[:, None] + 1.0)) * use[:, None]
    q_state = jnp.einsum(
        "thd,hde->the", q_blk.astype(jnp.float32), state, precision=lax.Precision.HIGHEST
    )
    out = intra + coef[:, :, None] * q_state
    last = seg_f[-1]
    k_weight = (
        jnp.exp(-rates[None, :] * (size - 1.0 - pos[:, None]))
        * (seg_f == last).astype(jnp.float32)[:, None]
    )
    k_dec = (k_blk.astype(jnp.float32) * k_weight[:, :, None]).astype(jnp.bfloat16)
    local = jnp.einsum("shd,she->hde", k_dec, v_blk, preferred_element_type=jnp.float32)
    keep = jnp.where(last == last_prev, 1.0, 0.0) * jnp.exp(-rates * size)
    return ((keep[:, None, None] * state + local, last), out)


def body(lin_q, lin_k, lin_v, decay_rates, norm_gain, soft_q, soft_k, soft_v, segment_ids):
    tok = lin_q.shape[0]
    heads = decay_rates.shape[0]
    width = lin_q.shape[1] // heads
    blocks = tok // BLOCK
    shape4 = (blocks, BLOCK, heads, width)
    init = (jnp.zeros((heads, width, width), jnp.float32), jnp.float32(-1.0))
    step_fn = lambda c, x: light_block(c, x, decay_rates)
    (state_loc, last_loc), outs = lax.scan(
        step_fn,
        init,
        (
            lin_q.reshape(shape4),
            lin_k.reshape(shape4),
            lin_v.reshape(shape4),
            segment_ids.reshape(blocks, BLOCK),
        ),
    )
    local_out = outs.reshape(tok, heads, width)
    mine = lax.axis_index("seq")
    parts = lax.axis_size("seq")
    q0 = (mine * tok).astype(jnp.int32)
    seg_i = segment_ids.astype(jnp.float32)
    last_here = seg_i[tok - 1]
    first_here = (q0 + jnp.sum((seg_i < last_here).astype(jnp.int32))).astype(jnp.float32)
    rows_per = heads * width // parts
    chunks = state_loc.reshape(parts, rows_per, width)
    lane = jnp.arange(width)
    info = jnp.where(lane == 0, last_here, jnp.where(lane == 1, first_here, 0.0))
    info = jnp.broadcast_to(info[None, None, :], (parts, 8, width))
    sent = lax.all_to_all(jnp.concatenate([chunks, info], axis=1), "seq", 0, 0)
    lasts = sent[:, rows_per, 0]
    firsts = sent[:, rows_per, 1]
    idx = jnp.arange(parts)
    last_prev = jnp.where(idx >= 1, jnp.roll(lasts, 1), -1.0)
    rate = decay_rates[(mine * rows_per) // width]
    gap = jnp.maximum(idx[:, None] - 1 - idx[None, :], 0).astype(jnp.float32)
    linked = (idx[None, :] < idx[:, None]) & (lasts[None, :] == last_prev[:, None])
    weight = jnp.where(linked, jnp.exp(-rate * tok * gap), 0.0)
    mixed = jnp.einsum(
        "pj,jrc->prc", weight, sent[:, :rows_per, :], precision=lax.Precision.HIGHEST
    )
    state_in = lax.all_to_all(mixed, "seq", 0, 0).reshape(heads, width, width)
    last_before = last_prev[mine]
    same_doc = (idx < mine) & (lasts == last_before)
    first_before = jnp.min(jnp.where(same_doc, firsts, jnp.float32(tok * parts)))
    last_in = last_before.reshape(1)
    seg_f = segment_ids.astype(jnp.float32)
    pos = jnp.arange(tok).astype(jnp.float32)
    coef = (
        jnp.exp(-decay_rates[None, :] * (pos[:, None] + 1.0))
        * (seg_f == last_in[0]).astype(jnp.float32)[:, None]
    )
    q_three = lin_q.reshape(tok, heads, width)
    q_state = jnp.einsum(
        "thd,hde->the", q_three.astype(jnp.float32), state_in, precision=lax.Precision.HIGHEST
    )
    raw = (local_out + coef[:, :, None] * q_state).reshape(tok, heads * width)
    sums = jnp.sum(raw * raw, axis=1)
    total_sq = lax.psum(sums, "heads")
    count = lax.axis_size("heads") * heads * width
    lin_out = (raw * lax.rsqrt(total_sq / count + 1e-06)[:, None] * norm_gain[None, :]).astype(
        jnp.bfloat16
    )
    shared_heads = soft_k.shape[1] // width
    group = heads // shared_heads
    keys, values = gather_earlier(soft_k, soft_v, parts)
    below = jnp.sum((seg_i[None, :] < seg_i[:, None]).astype(jnp.int32), axis=1)
    starts = jnp.where(
        seg_i == last_before, first_before.astype(jnp.int32), q0 + below
    )
    pieces = []
    for g in range(shared_heads):
        cols = slice(g * group * width, (g + 1) * group * width)
        pieces.append(
            flash_attention(
                soft_q[:, cols],
                keys[:, g * width:(g + 1) * width],
                values[:, g * width:(g + 1) * width],
                starts,
                q0,
            )
        )
    soft_out = pieces[0] if shared_heads == 1 else jnp.concatenate(pieces, axis=1)
    return (lin_out, soft_out)


def solution(mesh):
    placed = (
        P("seq", "heads"),
        P("seq", "heads"),
        P("seq", "heads"),
        P("heads"),
        P("heads"),
        P("seq", "heads"),
        P("seq", "heads"),
        P("seq", "heads"),
        P("seq"),
    )
    return jax.shard_map(
        body,
        mesh=mesh,
        in_specs=placed,
        out_specs=(P("seq", "heads"), P("seq", "heads")),
        check_vma=False,
    )
```

```python
import math

import jax
import jax.numpy as jnp
from jax import lax
from jax.experimental import pallas as pl
from jax.experimental.pallas import tpu as pltpu
from jax.sharding import PartitionSpec as P

BLOCK = 256
KEY_BLOCK = 512


def flash_body(sref, q_ref, k_ref, v_ref, st_ref, o_ref, m_ref, l_ref, acc_ref, *, heads, width, scale):
    j = pl.program_id(0)
    lo, hi, flo, fhi, q0 = sref[0], sref[1], sref[2], sref[3], sref[4]
    rows = q_ref.shape[0]
    kb = k_ref.shape[0]

    @pl.when(j == 0)
    def _():
        m_ref[...] = jnp.full(m_ref.shape, -1e30, jnp.float32)
        l_ref[...] = jnp.zeros(l_ref.shape, jnp.float32)
        acc_ref[...] = jnp.zeros(acc_ref.shape, jnp.float32)

    def step(masked):
        k = k_ref[...]
        v = v_ref[...]
        if masked:
            kpos = j * kb + lax.broadcasted_iota(jnp.int32, (rows, kb), 1)
            qpos = q0 + lax.broadcasted_iota(jnp.int32, (rows, kb), 0)
            valid = (kpos <= qpos) & (kpos >= st_ref[...])
        for h in range(heads):
            q = q_ref[:, h * width:(h + 1) * width]
            s = lax.dot_general(q, k, (((1,), (1,)), ((), ())), preferred_element_type=jnp.float32) * scale
            m_prev = m_ref[h]
            if masked:
                top = jnp.max(jnp.where(valid, s, -1e30), axis=1, keepdims=True)
            else:
                top = jnp.max(s, axis=1, keepdims=True)
            m_new = jnp.maximum(m_prev, top)
            corr = jnp.exp(m_prev - m_new)
            e = jnp.exp(s - m_new)
            p = jnp.where(valid, e, 0.0) if masked else e
            l_ref[h] = l_ref[h] * corr + jnp.sum(p, axis=1, keepdims=True)
            pv = jnp.dot(p.astype(jnp.bfloat16), v, preferred_element_type=jnp.float32)
            acc_ref[h] = acc_ref[h] * corr + pv
            m_ref[h] = m_new

    inside = (j >= lo) & (j <= hi)
    full = (j >= flo) & (j <= fhi)

    @pl.when(inside & full)
    def _():
        step(False)

    @pl.when(inside & jnp.logical_not(full))
    def _():
        step(True)

    @pl.when(j == pl.num_programs(0) - 1)
    def _():
        for h in range(heads):
            o_ref[:, h * width:(h + 1) * width] = (acc_ref[h] / l_ref[h]).astype(o_ref.dtype)


def flash_attention(q, keys, values, starts, q0):
    rows, total = q.shape
    length, width = keys.shape
    heads = total // width
    kb = min(KEY_BLOCK, length)
    nk = length // kb
    scale = 1.0 / math.sqrt(width)
    first = starts[0]
    last_start = starts[rows - 1]
    lo = first // kb
    hi = (q0 + rows - 1) // kb
    flo = (last_start + kb - 1) // kb
    fhi = (q0 + 1) // kb - 1
    sref = jnp.stack([lo, hi, flo, fhi, q0]).astype(jnp.int32)

    def kv_map(j, s):
        return (jnp.minimum(jnp.maximum(j, s[0]), s[1]), 0)

    kernel = lambda *refs: flash_body(*refs, heads=heads, width=width, scale=scale)
    return pl.pallas_call(
        kernel,
        out_shape=jax.ShapeDtypeStruct((rows, total), jnp.bfloat16),
        grid_spec=pltpu.PrefetchScalarGridSpec(
            num_scalar_prefetch=1,
            grid=(nk,),
            in_specs=[
                pl.BlockSpec((rows, total), lambda j, s: (0, 0)),
                pl.BlockSpec((kb, width), kv_map),
                pl.BlockSpec((kb, width), kv_map),
                pl.BlockSpec((rows, 1), lambda j, s: (0, 0)),
            ],
            out_specs=pl.BlockSpec((rows, total), lambda j, s: (0, 0)),
            scratch_shapes=[
                pltpu.VMEM((heads, rows, 1), jnp.float32),
                pltpu.VMEM((heads, rows, 1), jnp.float32),
                pltpu.VMEM((heads, rows, width), jnp.float32),
            ],
        ),
        compiler_params=pltpu.CompilerParams(dimension_semantics=("arbitrary",)),
        cost_estimate=pl.CostEstimate(
            flops=4 * rows * heads * length * width // 2,
            transcendentals=rows * heads * length // 2,
            bytes_accessed=2 * length * width * 2 + 2 * rows * total * 2,
        ),
    )(sref, q, keys, values, starts.reshape(rows, 1))


def light_block(carry, inputs, rates):
    state, last_prev = carry
    q_blk, k_blk, v_blk, seg_blk = inputs
    size = q_blk.shape[0]
    seg_f = seg_blk.astype(jnp.float32)
    pos = jnp.arange(size).astype(jnp.float32)
    diff = pos[:, None] - pos[None, :]
    linked = (diff >= 0.0) & (seg_f[:, None] == seg_f[None, :])
    decay = jnp.exp(-rates[:, None, None] * jnp.maximum(diff, 0.0)[None])
    scores = jnp.einsum("thd,shd->hts", q_blk, k_blk, preferred_element_type=jnp.float32)
    weights = jnp.where(linked[None], scores * decay, 0.0).astype(jnp.bfloat16)
    intra = jnp.einsum("hts,shd->thd", weights, v_blk, preferred_element_type=jnp.float32)
    use = (seg_f == last_prev).astype(jnp.float32)
    coef = jnp.exp(-rates[None, :] * (pos[:, None] + 1.0)) * use[:, None]
    q_state = jnp.einsum(
        "thd,hde->the", q_blk.astype(jnp.float32), state, precision=lax.Precision.HIGHEST
    )
    out = intra + coef[:, :, None] * q_state
    last = seg_f[-1]
    k_weight = (
        jnp.exp(-rates[None, :] * (size - 1.0 - pos[:, None]))
        * (seg_f == last).astype(jnp.float32)[:, None]
    )
    k_dec = (k_blk.astype(jnp.float32) * k_weight[:, :, None]).astype(jnp.bfloat16)
    local = jnp.einsum("shd,she->hde", k_dec, v_blk, preferred_element_type=jnp.float32)
    keep = jnp.where(last == last_prev, 1.0, 0.0) * jnp.exp(-rates * size)
    return ((keep[:, None, None] * state + local, last), out)


def body(lin_q, lin_k, lin_v, decay_rates, norm_gain, soft_q, soft_k, soft_v, segment_ids):
    tok = lin_q.shape[0]
    heads = decay_rates.shape[0]
    width = lin_q.shape[1] // heads
    blocks = tok // BLOCK
    shape4 = (blocks, BLOCK, heads, width)
    init = (jnp.zeros((heads, width, width), jnp.float32), jnp.float32(-1.0))
    step_fn = lambda c, x: light_block(c, x, decay_rates)
    (state_loc, last_loc), outs = lax.scan(
        step_fn,
        init,
        (
            lin_q.reshape(shape4),
            lin_k.reshape(shape4),
            lin_v.reshape(shape4),
            segment_ids.reshape(blocks, BLOCK),
        ),
    )
    local_out = outs.reshape(tok, heads, width)
    mine = lax.axis_index("seq")
    parts = lax.axis_size("seq")
    q0 = (mine * tok).astype(jnp.int32)
    seg_i = segment_ids.astype(jnp.float32)
    last_here = seg_i[tok - 1]
    first_here = (q0 + jnp.sum((seg_i < last_here).astype(jnp.int32))).astype(jnp.float32)
    rows_per = heads * width // parts
    chunks = state_loc.reshape(parts, rows_per, width)
    lane = jnp.arange(width)
    info = jnp.where(lane == 0, last_here, jnp.where(lane == 1, first_here, 0.0))
    info = jnp.broadcast_to(info[None, None, :], (parts, 8, width))
    sent = lax.all_to_all(jnp.concatenate([chunks, info], axis=1), "seq", 0, 0)
    lasts = sent[:, rows_per, 0]
    firsts = sent[:, rows_per, 1]
    idx = jnp.arange(parts)
    last_prev = jnp.where(idx >= 1, jnp.roll(lasts, 1), -1.0)
    rate = decay_rates[(mine * rows_per) // width]
    gap = jnp.maximum(idx[:, None] - 1 - idx[None, :], 0).astype(jnp.float32)
    linked = (idx[None, :] < idx[:, None]) & (lasts[None, :] == last_prev[:, None])
    weight = jnp.where(linked, jnp.exp(-rate * tok * gap), 0.0)
    mixed = jnp.einsum(
        "pj,jrc->prc", weight, sent[:, :rows_per, :], precision=lax.Precision.HIGHEST
    )
    state_in = lax.all_to_all(mixed, "seq", 0, 0).reshape(heads, width, width)
    last_before = last_prev[mine]
    same_doc = (idx < mine) & (lasts == last_before)
    first_before = jnp.min(jnp.where(same_doc, firsts, jnp.float32(tok * parts)))
    last_in = last_before.reshape(1)
    seg_f = segment_ids.astype(jnp.float32)
    pos = jnp.arange(tok).astype(jnp.float32)
    coef = (
        jnp.exp(-decay_rates[None, :] * (pos[:, None] + 1.0))
        * (seg_f == last_in[0]).astype(jnp.float32)[:, None]
    )
    q_three = lin_q.reshape(tok, heads, width)
    q_state = jnp.einsum(
        "thd,hde->the", q_three.astype(jnp.float32), state_in, precision=lax.Precision.HIGHEST
    )
    raw = (local_out + coef[:, :, None] * q_state).reshape(tok, heads * width)
    sums = jnp.sum(raw * raw, axis=1)
    total_sq = lax.psum(sums, "heads")
    count = lax.axis_size("heads") * heads * width
    lin_out = (raw * lax.rsqrt(total_sq / count + 1e-06)[:, None] * norm_gain[None, :]).astype(
        jnp.bfloat16
    )
    shared_heads = soft_k.shape[1] // width
    group = heads // shared_heads
    window = jnp.concatenate([soft_k, soft_v], axis=1)
    reach = 1
    while reach < parts:
        pairs = [(i, i + reach) for i in range(parts - reach)]
        window = jnp.concatenate([lax.ppermute(window, "seq", pairs), window], axis=0)
        reach *= 2
    padded = jnp.concatenate([window, jnp.zeros_like(window[: (parts - 1) * tok])], axis=0)
    ordered = lax.dynamic_slice_in_dim(padded, (parts - 1 - mine) * tok, parts * tok, axis=0)
    kv_cols = soft_k.shape[1]
    keys = ordered[:, :kv_cols]
    values = ordered[:, kv_cols:]
    below = jnp.sum((seg_i[None, :] < seg_i[:, None]).astype(jnp.int32), axis=1)
    starts = jnp.where(
        seg_i == last_before, first_before.astype(jnp.int32), q0 + below
    )
    pieces = []
    for g in range(shared_heads):
        cols = slice(g * group * width, (g + 1) * group * width)
        pieces.append(
            flash_attention(
                soft_q[:, cols],
                keys[:, g * width:(g + 1) * width],
                values[:, g * width:(g + 1) * width],
                starts,
                q0,
            )
        )
    soft_out = pieces[0] if shared_heads == 1 else jnp.concatenate(pieces, axis=1)
    return (lin_out, soft_out)


def solution(mesh):
    placed = (
        P("seq", "heads"),
        P("seq", "heads"),
        P("seq", "heads"),
        P("heads"),
        P("heads"),
        P("seq", "heads"),
        P("seq", "heads"),
        P("seq", "heads"),
        P("seq"),
    )
    return jax.shard_map(
        body,
        mesh=mesh,
        in_specs=placed,
        out_specs=(P("seq", "heads"), P("seq", "heads")),
        check_vma=False,
    )
```

```python
import math

import jax
import jax.numpy as jnp
from jax import lax
from jax.experimental import pallas as pl
from jax.experimental.pallas import tpu as pltpu
from jax.sharding import PartitionSpec as P

BLOCK = 256
KEY_BLOCK = 512


def flash_body(sref, q_ref, k_ref, v_ref, st_ref, o_ref, m_ref, l_ref, acc_ref, *, heads, width, scale):
    j = pl.program_id(0)
    lo, hi, flo, fhi, q0 = sref[0], sref[1], sref[2], sref[3], sref[4]
    rows = q_ref.shape[0]
    kb = k_ref.shape[0]

    @pl.when(j == 0)
    def _():
        m_ref[...] = jnp.full(m_ref.shape, -1e30, jnp.float32)
        l_ref[...] = jnp.zeros(l_ref.shape, jnp.float32)
        acc_ref[...] = jnp.zeros(acc_ref.shape, jnp.float32)

    def step(masked):
        k = k_ref[...]
        v = v_ref[...]
        if masked:
            kpos = j * kb + lax.broadcasted_iota(jnp.int32, (rows, kb), 1)
            qpos = q0 + lax.broadcasted_iota(jnp.int32, (rows, kb), 0)
            valid = (kpos <= qpos) & (kpos >= st_ref[...])
        for h in range(heads):
            q = q_ref[:, h * width:(h + 1) * width]
            s = lax.dot_general(q, k, (((1,), (1,)), ((), ())), preferred_element_type=jnp.float32) * scale
            m_prev = m_ref[h]
            if masked:
                top = jnp.max(jnp.where(valid, s, -1e30), axis=1, keepdims=True)
            else:
                top = jnp.max(s, axis=1, keepdims=True)
            m_new = jnp.maximum(m_prev, top)
            corr = jnp.exp(m_prev - m_new)
            e = jnp.exp(s - m_new)
            p = jnp.where(valid, e, 0.0) if masked else e
            l_ref[h] = l_ref[h] * corr + jnp.sum(p, axis=1, keepdims=True)
            pv = jnp.dot(p.astype(jnp.bfloat16), v, preferred_element_type=jnp.float32)
            acc_ref[h] = acc_ref[h] * corr + pv
            m_ref[h] = m_new

    inside = (j >= lo) & (j <= hi)
    full = (j >= flo) & (j <= fhi)

    @pl.when(inside & full)
    def _():
        step(False)

    @pl.when(inside & jnp.logical_not(full))
    def _():
        step(True)

    @pl.when(j == pl.num_programs(0) - 1)
    def _():
        for h in range(heads):
            o_ref[:, h * width:(h + 1) * width] = (acc_ref[h] / l_ref[h]).astype(o_ref.dtype)


def flash_attention(q, keys, values, starts, q0):
    rows, total = q.shape
    length, width = keys.shape
    heads = total // width
    kb = min(KEY_BLOCK, length)
    nk = length // kb
    scale = 1.0 / math.sqrt(width)
    first = starts[0]
    last_start = starts[rows - 1]
    lo = first // kb
    hi = (q0 + rows - 1) // kb
    flo = (last_start + kb - 1) // kb
    fhi = (q0 + 1) // kb - 1
    sref = jnp.stack([lo, hi, flo, fhi, q0]).astype(jnp.int32)

    def kv_map(j, s):
        return (jnp.minimum(jnp.maximum(j, s[0]), s[1]), 0)

    kernel = lambda *refs: flash_body(*refs, heads=heads, width=width, scale=scale)
    return pl.pallas_call(
        kernel,
        out_shape=jax.ShapeDtypeStruct((rows, total), jnp.bfloat16),
        grid_spec=pltpu.PrefetchScalarGridSpec(
            num_scalar_prefetch=1,
            grid=(nk,),
            in_specs=[
                pl.BlockSpec((rows, total), lambda j, s: (0, 0)),
                pl.BlockSpec((kb, width), kv_map),
                pl.BlockSpec((kb, width), kv_map),
                pl.BlockSpec((rows, 1), lambda j, s: (0, 0)),
            ],
            out_specs=pl.BlockSpec((rows, total), lambda j, s: (0, 0)),
            scratch_shapes=[
                pltpu.VMEM((heads, rows, 1), jnp.float32),
                pltpu.VMEM((heads, rows, 1), jnp.float32),
                pltpu.VMEM((heads, rows, width), jnp.float32),
            ],
        ),
        compiler_params=pltpu.CompilerParams(dimension_semantics=("arbitrary",)),
        cost_estimate=pl.CostEstimate(
            flops=4 * rows * heads * length * width // 2,
            transcendentals=rows * heads * length // 2,
            bytes_accessed=2 * length * width * 2 + 2 * rows * total * 2,
        ),
    )(sref, q, keys, values, starts.reshape(rows, 1))


def light_block(carry, inputs, rates):
    state, last_prev = carry
    q_blk, k_blk, v_blk, seg_blk = inputs
    size = q_blk.shape[0]
    seg_f = seg_blk.astype(jnp.float32)
    pos = jnp.arange(size).astype(jnp.float32)
    diff = pos[:, None] - pos[None, :]
    linked = (diff >= 0.0) & (seg_f[:, None] == seg_f[None, :])
    decay = jnp.exp(-rates[:, None, None] * jnp.maximum(diff, 0.0)[None])
    scores = jnp.einsum("thd,shd->hts", q_blk, k_blk, preferred_element_type=jnp.float32)
    weights = jnp.where(linked[None], scores * decay, 0.0).astype(jnp.bfloat16)
    intra = jnp.einsum("hts,shd->thd", weights, v_blk, preferred_element_type=jnp.float32)
    use = (seg_f == last_prev).astype(jnp.float32)
    coef = jnp.exp(-rates[None, :] * (pos[:, None] + 1.0)) * use[:, None]
    q_state = jnp.einsum(
        "thd,hde->the", q_blk.astype(jnp.float32), state, precision=lax.Precision.HIGHEST
    )
    out = intra + coef[:, :, None] * q_state
    last = seg_f[-1]
    k_weight = (
        jnp.exp(-rates[None, :] * (size - 1.0 - pos[:, None]))
        * (seg_f == last).astype(jnp.float32)[:, None]
    )
    k_dec = (k_blk.astype(jnp.float32) * k_weight[:, :, None]).astype(jnp.bfloat16)
    local = jnp.einsum("shd,she->hde", k_dec, v_blk, preferred_element_type=jnp.float32)
    keep = jnp.where(last == last_prev, 1.0, 0.0) * jnp.exp(-rates * size)
    return ((keep[:, None, None] * state + local, last), out)


def body(lin_q, lin_k, lin_v, decay_rates, norm_gain, soft_q, soft_k, soft_v, segment_ids):
    tok = lin_q.shape[0]
    heads = decay_rates.shape[0]
    width = lin_q.shape[1] // heads
    blocks = tok // BLOCK
    shape4 = (blocks, BLOCK, heads, width)
    init = (jnp.zeros((heads, width, width), jnp.float32), jnp.float32(-1.0))
    step_fn = lambda c, x: light_block(c, x, decay_rates)
    (state_loc, last_loc), outs = lax.scan(
        step_fn,
        init,
        (
            lin_q.reshape(shape4),
            lin_k.reshape(shape4),
            lin_v.reshape(shape4),
            segment_ids.reshape(blocks, BLOCK),
        ),
    )
    local_out = outs.reshape(tok, heads, width)
    mine = lax.axis_index("seq")
    parts = lax.axis_size("seq")
    q0 = (mine * tok).astype(jnp.int32)
    seg_i = segment_ids.astype(jnp.float32)
    last_here = seg_i[tok - 1]
    first_here = (q0 + jnp.sum((seg_i < last_here).astype(jnp.int32))).astype(jnp.float32)
    rows_per = heads * width // parts
    chunks = state_loc.reshape(parts, rows_per, width)
    lane = jnp.arange(width)
    info = jnp.where(lane == 0, last_here, jnp.where(lane == 1, first_here, 0.0))
    info = jnp.broadcast_to(info[None, None, :], (parts, 8, width))
    sent = lax.all_to_all(jnp.concatenate([chunks, info], axis=1), "seq", 0, 0)
    lasts = sent[:, rows_per, 0]
    firsts = sent[:, rows_per, 1]
    idx = jnp.arange(parts)
    last_prev = jnp.where(idx >= 1, jnp.roll(lasts, 1), -1.0)
    rate = decay_rates[(mine * rows_per) // width]
    gap = jnp.maximum(idx[:, None] - 1 - idx[None, :], 0).astype(jnp.float32)
    linked = (idx[None, :] < idx[:, None]) & (lasts[None, :] == last_prev[:, None])
    weight = jnp.where(linked, jnp.exp(-rate * tok * gap), 0.0)
    mixed = jnp.einsum(
        "pj,jrc->prc", weight, sent[:, :rows_per, :], precision=lax.Precision.HIGHEST
    )
    state_in = lax.all_to_all(mixed, "seq", 0, 0).reshape(heads, width, width)
    last_before = last_prev[mine]
    same_doc = (idx < mine) & (lasts == last_before)
    first_before = jnp.min(jnp.where(same_doc, firsts, jnp.float32(tok * parts)))
    last_in = last_before.reshape(1)
    seg_f = segment_ids.astype(jnp.float32)
    pos = jnp.arange(tok).astype(jnp.float32)
    coef = (
        jnp.exp(-decay_rates[None, :] * (pos[:, None] + 1.0))
        * (seg_f == last_in[0]).astype(jnp.float32)[:, None]
    )
    q_three = lin_q.reshape(tok, heads, width)
    q_state = jnp.einsum(
        "thd,hde->the", q_three.astype(jnp.float32), state_in, precision=lax.Precision.HIGHEST
    )
    raw = (local_out + coef[:, :, None] * q_state).reshape(tok, heads * width)
    sums = jnp.sum(raw * raw, axis=1)
    total_sq = lax.psum(sums, "heads")
    count = lax.axis_size("heads") * heads * width
    lin_out = (raw * lax.rsqrt(total_sq / count + 1e-06)[:, None] * norm_gain[None, :]).astype(
        jnp.bfloat16
    )
    shared_heads = soft_k.shape[1] // width
    group = heads // shared_heads
    both = lax.all_gather(jnp.concatenate([soft_k, soft_v], axis=1), "seq", axis=0, tiled=True)
    kv_cols = soft_k.shape[1]
    keys = both[:, :kv_cols]
    values = both[:, kv_cols:]
    below = jnp.sum((seg_i[None, :] < seg_i[:, None]).astype(jnp.int32), axis=1)
    starts = jnp.where(
        seg_i == last_before, first_before.astype(jnp.int32), q0 + below
    )
    pieces = []
    for g in range(shared_heads):
        cols = slice(g * group * width, (g + 1) * group * width)
        pieces.append(
            flash_attention(
                soft_q[:, cols],
                keys[:, g * width:(g + 1) * width],
                values[:, g * width:(g + 1) * width],
                starts,
                q0,
            )
        )
    soft_out = pieces[0] if shared_heads == 1 else jnp.concatenate(pieces, axis=1)
    return (lin_out, soft_out)


def solution(mesh):
    placed = (
        P("seq", "heads"),
        P("seq", "heads"),
        P("seq", "heads"),
        P("heads"),
        P("heads"),
        P("seq", "heads"),
        P("seq", "heads"),
        P("seq", "heads"),
        P("seq"),
    )
    return jax.shard_map(
        body,
        mesh=mesh,
        in_specs=placed,
        out_specs=(P("seq", "heads"), P("seq", "heads")),
        check_vma=False,
    )
```

```python
import math

import jax
import jax.numpy as jnp
from jax import lax
from jax.experimental import pallas as pl
from jax.experimental.pallas import tpu as pltpu
from jax.sharding import PartitionSpec as P

BLOCK = 256
KEY_BLOCK = 512


def flash_body(sref, q_ref, k_ref, v_ref, st_ref, o_ref, m_ref, l_ref, acc_ref, *, heads, width, scale):
    j = pl.program_id(0)
    lo, hi, flo, fhi, q0 = sref[0], sref[1], sref[2], sref[3], sref[4]
    rows = q_ref.shape[0]
    kb = k_ref.shape[0]

    @pl.when(j == 0)
    def _():
        m_ref[...] = jnp.full(m_ref.shape, -1e30, jnp.float32)
        l_ref[...] = jnp.zeros(l_ref.shape, jnp.float32)
        acc_ref[...] = jnp.zeros(acc_ref.shape, jnp.float32)

    def step(masked):
        k = k_ref[...]
        v = v_ref[...]
        if masked:
            kpos = j * kb + lax.broadcasted_iota(jnp.int32, (rows, kb), 1)
            qpos = q0 + lax.broadcasted_iota(jnp.int32, (rows, kb), 0)
            valid = (kpos <= qpos) & (kpos >= st_ref[...])
        for h in range(heads):
            q = q_ref[:, h * width:(h + 1) * width]
            s = lax.dot_general(q, k, (((1,), (1,)), ((), ())), preferred_element_type=jnp.float32) * scale
            m_prev = m_ref[h]
            if masked:
                top = jnp.max(jnp.where(valid, s, -1e30), axis=1, keepdims=True)
            else:
                top = jnp.max(s, axis=1, keepdims=True)
            m_new = jnp.maximum(m_prev, top)
            corr = jnp.exp(m_prev - m_new)
            e = jnp.exp(s - m_new)
            p = jnp.where(valid, e, 0.0) if masked else e
            l_ref[h] = l_ref[h] * corr + jnp.sum(p, axis=1, keepdims=True)
            pv = jnp.dot(p.astype(jnp.bfloat16), v, preferred_element_type=jnp.float32)
            acc_ref[h] = acc_ref[h] * corr + pv
            m_ref[h] = m_new

    inside = (j >= lo) & (j <= hi)
    full = (j >= flo) & (j <= fhi)

    @pl.when(inside & full)
    def _():
        step(False)

    @pl.when(inside & jnp.logical_not(full))
    def _():
        step(True)

    @pl.when(j == pl.num_programs(0) - 1)
    def _():
        for h in range(heads):
            o_ref[:, h * width:(h + 1) * width] = (acc_ref[h] / l_ref[h]).astype(o_ref.dtype)


def flash_attention(q, keys, values, starts, q0):
    rows, total = q.shape
    length, width = keys.shape
    heads = total // width
    kb = min(KEY_BLOCK, length)
    nk = length // kb
    scale = 1.0 / math.sqrt(width)
    first = starts[0]
    last_start = starts[rows - 1]
    lo = first // kb
    hi = (q0 + rows - 1) // kb
    flo = (last_start + kb - 1) // kb
    fhi = (q0 + 1) // kb - 1
    sref = jnp.stack([lo, hi, flo, fhi, q0]).astype(jnp.int32)

    def kv_map(j, s):
        return (jnp.minimum(jnp.maximum(j, s[0]), s[1]), 0)

    kernel = lambda *refs: flash_body(*refs, heads=heads, width=width, scale=scale)
    return pl.pallas_call(
        kernel,
        out_shape=jax.ShapeDtypeStruct((rows, total), jnp.bfloat16),
        grid_spec=pltpu.PrefetchScalarGridSpec(
            num_scalar_prefetch=1,
            grid=(nk,),
            in_specs=[
                pl.BlockSpec((rows, total), lambda j, s: (0, 0)),
                pl.BlockSpec((kb, width), kv_map),
                pl.BlockSpec((kb, width), kv_map),
                pl.BlockSpec((rows, 1), lambda j, s: (0, 0)),
            ],
            out_specs=pl.BlockSpec((rows, total), lambda j, s: (0, 0)),
            scratch_shapes=[
                pltpu.VMEM((heads, rows, 1), jnp.float32),
                pltpu.VMEM((heads, rows, 1), jnp.float32),
                pltpu.VMEM((heads, rows, width), jnp.float32),
            ],
        ),
        compiler_params=pltpu.CompilerParams(dimension_semantics=("arbitrary",)),
        cost_estimate=pl.CostEstimate(
            flops=4 * rows * heads * length * width // 2,
            transcendentals=rows * heads * length // 2,
            bytes_accessed=2 * length * width * 2 + 2 * rows * total * 2,
        ),
    )(sref, q, keys, values, starts.reshape(rows, 1))


def light_block(carry, inputs, rates):
    state, last_prev = carry
    q_blk, k_blk, v_blk, seg_blk = inputs
    size = q_blk.shape[0]
    seg_f = seg_blk.astype(jnp.float32)
    pos = jnp.arange(size).astype(jnp.float32)
    diff = pos[:, None] - pos[None, :]
    linked = (diff >= 0.0) & (seg_f[:, None] == seg_f[None, :])
    decay = jnp.exp(-rates[:, None, None] * jnp.maximum(diff, 0.0)[None])
    scores = jnp.einsum("thd,shd->hts", q_blk, k_blk, preferred_element_type=jnp.float32)
    weights = jnp.where(linked[None], scores * decay, 0.0).astype(jnp.bfloat16)
    intra = jnp.einsum("hts,shd->thd", weights, v_blk, preferred_element_type=jnp.float32)
    use = (seg_f == last_prev).astype(jnp.float32)
    coef = jnp.exp(-rates[None, :] * (pos[:, None] + 1.0)) * use[:, None]
    q_state = jnp.einsum(
        "thd,hde->the", q_blk.astype(jnp.float32), state, precision=lax.Precision.HIGHEST
    )
    out = intra + coef[:, :, None] * q_state
    last = seg_f[-1]
    k_weight = (
        jnp.exp(-rates[None, :] * (size - 1.0 - pos[:, None]))
        * (seg_f == last).astype(jnp.float32)[:, None]
    )
    k_dec = (k_blk.astype(jnp.float32) * k_weight[:, :, None]).astype(jnp.bfloat16)
    local = jnp.einsum("shd,she->hde", k_dec, v_blk, preferred_element_type=jnp.float32)
    keep = jnp.where(last == last_prev, 1.0, 0.0) * jnp.exp(-rates * size)
    return ((keep[:, None, None] * state + local, last), out)


def body(lin_q, lin_k, lin_v, decay_rates, norm_gain, soft_q, soft_k, soft_v, segment_ids):
    tok = lin_q.shape[0]
    heads = decay_rates.shape[0]
    width = lin_q.shape[1] // heads
    blocks = tok // BLOCK
    shape4 = (blocks, BLOCK, heads, width)
    init = (jnp.zeros((heads, width, width), jnp.float32), jnp.float32(-1.0))
    step_fn = lambda c, x: light_block(c, x, decay_rates)
    (state_loc, last_loc), outs = lax.scan(
        step_fn,
        init,
        (
            lin_q.reshape(shape4),
            lin_k.reshape(shape4),
            lin_v.reshape(shape4),
            segment_ids.reshape(blocks, BLOCK),
        ),
    )
    local_out = outs.reshape(tok, heads, width)
    mine = lax.axis_index("seq")
    parts = lax.axis_size("seq")
    q0 = (mine * tok).astype(jnp.int32)
    seg_i = segment_ids.astype(jnp.float32)
    last_here = seg_i[tok - 1]
    first_here = (q0 + jnp.sum((seg_i < last_here).astype(jnp.int32))).astype(jnp.float32)
    rows_per = heads * width // parts
    chunks = state_loc.reshape(parts, rows_per, width)
    lane = jnp.arange(width)
    info = jnp.where(lane == 0, last_here, jnp.where(lane == 1, first_here, 0.0))
    info = jnp.broadcast_to(info[None, None, :], (parts, 8, width))
    sent = lax.all_to_all(jnp.concatenate([chunks, info], axis=1), "seq", 0, 0)
    lasts = sent[:, rows_per, 0]
    firsts = sent[:, rows_per, 1]
    idx = jnp.arange(parts)
    last_prev = jnp.where(idx >= 1, jnp.roll(lasts, 1), -1.0)
    rate = decay_rates[(mine * rows_per) // width]
    gap = jnp.maximum(idx[:, None] - 1 - idx[None, :], 0).astype(jnp.float32)
    linked = (idx[None, :] < idx[:, None]) & (lasts[None, :] == last_prev[:, None])
    weight = jnp.where(linked, jnp.exp(-rate * tok * gap), 0.0)
    mixed = jnp.einsum(
        "pj,jrc->prc", weight, sent[:, :rows_per, :], precision=lax.Precision.HIGHEST
    )
    state_in = lax.all_to_all(mixed, "seq", 0, 0).reshape(heads, width, width)
    last_before = last_prev[mine]
    same_doc = (idx < mine) & (lasts == last_before)
    first_before = jnp.min(jnp.where(same_doc, firsts, jnp.float32(tok * parts)))
    last_in = last_before.reshape(1)
    shared_heads = soft_k.shape[1] // width
    group = heads // shared_heads
    both = lax.all_gather(jnp.concatenate([soft_k, soft_v], axis=1), "seq", axis=0, tiled=True)
    kv_cols = soft_k.shape[1]
    keys = both[:, :kv_cols]
    values = both[:, kv_cols:]
    below = jnp.sum((seg_i[None, :] < seg_i[:, None]).astype(jnp.int32), axis=1)
    starts = jnp.where(
        seg_i == last_before, first_before.astype(jnp.int32), q0 + below
    )
    pieces = []
    for g in range(shared_heads):
        cols = slice(g * group * width, (g + 1) * group * width)
        pieces.append(
            flash_attention(
                soft_q[:, cols],
                keys[:, g * width:(g + 1) * width],
                values[:, g * width:(g + 1) * width],
                starts,
                q0,
            )
        )
    soft_out = pieces[0] if shared_heads == 1 else jnp.concatenate(pieces, axis=1)
    soft_out, state_in = lax.optimization_barrier((soft_out, state_in))
    seg_f = segment_ids.astype(jnp.float32)
    pos = jnp.arange(tok).astype(jnp.float32)
    coef = (
        jnp.exp(-decay_rates[None, :] * (pos[:, None] + 1.0))
        * (seg_f == last_in[0]).astype(jnp.float32)[:, None]
    )
    q_three = lin_q.reshape(tok, heads, width)
    q_state = jnp.einsum(
        "thd,hde->the", q_three.astype(jnp.float32), state_in, precision=lax.Precision.HIGHEST
    )
    raw = (local_out + coef[:, :, None] * q_state).reshape(tok, heads * width)
    sums = jnp.sum(raw * raw, axis=1)
    total_sq = lax.psum(sums, "heads")
    count = lax.axis_size("heads") * heads * width
    lin_out = (raw * lax.rsqrt(total_sq / count + 1e-06)[:, None] * norm_gain[None, :]).astype(
        jnp.bfloat16
    )
    return (lin_out, soft_out)


def solution(mesh):
    placed = (
        P("seq", "heads"),
        P("seq", "heads"),
        P("seq", "heads"),
        P("heads"),
        P("heads"),
        P("seq", "heads"),
        P("seq", "heads"),
        P("seq", "heads"),
        P("seq"),
    )
    return jax.shard_map(
        body,
        mesh=mesh,
        in_specs=placed,
        out_specs=(P("seq", "heads"), P("seq", "heads")),
        check_vma=False,
    )
```

```python
import math

import jax
import jax.numpy as jnp
from jax import lax
from jax.experimental import pallas as pl
from jax.experimental.pallas import tpu as pltpu
from jax.sharding import PartitionSpec as P

BLOCK = 256
KEY_BLOCK = 1024


def flash_body(sref, q_ref, k_ref, v_ref, st_ref, o_ref, m_ref, l_ref, acc_ref, *, heads, width, scale):
    j = pl.program_id(0)
    lo, hi, flo, fhi, q0 = sref[0], sref[1], sref[2], sref[3], sref[4]
    rows = q_ref.shape[0]
    kb = k_ref.shape[0]

    @pl.when(j == 0)
    def _():
        m_ref[...] = jnp.full(m_ref.shape, -1e30, jnp.float32)
        l_ref[...] = jnp.zeros(l_ref.shape, jnp.float32)
        acc_ref[...] = jnp.zeros(acc_ref.shape, jnp.float32)

    def step(masked):
        k = k_ref[...]
        v = v_ref[...]
        if masked:
            kpos = j * kb + lax.broadcasted_iota(jnp.int32, (rows, kb), 1)
            qpos = q0 + lax.broadcasted_iota(jnp.int32, (rows, kb), 0)
            valid = (kpos <= qpos) & (kpos >= st_ref[...])
        for h in range(heads):
            q = q_ref[:, h * width:(h + 1) * width]
            s = lax.dot_general(q, k, (((1,), (1,)), ((), ())), preferred_element_type=jnp.float32) * scale
            m_prev = m_ref[h]
            if masked:
                top = jnp.max(jnp.where(valid, s, -1e30), axis=1, keepdims=True)
            else:
                top = jnp.max(s, axis=1, keepdims=True)
            m_new = jnp.maximum(m_prev, top)
            corr = jnp.exp(m_prev - m_new)
            e = jnp.exp(s - m_new)
            p = jnp.where(valid, e, 0.0) if masked else e
            l_ref[h] = l_ref[h] * corr + jnp.sum(p, axis=1, keepdims=True)
            pv = jnp.dot(p.astype(jnp.bfloat16), v, preferred_element_type=jnp.float32)
            acc_ref[h] = acc_ref[h] * corr + pv
            m_ref[h] = m_new

    inside = (j >= lo) & (j <= hi)
    full = (j >= flo) & (j <= fhi)

    @pl.when(inside & full)
    def _():
        step(False)

    @pl.when(inside & jnp.logical_not(full))
    def _():
        step(True)

    @pl.when(j == pl.num_programs(0) - 1)
    def _():
        for h in range(heads):
            o_ref[:, h * width:(h + 1) * width] = (acc_ref[h] / l_ref[h]).astype(o_ref.dtype)


def flash_attention(q, both, starts, q0):
    rows, total = q.shape
    length = both.shape[0]
    width = both.shape[1] // 2
    heads = total // width
    kb = min(KEY_BLOCK, length)
    nk = length // kb
    scale = 1.0 / math.sqrt(width)
    first = starts[0]
    last_start = starts[rows - 1]
    lo = first // kb
    hi = (q0 + rows - 1) // kb
    flo = (last_start + kb - 1) // kb
    fhi = (q0 + 1) // kb - 1
    sref = jnp.stack([lo, hi, flo, fhi, q0]).astype(jnp.int32)

    def k_map(j, s):
        return (jnp.minimum(jnp.maximum(j, s[0]), s[1]), 0)

    def v_map(j, s):
        return (jnp.minimum(jnp.maximum(j, s[0]), s[1]), 1)

    kernel = lambda *refs: flash_body(*refs, heads=heads, width=width, scale=scale)
    return pl.pallas_call(
        kernel,
        out_shape=jax.ShapeDtypeStruct((rows, total), jnp.bfloat16),
        grid_spec=pltpu.PrefetchScalarGridSpec(
            num_scalar_prefetch=1,
            grid=(nk,),
            in_specs=[
                pl.BlockSpec((rows, total), lambda j, s: (0, 0)),
                pl.BlockSpec((kb, width), k_map),
                pl.BlockSpec((kb, width), v_map),
                pl.BlockSpec((rows, 1), lambda j, s: (0, 0)),
            ],
            out_specs=pl.BlockSpec((rows, total), lambda j, s: (0, 0)),
            scratch_shapes=[
                pltpu.VMEM((heads, rows, 1), jnp.float32),
                pltpu.VMEM((heads, rows, 1), jnp.float32),
                pltpu.VMEM((heads, rows, width), jnp.float32),
            ],
        ),
        compiler_params=pltpu.CompilerParams(dimension_semantics=("arbitrary",)),
        cost_estimate=pl.CostEstimate(
            flops=4 * rows * heads * length * width // 2,
            transcendentals=rows * heads * length // 2,
            bytes_accessed=2 * length * width * 2 + 2 * rows * total * 2,
        ),
    )(sref, q, both, both, starts.reshape(rows, 1))


def light_block(carry, inputs, rates):
    state, last_prev = carry
    q_blk, k_blk, v_blk, seg_blk = inputs
    size = q_blk.shape[0]
    seg_f = seg_blk.astype(jnp.float32)
    pos = jnp.arange(size).astype(jnp.float32)
    diff = pos[:, None] - pos[None, :]
    linked = (diff >= 0.0) & (seg_f[:, None] == seg_f[None, :])
    decay = jnp.exp(-rates[:, None, None] * jnp.maximum(diff, 0.0)[None])
    scores = jnp.einsum("thd,shd->hts", q_blk, k_blk, preferred_element_type=jnp.float32)
    weights = jnp.where(linked[None], scores * decay, 0.0).astype(jnp.bfloat16)
    intra = jnp.einsum("hts,shd->thd", weights, v_blk, preferred_element_type=jnp.float32)
    use = (seg_f == last_prev).astype(jnp.float32)
    coef = jnp.exp(-rates[None, :] * (pos[:, None] + 1.0)) * use[:, None]
    q_state = jnp.einsum(
        "thd,hde->the", q_blk.astype(jnp.float32), state, precision=lax.Precision.HIGHEST
    )
    out = intra + coef[:, :, None] * q_state
    last = seg_f[-1]
    k_weight = (
        jnp.exp(-rates[None, :] * (size - 1.0 - pos[:, None]))
        * (seg_f == last).astype(jnp.float32)[:, None]
    )
    k_dec = (k_blk.astype(jnp.float32) * k_weight[:, :, None]).astype(jnp.bfloat16)
    local = jnp.einsum("shd,she->hde", k_dec, v_blk, preferred_element_type=jnp.float32)
    keep = jnp.where(last == last_prev, 1.0, 0.0) * jnp.exp(-rates * size)
    return ((keep[:, None, None] * state + local, last), out)


def body(lin_q, lin_k, lin_v, decay_rates, norm_gain, soft_q, soft_k, soft_v, segment_ids):
    tok = lin_q.shape[0]
    heads = decay_rates.shape[0]
    width = lin_q.shape[1] // heads
    blocks = tok // BLOCK
    shape4 = (blocks, BLOCK, heads, width)
    init = (jnp.zeros((heads, width, width), jnp.float32), jnp.float32(-1.0))
    step_fn = lambda c, x: light_block(c, x, decay_rates)
    (state_loc, last_loc), outs = lax.scan(
        step_fn,
        init,
        (
            lin_q.reshape(shape4),
            lin_k.reshape(shape4),
            lin_v.reshape(shape4),
            segment_ids.reshape(blocks, BLOCK),
        ),
    )
    local_out = outs.reshape(tok, heads, width)
    mine = lax.axis_index("seq")
    parts = lax.axis_size("seq")
    q0 = (mine * tok).astype(jnp.int32)
    seg_i = segment_ids.astype(jnp.float32)
    last_here = seg_i[tok - 1]
    first_here = (q0 + jnp.sum((seg_i < last_here).astype(jnp.int32))).astype(jnp.float32)
    rows_per = heads * width // parts
    chunks = state_loc.reshape(parts, rows_per, width)
    lane = jnp.arange(width)
    info = jnp.where(lane == 0, last_here, jnp.where(lane == 1, first_here, 0.0))
    info = jnp.broadcast_to(info[None, None, :], (parts, 8, width))
    sent = lax.all_to_all(jnp.concatenate([chunks, info], axis=1), "seq", 0, 0)
    lasts = sent[:, rows_per, 0]
    firsts = sent[:, rows_per, 1]
    idx = jnp.arange(parts)
    last_prev = jnp.where(idx >= 1, jnp.roll(lasts, 1), -1.0)
    rate = decay_rates[(mine * rows_per) // width]
    gap = jnp.maximum(idx[:, None] - 1 - idx[None, :], 0).astype(jnp.float32)
    linked = (idx[None, :] < idx[:, None]) & (lasts[None, :] == last_prev[:, None])
    weight = jnp.where(linked, jnp.exp(-rate * tok * gap), 0.0)
    mixed = jnp.einsum(
        "pj,jrc->prc", weight, sent[:, :rows_per, :], precision=lax.Precision.HIGHEST
    )
    state_in = lax.all_to_all(mixed, "seq", 0, 0).reshape(heads, width, width)
    last_before = last_prev[mine]
    same_doc = (idx < mine) & (lasts == last_before)
    first_before = jnp.min(jnp.where(same_doc, firsts, jnp.float32(tok * parts)))
    last_in = last_before.reshape(1)
    seg_f = segment_ids.astype(jnp.float32)
    pos = jnp.arange(tok).astype(jnp.float32)
    coef = (
        jnp.exp(-decay_rates[None, :] * (pos[:, None] + 1.0))
        * (seg_f == last_in[0]).astype(jnp.float32)[:, None]
    )
    q_three = lin_q.reshape(tok, heads, width)
    q_state = jnp.einsum(
        "thd,hde->the", q_three.astype(jnp.float32), state_in, precision=lax.Precision.HIGHEST
    )
    raw = (local_out + coef[:, :, None] * q_state).reshape(tok, heads * width)
    sums = jnp.sum(raw * raw, axis=1)
    total_sq = lax.psum(sums, "heads")
    count = lax.axis_size("heads") * heads * width
    lin_out = (raw * lax.rsqrt(total_sq / count + 1e-06)[:, None] * norm_gain[None, :]).astype(
        jnp.bfloat16
    )
    shared_heads = soft_k.shape[1] // width
    group = heads // shared_heads
    both = lax.all_gather(jnp.concatenate([soft_k, soft_v], axis=1), "seq", axis=0, tiled=True)
    below = jnp.sum((seg_i[None, :] < seg_i[:, None]).astype(jnp.int32), axis=1)
    starts = jnp.where(
        seg_i == last_before, first_before.astype(jnp.int32), q0 + below
    )
    pieces = []
    for g in range(shared_heads):
        cols = slice(g * group * width, (g + 1) * group * width)
        pieces.append(
            flash_attention(
                soft_q[:, cols],
                both,
                starts,
                q0,
            )
        )
    soft_out = pieces[0] if shared_heads == 1 else jnp.concatenate(pieces, axis=1)
    return (lin_out, soft_out)


def solution(mesh):
    placed = (
        P("seq", "heads"),
        P("seq", "heads"),
        P("seq", "heads"),
        P("heads"),
        P("heads"),
        P("seq", "heads"),
        P("seq", "heads"),
        P("seq", "heads"),
        P("seq"),
    )
    return jax.shard_map(
        body,
        mesh=mesh,
        in_specs=placed,
        out_specs=(P("seq", "heads"), P("seq", "heads")),
        check_vma=False,
    )
```

```python
import math

import jax
import jax.numpy as jnp
from jax import lax
from jax.experimental import pallas as pl
from jax.experimental.pallas import tpu as pltpu
from jax.sharding import PartitionSpec as P

BLOCK = 256
KEY_BLOCK = 1024


def flash_body(sref, q_ref, k_ref, v_ref, st_ref, o_ref, m_ref, l_ref, acc_ref, *, heads, width, scale):
    j = pl.program_id(0)
    lo, hi, flo, fhi, q0 = sref[0], sref[1], sref[2], sref[3], sref[4]
    rows = q_ref.shape[0]
    kb = k_ref.shape[0]

    @pl.when(j == 0)
    def _():
        m_ref[...] = jnp.full(m_ref.shape, -1e30, jnp.float32)
        l_ref[...] = jnp.zeros(l_ref.shape, jnp.float32)
        acc_ref[...] = jnp.zeros(acc_ref.shape, jnp.float32)

    def step(masked):
        k = k_ref[...]
        v = v_ref[...]
        if masked:
            kpos = j * kb + lax.broadcasted_iota(jnp.int32, (rows, kb), 1)
            qpos = q0 + lax.broadcasted_iota(jnp.int32, (rows, kb), 0)
            valid = (kpos <= qpos) & (kpos >= st_ref[...])
        for h in range(heads):
            q = q_ref[:, h * width:(h + 1) * width]
            s = lax.dot_general(q, k, (((1,), (1,)), ((), ())), preferred_element_type=jnp.float32) * scale
            if masked:
                s = jnp.where(valid, s, -jnp.inf)
            m_prev = m_ref[h]
            m_new = jnp.maximum(m_prev, jnp.max(s, axis=1, keepdims=True))
            corr = jnp.exp2(m_prev - m_new)
            p = jnp.exp2(s - m_new)
            l_ref[h] = l_ref[h] * corr + jnp.sum(p, axis=1, keepdims=True)
            pv = jnp.dot(p.astype(jnp.bfloat16), v, preferred_element_type=jnp.float32)
            acc_ref[h] = acc_ref[h] * corr + pv
            m_ref[h] = m_new

    inside = (j >= lo) & (j <= hi)
    full = (j >= flo) & (j <= fhi)

    @pl.when(inside & full)
    def _():
        step(False)

    @pl.when(inside & jnp.logical_not(full))
    def _():
        step(True)

    @pl.when(j == pl.num_programs(0) - 1)
    def _():
        for h in range(heads):
            o_ref[:, h * width:(h + 1) * width] = (acc_ref[h] / l_ref[h]).astype(o_ref.dtype)


def flash_attention(q, both, starts, q0):
    rows, total = q.shape
    length = both.shape[0]
    width = both.shape[1] // 2
    heads = total // width
    kb = min(KEY_BLOCK, length)
    nk = length // kb
    scale = math.log2(math.e) / math.sqrt(width)
    first = starts[0]
    last_start = starts[rows - 1]
    lo = first // kb
    hi = (q0 + rows - 1) // kb
    flo = (last_start + kb - 1) // kb
    fhi = (q0 + 1) // kb - 1
    sref = jnp.stack([lo, hi, flo, fhi, q0]).astype(jnp.int32)

    def k_map(j, s):
        return (jnp.minimum(jnp.maximum(j, s[0]), s[1]), 0)

    def v_map(j, s):
        return (jnp.minimum(jnp.maximum(j, s[0]), s[1]), 1)

    kernel = lambda *refs: flash_body(*refs, heads=heads, width=width, scale=scale)
    return pl.pallas_call(
        kernel,
        out_shape=jax.ShapeDtypeStruct((rows, total), jnp.bfloat16),
        grid_spec=pltpu.PrefetchScalarGridSpec(
            num_scalar_prefetch=1,
            grid=(nk,),
            in_specs=[
                pl.BlockSpec((rows, total), lambda j, s: (0, 0)),
                pl.BlockSpec((kb, width), k_map),
                pl.BlockSpec((kb, width), v_map),
                pl.BlockSpec((rows, 1), lambda j, s: (0, 0)),
            ],
            out_specs=pl.BlockSpec((rows, total), lambda j, s: (0, 0)),
            scratch_shapes=[
                pltpu.VMEM((heads, rows, 1), jnp.float32),
                pltpu.VMEM((heads, rows, 1), jnp.float32),
                pltpu.VMEM((heads, rows, width), jnp.float32),
            ],
        ),
        compiler_params=pltpu.CompilerParams(dimension_semantics=("arbitrary",)),
        cost_estimate=pl.CostEstimate(
            flops=4 * rows * heads * length * width // 2,
            transcendentals=rows * heads * length // 2,
            bytes_accessed=2 * length * width * 2 + 2 * rows * total * 2,
        ),
    )(sref, q, both, both, starts.reshape(rows, 1))


def light_block(carry, inputs, rates):
    state, last_prev = carry
    q_blk, k_blk, v_blk, seg_blk = inputs
    size = q_blk.shape[0]
    seg_f = seg_blk.astype(jnp.float32)
    pos = jnp.arange(size).astype(jnp.float32)
    diff = pos[:, None] - pos[None, :]
    linked = (diff >= 0.0) & (seg_f[:, None] == seg_f[None, :])
    decay = jnp.exp(-rates[:, None, None] * jnp.maximum(diff, 0.0)[None])
    scores = jnp.einsum("thd,shd->hts", q_blk, k_blk, preferred_element_type=jnp.float32)
    weights = jnp.where(linked[None], scores * decay, 0.0).astype(jnp.bfloat16)
    intra = jnp.einsum("hts,shd->thd", weights, v_blk, preferred_element_type=jnp.float32)
    use = (seg_f == last_prev).astype(jnp.float32)
    coef = jnp.exp(-rates[None, :] * (pos[:, None] + 1.0)) * use[:, None]
    q_state = jnp.einsum(
        "thd,hde->the", q_blk.astype(jnp.float32), state, precision=lax.Precision.HIGHEST
    )
    out = intra + coef[:, :, None] * q_state
    last = seg_f[-1]
    k_weight = (
        jnp.exp(-rates[None, :] * (size - 1.0 - pos[:, None]))
        * (seg_f == last).astype(jnp.float32)[:, None]
    )
    k_dec = (k_blk.astype(jnp.float32) * k_weight[:, :, None]).astype(jnp.bfloat16)
    local = jnp.einsum("shd,she->hde", k_dec, v_blk, preferred_element_type=jnp.float32)
    keep = jnp.where(last == last_prev, 1.0, 0.0) * jnp.exp(-rates * size)
    return ((keep[:, None, None] * state + local, last), out)


def body(lin_q, lin_k, lin_v, decay_rates, norm_gain, soft_q, soft_k, soft_v, segment_ids):
    tok = lin_q.shape[0]
    heads = decay_rates.shape[0]
    width = lin_q.shape[1] // heads
    blocks = tok // BLOCK
    shape4 = (blocks, BLOCK, heads, width)
    init = (jnp.zeros((heads, width, width), jnp.float32), jnp.float32(-1.0))
    step_fn = lambda c, x: light_block(c, x, decay_rates)
    (state_loc, last_loc), outs = lax.scan(
        step_fn,
        init,
        (
            lin_q.reshape(shape4),
            lin_k.reshape(shape4),
            lin_v.reshape(shape4),
            segment_ids.reshape(blocks, BLOCK),
        ),
    )
    local_out = outs.reshape(tok, heads, width)
    mine = lax.axis_index("seq")
    parts = lax.axis_size("seq")
    q0 = (mine * tok).astype(jnp.int32)
    seg_i = segment_ids.astype(jnp.float32)
    last_here = seg_i[tok - 1]
    first_here = (q0 + jnp.sum((seg_i < last_here).astype(jnp.int32))).astype(jnp.float32)
    rows_per = heads * width // parts
    chunks = state_loc.reshape(parts, rows_per, width)
    lane = jnp.arange(width)
    info = jnp.where(lane == 0, last_here, jnp.where(lane == 1, first_here, 0.0))
    info = jnp.broadcast_to(info[None, None, :], (parts, 8, width))
    sent = lax.all_to_all(jnp.concatenate([chunks, info], axis=1), "seq", 0, 0)
    lasts = sent[:, rows_per, 0]
    firsts = sent[:, rows_per, 1]
    idx = jnp.arange(parts)
    last_prev = jnp.where(idx >= 1, jnp.roll(lasts, 1), -1.0)
    rate = decay_rates[(mine * rows_per) // width]
    gap = jnp.maximum(idx[:, None] - 1 - idx[None, :], 0).astype(jnp.float32)
    linked = (idx[None, :] < idx[:, None]) & (lasts[None, :] == last_prev[:, None])
    weight = jnp.where(linked, jnp.exp(-rate * tok * gap), 0.0)
    mixed = jnp.einsum(
        "pj,jrc->prc", weight, sent[:, :rows_per, :], precision=lax.Precision.HIGHEST
    )
    state_in = lax.all_to_all(mixed, "seq", 0, 0).reshape(heads, width, width)
    last_before = last_prev[mine]
    same_doc = (idx < mine) & (lasts == last_before)
    first_before = jnp.min(jnp.where(same_doc, firsts, jnp.float32(tok * parts)))
    last_in = last_before.reshape(1)
    seg_f = segment_ids.astype(jnp.float32)
    pos = jnp.arange(tok).astype(jnp.float32)
    coef = (
        jnp.exp(-decay_rates[None, :] * (pos[:, None] + 1.0))
        * (seg_f == last_in[0]).astype(jnp.float32)[:, None]
    )
    q_three = lin_q.reshape(tok, heads, width)
    q_state = jnp.einsum(
        "thd,hde->the", q_three.astype(jnp.float32), state_in, precision=lax.Precision.HIGHEST
    )
    raw = (local_out + coef[:, :, None] * q_state).reshape(tok, heads * width)
    sums = jnp.sum(raw * raw, axis=1)
    total_sq = lax.psum(sums, "heads")
    count = lax.axis_size("heads") * heads * width
    lin_out = (raw * lax.rsqrt(total_sq / count + 1e-06)[:, None] * norm_gain[None, :]).astype(
        jnp.bfloat16
    )
    shared_heads = soft_k.shape[1] // width
    group = heads // shared_heads
    both = lax.all_gather(jnp.concatenate([soft_k, soft_v], axis=1), "seq", axis=0, tiled=True)
    below = jnp.sum((seg_i[None, :] < seg_i[:, None]).astype(jnp.int32), axis=1)
    starts = jnp.where(
        seg_i == last_before, first_before.astype(jnp.int32), q0 + below
    )
    pieces = []
    for g in range(shared_heads):
        cols = slice(g * group * width, (g + 1) * group * width)
        pieces.append(
            flash_attention(
                soft_q[:, cols],
                both,
                starts,
                q0,
            )
        )
    soft_out = pieces[0] if shared_heads == 1 else jnp.concatenate(pieces, axis=1)
    return (lin_out, soft_out)


def solution(mesh):
    placed = (
        P("seq", "heads"),
        P("seq", "heads"),
        P("seq", "heads"),
        P("heads"),
        P("heads"),
        P("seq", "heads"),
        P("seq", "heads"),
        P("seq", "heads"),
        P("seq"),
    )
    return jax.shard_map(
        body,
        mesh=mesh,
        in_specs=placed,
        out_specs=(P("seq", "heads"), P("seq", "heads")),
        check_vma=False,
    )
```

```python
import math

import jax
import jax.numpy as jnp
from jax import lax
from jax.experimental import pallas as pl
from jax.experimental.pallas import tpu as pltpu
from jax.sharding import PartitionSpec as P

BLOCK = 256
KEY_BLOCK = 1024


def flash_body(sref, q_ref, k_ref, v_ref, st_ref, o_ref, m_ref, l_ref, acc_ref, vx_ref, *, heads, width, scale):
    j = pl.program_id(0)
    lo, hi, flo, fhi, q0 = sref[0], sref[1], sref[2], sref[3], sref[4]
    rows = q_ref.shape[0]
    kb = k_ref.shape[0]

    @pl.when(j == 0)
    def _():
        m_ref[...] = jnp.full(m_ref.shape, -1e30, jnp.float32)
        l_ref[...] = jnp.zeros(l_ref.shape, jnp.float32)
        acc_ref[...] = jnp.zeros(acc_ref.shape, jnp.float32)
        vx_ref[:, width:] = jnp.ones((vx_ref.shape[0], width), vx_ref.dtype)

    def step(masked):
        k = k_ref[...]
        vx_ref[:, :width] = v_ref[...]
        vx = vx_ref[...]
        if masked:
            kpos = j * kb + lax.broadcasted_iota(jnp.int32, (rows, kb), 1)
            qpos = q0 + lax.broadcasted_iota(jnp.int32, (rows, kb), 0)
            valid = (kpos <= qpos) & (kpos >= st_ref[...])
        for h in range(heads):
            q = q_ref[:, h * width:(h + 1) * width]
            s = lax.dot_general(q, k, (((1,), (1,)), ((), ())), preferred_element_type=jnp.float32) * scale
            if masked:
                s = jnp.where(valid, s, -jnp.inf)
            m_prev = m_ref[h]
            m_new = jnp.maximum(m_prev, jnp.max(s, axis=1, keepdims=True))
            corr = jnp.exp2(m_prev - m_new)
            p = jnp.exp2(s - m_new)
            pv = jnp.dot(p.astype(jnp.bfloat16), vx, preferred_element_type=jnp.float32)
            l_ref[h] = l_ref[h] * corr + pv[:, width:width + 1]
            acc_ref[h] = acc_ref[h] * corr + pv[:, :width]
            m_ref[h] = m_new

    inside = (j >= lo) & (j <= hi)
    full = (j >= flo) & (j <= fhi)

    @pl.when(inside & full)
    def _():
        step(False)

    @pl.when(inside & jnp.logical_not(full))
    def _():
        step(True)

    @pl.when(j == pl.num_programs(0) - 1)
    def _():
        for h in range(heads):
            o_ref[:, h * width:(h + 1) * width] = (acc_ref[h] / l_ref[h]).astype(o_ref.dtype)


def flash_attention(q, both, starts, q0):
    rows, total = q.shape
    length = both.shape[0]
    width = both.shape[1] // 2
    heads = total // width
    kb = min(KEY_BLOCK, length)
    nk = length // kb
    scale = math.log2(math.e) / math.sqrt(width)
    first = starts[0]
    last_start = starts[rows - 1]
    lo = first // kb
    hi = (q0 + rows - 1) // kb
    flo = (last_start + kb - 1) // kb
    fhi = (q0 + 1) // kb - 1
    sref = jnp.stack([lo, hi, flo, fhi, q0]).astype(jnp.int32)

    def k_map(j, s):
        return (jnp.minimum(jnp.maximum(j, s[0]), s[1]), 0)

    def v_map(j, s):
        return (jnp.minimum(jnp.maximum(j, s[0]), s[1]), 1)

    kernel = lambda *refs: flash_body(*refs, heads=heads, width=width, scale=scale)
    return pl.pallas_call(
        kernel,
        out_shape=jax.ShapeDtypeStruct((rows, total), jnp.bfloat16),
        grid_spec=pltpu.PrefetchScalarGridSpec(
            num_scalar_prefetch=1,
            grid=(nk,),
            in_specs=[
                pl.BlockSpec((rows, total), lambda j, s: (0, 0)),
                pl.BlockSpec((kb, width), k_map),
                pl.BlockSpec((kb, width), v_map),
                pl.BlockSpec((rows, 1), lambda j, s: (0, 0)),
            ],
            out_specs=pl.BlockSpec((rows, total), lambda j, s: (0, 0)),
            scratch_shapes=[
                pltpu.VMEM((heads, rows, 1), jnp.float32),
                pltpu.VMEM((heads, rows, 1), jnp.float32),
                pltpu.VMEM((heads, rows, width), jnp.float32),
                pltpu.VMEM((kb, 2 * width), jnp.bfloat16),
            ],
        ),
        compiler_params=pltpu.CompilerParams(dimension_semantics=("arbitrary",)),
        cost_estimate=pl.CostEstimate(
            flops=4 * rows * heads * length * width // 2,
            transcendentals=rows * heads * length // 2,
            bytes_accessed=2 * length * width * 2 + 2 * rows * total * 2,
        ),
    )(sref, q, both, both, starts.reshape(rows, 1))


def light_block(carry, inputs, rates):
    state, last_prev = carry
    q_blk, k_blk, v_blk, seg_blk = inputs
    size = q_blk.shape[0]
    seg_f = seg_blk.astype(jnp.float32)
    pos = jnp.arange(size).astype(jnp.float32)
    diff = pos[:, None] - pos[None, :]
    linked = (diff >= 0.0) & (seg_f[:, None] == seg_f[None, :])
    decay = jnp.exp(-rates[:, None, None] * jnp.maximum(diff, 0.0)[None])
    scores = jnp.einsum("thd,shd->hts", q_blk, k_blk, preferred_element_type=jnp.float32)
    weights = jnp.where(linked[None], scores * decay, 0.0).astype(jnp.bfloat16)
    intra = jnp.einsum("hts,shd->thd", weights, v_blk, preferred_element_type=jnp.float32)
    use = (seg_f == last_prev).astype(jnp.float32)
    coef = jnp.exp(-rates[None, :] * (pos[:, None] + 1.0)) * use[:, None]
    q_state = jnp.einsum(
        "thd,hde->the", q_blk.astype(jnp.float32), state, precision=lax.Precision.HIGHEST
    )
    out = intra + coef[:, :, None] * q_state
    last = seg_f[-1]
    k_weight = (
        jnp.exp(-rates[None, :] * (size - 1.0 - pos[:, None]))
        * (seg_f == last).astype(jnp.float32)[:, None]
    )
    k_dec = (k_blk.astype(jnp.float32) * k_weight[:, :, None]).astype(jnp.bfloat16)
    local = jnp.einsum("shd,she->hde", k_dec, v_blk, preferred_element_type=jnp.float32)
    keep = jnp.where(last == last_prev, 1.0, 0.0) * jnp.exp(-rates * size)
    return ((keep[:, None, None] * state + local, last), out)


def body(lin_q, lin_k, lin_v, decay_rates, norm_gain, soft_q, soft_k, soft_v, segment_ids):
    tok = lin_q.shape[0]
    heads = decay_rates.shape[0]
    width = lin_q.shape[1] // heads
    blocks = tok // BLOCK
    shape4 = (blocks, BLOCK, heads, width)
    init = (jnp.zeros((heads, width, width), jnp.float32), jnp.float32(-1.0))
    step_fn = lambda c, x: light_block(c, x, decay_rates)
    (state_loc, last_loc), outs = lax.scan(
        step_fn,
        init,
        (
            lin_q.reshape(shape4),
            lin_k.reshape(shape4),
            lin_v.reshape(shape4),
            segment_ids.reshape(blocks, BLOCK),
        ),
    )
    local_out = outs.reshape(tok, heads, width)
    mine = lax.axis_index("seq")
    parts = lax.axis_size("seq")
    q0 = (mine * tok).astype(jnp.int32)
    seg_i = segment_ids.astype(jnp.float32)
    last_here = seg_i[tok - 1]
    first_here = (q0 + jnp.sum((seg_i < last_here).astype(jnp.int32))).astype(jnp.float32)
    rows_per = heads * width // parts
    chunks = state_loc.reshape(parts, rows_per, width)
    lane = jnp.arange(width)
    info = jnp.where(lane == 0, last_here, jnp.where(lane == 1, first_here, 0.0))
    info = jnp.broadcast_to(info[None, None, :], (parts, 8, width))
    sent = lax.all_to_all(jnp.concatenate([chunks, info], axis=1), "seq", 0, 0)
    lasts = sent[:, rows_per, 0]
    firsts = sent[:, rows_per, 1]
    idx = jnp.arange(parts)
    last_prev = jnp.where(idx >= 1, jnp.roll(lasts, 1), -1.0)
    rate = decay_rates[(mine * rows_per) // width]
    gap = jnp.maximum(idx[:, None] - 1 - idx[None, :], 0).astype(jnp.float32)
    linked = (idx[None, :] < idx[:, None]) & (lasts[None, :] == last_prev[:, None])
    weight = jnp.where(linked, jnp.exp(-rate * tok * gap), 0.0)
    mixed = jnp.einsum(
        "pj,jrc->prc", weight, sent[:, :rows_per, :], precision=lax.Precision.HIGHEST
    )
    state_in = lax.all_to_all(mixed, "seq", 0, 0).reshape(heads, width, width)
    last_before = last_prev[mine]
    same_doc = (idx < mine) & (lasts == last_before)
    first_before = jnp.min(jnp.where(same_doc, firsts, jnp.float32(tok * parts)))
    last_in = last_before.reshape(1)
    seg_f = segment_ids.astype(jnp.float32)
    pos = jnp.arange(tok).astype(jnp.float32)
    coef = (
        jnp.exp(-decay_rates[None, :] * (pos[:, None] + 1.0))
        * (seg_f == last_in[0]).astype(jnp.float32)[:, None]
    )
    q_three = lin_q.reshape(tok, heads, width)
    q_state = jnp.einsum(
        "thd,hde->the", q_three.astype(jnp.float32), state_in, precision=lax.Precision.HIGHEST
    )
    raw = (local_out + coef[:, :, None] * q_state).reshape(tok, heads * width)
    sums = jnp.sum(raw * raw, axis=1)
    total_sq = lax.psum(sums, "heads")
    count = lax.axis_size("heads") * heads * width
    lin_out = (raw * lax.rsqrt(total_sq / count + 1e-06)[:, None] * norm_gain[None, :]).astype(
        jnp.bfloat16
    )
    shared_heads = soft_k.shape[1] // width
    group = heads // shared_heads
    both = lax.all_gather(jnp.concatenate([soft_k, soft_v], axis=1), "seq", axis=0, tiled=True)
    below = jnp.sum((seg_i[None, :] < seg_i[:, None]).astype(jnp.int32), axis=1)
    starts = jnp.where(
        seg_i == last_before, first_before.astype(jnp.int32), q0 + below
    )
    pieces = []
    for g in range(shared_heads):
        cols = slice(g * group * width, (g + 1) * group * width)
        pieces.append(
            flash_attention(
                soft_q[:, cols],
                both,
                starts,
                q0,
            )
        )
    soft_out = pieces[0] if shared_heads == 1 else jnp.concatenate(pieces, axis=1)
    return (lin_out, soft_out)


def solution(mesh):
    placed = (
        P("seq", "heads"),
        P("seq", "heads"),
        P("seq", "heads"),
        P("heads"),
        P("heads"),
        P("seq", "heads"),
        P("seq", "heads"),
        P("seq", "heads"),
        P("seq"),
    )
    return jax.shard_map(
        body,
        mesh=mesh,
        in_specs=placed,
        out_specs=(P("seq", "heads"), P("seq", "heads")),
        check_vma=False,
    )
```

```python
import math

import jax
import jax.numpy as jnp
from jax import lax
from jax.experimental import pallas as pl
from jax.experimental.pallas import tpu as pltpu
from jax.sharding import PartitionSpec as P

BLOCK = 256
KEY_BLOCK = 1024


def flash_body(sref, q_ref, k_ref, v_ref, st_ref, o_ref, m_ref, l_ref, acc_ref, vx_ref, *, heads, width, scale):
    j = pl.program_id(0)
    lo, hi, flo, fhi, q0 = sref[0], sref[1], sref[2], sref[3], sref[4]
    rows = q_ref.shape[0]
    kb = k_ref.shape[0]

    @pl.when(j == 0)
    def _():
        m_ref[...] = jnp.full(m_ref.shape, -1e30, jnp.float32)
        l_ref[...] = jnp.zeros(l_ref.shape, jnp.float32)
        acc_ref[...] = jnp.zeros(acc_ref.shape, jnp.float32)
        vx_ref[:, width:] = jnp.ones((vx_ref.shape[0], width), vx_ref.dtype)

    def step(masked):
        k = k_ref[...]
        vx_ref[:, :width] = v_ref[...]
        vx = vx_ref[...]
        if masked:
            kpos = j * kb + lax.broadcasted_iota(jnp.int32, (rows, kb), 1)
            qpos = q0 + lax.broadcasted_iota(jnp.int32, (rows, kb), 0)
            valid = (kpos <= qpos) & (kpos >= st_ref[...])
        for h in range(heads):
            q = q_ref[:, h * width:(h + 1) * width]
            s = lax.dot_general(q, k, (((1,), (1,)), ((), ())), preferred_element_type=jnp.float32) * scale
            if masked:
                s = jnp.where(valid, s, -jnp.inf)
            m_prev = m_ref[h]
            m_new = jnp.maximum(m_prev, jnp.max(s, axis=1, keepdims=True))
            corr = jnp.exp2(m_prev - m_new)
            p = jnp.exp2(s - m_new)
            pv = jnp.dot(p.astype(jnp.bfloat16), vx, preferred_element_type=jnp.float32)
            l_ref[h] = l_ref[h] * corr + pv[:, width:width + 1]
            acc_ref[h] = acc_ref[h] * corr + pv[:, :width]
            m_ref[h] = m_new

    inside = (j >= lo) & (j <= hi)
    full = (j >= flo) & (j <= fhi)

    @pl.when(inside & full)
    def _():
        step(False)

    @pl.when(inside & jnp.logical_not(full))
    def _():
        step(True)

    @pl.when(j == pl.num_programs(0) - 1)
    def _():
        for h in range(heads):
            o_ref[:, h * width:(h + 1) * width] = (acc_ref[h] / l_ref[h]).astype(o_ref.dtype)


def flash_attention(q, both, starts, q0):
    rows, total = q.shape
    length = both.shape[0]
    width = both.shape[1] // 2
    heads = total // width
    kb = min(KEY_BLOCK, length)
    nk = length // kb
    scale = math.log2(math.e) / math.sqrt(width)
    first = starts[0]
    last_start = starts[rows - 1]
    lo = first // kb
    hi = (q0 + rows - 1) // kb
    flo = (last_start + kb - 1) // kb
    fhi = (q0 + 1) // kb - 1
    sref = jnp.stack([lo, hi, flo, fhi, q0]).astype(jnp.int32)

    def k_map(j, s):
        return (jnp.minimum(jnp.maximum(j, s[0]), s[1]), 0)

    def v_map(j, s):
        return (jnp.minimum(jnp.maximum(j, s[0]), s[1]), 1)

    kernel = lambda *refs: flash_body(*refs, heads=heads, width=width, scale=scale)
    return pl.pallas_call(
        kernel,
        out_shape=jax.ShapeDtypeStruct((rows, total), jnp.bfloat16),
        grid_spec=pltpu.PrefetchScalarGridSpec(
            num_scalar_prefetch=1,
            grid=(nk,),
            in_specs=[
                pl.BlockSpec((rows, total), lambda j, s: (0, 0)),
                pl.BlockSpec((kb, width), k_map),
                pl.BlockSpec((kb, width), v_map),
                pl.BlockSpec((rows, 1), lambda j, s: (0, 0)),
            ],
            out_specs=pl.BlockSpec((rows, total), lambda j, s: (0, 0)),
            scratch_shapes=[
                pltpu.VMEM((heads, rows, 1), jnp.float32),
                pltpu.VMEM((heads, rows, 1), jnp.float32),
                pltpu.VMEM((heads, rows, width), jnp.float32),
                pltpu.VMEM((kb, 2 * width), jnp.bfloat16),
            ],
        ),
        compiler_params=pltpu.CompilerParams(dimension_semantics=("arbitrary",)),
        cost_estimate=pl.CostEstimate(
            flops=4 * rows * heads * length * width // 2,
            transcendentals=rows * heads * length // 2,
            bytes_accessed=2 * length * width * 2 + 2 * rows * total * 2,
        ),
    )(sref, q, both, both, starts.reshape(rows, 1))


def light_block(carry, inputs, rates):
    state, last_prev = carry
    q_blk, k_blk, v_blk, seg_blk = inputs
    size = q_blk.shape[0]
    seg_f = seg_blk.astype(jnp.float32)
    pos = jnp.arange(size).astype(jnp.float32)
    diff = pos[:, None] - pos[None, :]
    linked = (diff >= 0.0) & (seg_f[:, None] == seg_f[None, :])
    decay = jnp.exp(-rates[:, None, None] * jnp.maximum(diff, 0.0)[None])
    scores = jnp.einsum("thd,shd->hts", q_blk, k_blk, preferred_element_type=jnp.float32)
    weights = jnp.where(linked[None], scores * decay, 0.0).astype(jnp.bfloat16)
    intra = jnp.einsum("hts,shd->thd", weights, v_blk, preferred_element_type=jnp.float32)
    use = (seg_f == last_prev).astype(jnp.float32)
    coef = jnp.exp(-rates[None, :] * (pos[:, None] + 1.0)) * use[:, None]
    q_state = jnp.einsum(
        "thd,hde->the", q_blk.astype(jnp.float32), state, precision=lax.Precision.HIGHEST
    )
    out = intra + coef[:, :, None] * q_state
    last = seg_f[-1]
    k_weight = (
        jnp.exp(-rates[None, :] * (size - 1.0 - pos[:, None]))
        * (seg_f == last).astype(jnp.float32)[:, None]
    )
    k_dec = (k_blk.astype(jnp.float32) * k_weight[:, :, None]).astype(jnp.bfloat16)
    local = jnp.einsum("shd,she->hde", k_dec, v_blk, preferred_element_type=jnp.float32)
    keep = jnp.where(last == last_prev, 1.0, 0.0) * jnp.exp(-rates * size)
    return ((keep[:, None, None] * state + local, last), out)


def body(lin_q, lin_k, lin_v, decay_rates, norm_gain, soft_q, soft_k, soft_v, segment_ids):
    tok = lin_q.shape[0]
    kv_here, lin_q, lin_k, lin_v = lax.optimization_barrier(
        (jnp.concatenate([soft_k, soft_v], axis=1), lin_q, lin_k, lin_v)
    )
    both = lax.all_gather(kv_here, "seq", axis=0, tiled=True)
    heads = decay_rates.shape[0]
    width = lin_q.shape[1] // heads
    blocks = tok // BLOCK
    shape4 = (blocks, BLOCK, heads, width)
    init = (jnp.zeros((heads, width, width), jnp.float32), jnp.float32(-1.0))
    step_fn = lambda c, x: light_block(c, x, decay_rates)
    (state_loc, last_loc), outs = lax.scan(
        step_fn,
        init,
        (
            lin_q.reshape(shape4),
            lin_k.reshape(shape4),
            lin_v.reshape(shape4),
            segment_ids.reshape(blocks, BLOCK),
        ),
    )
    local_out = outs.reshape(tok, heads, width)
    mine = lax.axis_index("seq")
    parts = lax.axis_size("seq")
    q0 = (mine * tok).astype(jnp.int32)
    seg_i = segment_ids.astype(jnp.float32)
    last_here = seg_i[tok - 1]
    first_here = (q0 + jnp.sum((seg_i < last_here).astype(jnp.int32))).astype(jnp.float32)
    rows_per = heads * width // parts
    chunks = state_loc.reshape(parts, rows_per, width)
    lane = jnp.arange(width)
    info = jnp.where(lane == 0, last_here, jnp.where(lane == 1, first_here, 0.0))
    info = jnp.broadcast_to(info[None, None, :], (parts, 8, width))
    sent = lax.all_to_all(jnp.concatenate([chunks, info], axis=1), "seq", 0, 0)
    lasts = sent[:, rows_per, 0]
    firsts = sent[:, rows_per, 1]
    idx = jnp.arange(parts)
    last_prev = jnp.where(idx >= 1, jnp.roll(lasts, 1), -1.0)
    rate = decay_rates[(mine * rows_per) // width]
    gap = jnp.maximum(idx[:, None] - 1 - idx[None, :], 0).astype(jnp.float32)
    linked = (idx[None, :] < idx[:, None]) & (lasts[None, :] == last_prev[:, None])
    weight = jnp.where(linked, jnp.exp(-rate * tok * gap), 0.0)
    mixed = jnp.einsum(
        "pj,jrc->prc", weight, sent[:, :rows_per, :], precision=lax.Precision.HIGHEST
    )
    state_in = lax.all_to_all(mixed, "seq", 0, 0).reshape(heads, width, width)
    last_before = last_prev[mine]
    same_doc = (idx < mine) & (lasts == last_before)
    first_before = jnp.min(jnp.where(same_doc, firsts, jnp.float32(tok * parts)))
    last_in = last_before.reshape(1)
    seg_f = segment_ids.astype(jnp.float32)
    pos = jnp.arange(tok).astype(jnp.float32)
    coef = (
        jnp.exp(-decay_rates[None, :] * (pos[:, None] + 1.0))
        * (seg_f == last_in[0]).astype(jnp.float32)[:, None]
    )
    q_three = lin_q.reshape(tok, heads, width)
    q_state = jnp.einsum(
        "thd,hde->the", q_three.astype(jnp.float32), state_in, precision=lax.Precision.HIGHEST
    )
    raw = (local_out + coef[:, :, None] * q_state).reshape(tok, heads * width)
    sums = jnp.sum(raw * raw, axis=1)
    total_sq = lax.psum(sums, "heads")
    count = lax.axis_size("heads") * heads * width
    lin_out = (raw * lax.rsqrt(total_sq / count + 1e-06)[:, None] * norm_gain[None, :]).astype(
        jnp.bfloat16
    )
    shared_heads = soft_k.shape[1] // width
    group = heads // shared_heads
    below = jnp.sum((seg_i[None, :] < seg_i[:, None]).astype(jnp.int32), axis=1)
    starts = jnp.where(
        seg_i == last_before, first_before.astype(jnp.int32), q0 + below
    )
    pieces = []
    for g in range(shared_heads):
        cols = slice(g * group * width, (g + 1) * group * width)
        pieces.append(
            flash_attention(
                soft_q[:, cols],
                both,
                starts,
                q0,
            )
        )
    soft_out = pieces[0] if shared_heads == 1 else jnp.concatenate(pieces, axis=1)
    return (lin_out, soft_out)


def solution(mesh):
    placed = (
        P("seq", "heads"),
        P("seq", "heads"),
        P("seq", "heads"),
        P("heads"),
        P("heads"),
        P("seq", "heads"),
        P("seq", "heads"),
        P("seq", "heads"),
        P("seq"),
    )
    return jax.shard_map(
        body,
        mesh=mesh,
        in_specs=placed,
        out_specs=(P("seq", "heads"), P("seq", "heads")),
        check_vma=False,
    )
```

```python
import math

import jax
import jax.numpy as jnp
from jax import lax
from jax.experimental import pallas as pl
from jax.experimental.pallas import tpu as pltpu
from jax.sharding import PartitionSpec as P

BLOCK = 256
SEQ = ("z", "x")
KEY_BLOCK = 1024


def flash_body(sref, q_ref, k_ref, v_ref, st_ref, o_ref, m_ref, l_ref, acc_ref, vx_ref, *, heads, width, scale):
    j = pl.program_id(0)
    lo, hi, flo, fhi, q0 = sref[0], sref[1], sref[2], sref[3], sref[4]
    rows = q_ref.shape[0]
    kb = k_ref.shape[0]

    @pl.when(j == 0)
    def _():
        m_ref[...] = jnp.full(m_ref.shape, -1e30, jnp.float32)
        l_ref[...] = jnp.zeros(l_ref.shape, jnp.float32)
        acc_ref[...] = jnp.zeros(acc_ref.shape, jnp.float32)
        vx_ref[:, width:] = jnp.ones((vx_ref.shape[0], width), vx_ref.dtype)

    def step(masked):
        k = k_ref[...]
        vx_ref[:, :width] = v_ref[...]
        vx = vx_ref[...]
        if masked:
            kpos = j * kb + lax.broadcasted_iota(jnp.int32, (rows, kb), 1)
            qpos = q0 + lax.broadcasted_iota(jnp.int32, (rows, kb), 0)
            valid = (kpos <= qpos) & (kpos >= st_ref[...])
        for h in range(heads):
            q = q_ref[:, h * width:(h + 1) * width]
            s = lax.dot_general(q, k, (((1,), (1,)), ((), ())), preferred_element_type=jnp.float32) * scale
            if masked:
                s = jnp.where(valid, s, -jnp.inf)
            m_prev = m_ref[h]
            m_new = jnp.maximum(m_prev, jnp.max(s, axis=1, keepdims=True))
            corr = jnp.exp2(m_prev - m_new)
            p = jnp.exp2(s - m_new)
            pv = jnp.dot(p.astype(jnp.bfloat16), vx, preferred_element_type=jnp.float32)
            l_ref[h] = l_ref[h] * corr + pv[:, width:width + 1]
            acc_ref[h] = acc_ref[h] * corr + pv[:, :width]
            m_ref[h] = m_new

    inside = (j >= lo) & (j <= hi)
    full = (j >= flo) & (j <= fhi)

    @pl.when(inside & full)
    def _():
        step(False)

    @pl.when(inside & jnp.logical_not(full))
    def _():
        step(True)

    @pl.when(j == pl.num_programs(0) - 1)
    def _():
        for h in range(heads):
            o_ref[:, h * width:(h + 1) * width] = (acc_ref[h] / l_ref[h]).astype(o_ref.dtype)


def flash_attention(q, both, starts, q0):
    rows, total = q.shape
    length = both.shape[0]
    width = both.shape[1] // 2
    heads = total // width
    kb = min(KEY_BLOCK, length)
    nk = length // kb
    scale = math.log2(math.e) / math.sqrt(width)
    first = starts[0]
    last_start = starts[rows - 1]
    lo = first // kb
    hi = (q0 + rows - 1) // kb
    flo = (last_start + kb - 1) // kb
    fhi = (q0 + 1) // kb - 1
    sref = jnp.stack([lo, hi, flo, fhi, q0]).astype(jnp.int32)

    def k_map(j, s):
        return (jnp.minimum(jnp.maximum(j, s[0]), s[1]), 0)

    def v_map(j, s):
        return (jnp.minimum(jnp.maximum(j, s[0]), s[1]), 1)

    kernel = lambda *refs: flash_body(*refs, heads=heads, width=width, scale=scale)
    return pl.pallas_call(
        kernel,
        out_shape=jax.ShapeDtypeStruct((rows, total), jnp.bfloat16),
        grid_spec=pltpu.PrefetchScalarGridSpec(
            num_scalar_prefetch=1,
            grid=(nk,),
            in_specs=[
                pl.BlockSpec((rows, total), lambda j, s: (0, 0)),
                pl.BlockSpec((kb, width), k_map),
                pl.BlockSpec((kb, width), v_map),
                pl.BlockSpec((rows, 1), lambda j, s: (0, 0)),
            ],
            out_specs=pl.BlockSpec((rows, total), lambda j, s: (0, 0)),
            scratch_shapes=[
                pltpu.VMEM((heads, rows, 1), jnp.float32),
                pltpu.VMEM((heads, rows, 1), jnp.float32),
                pltpu.VMEM((heads, rows, width), jnp.float32),
                pltpu.VMEM((kb, 2 * width), jnp.bfloat16),
            ],
        ),
        compiler_params=pltpu.CompilerParams(dimension_semantics=("arbitrary",)),
        cost_estimate=pl.CostEstimate(
            flops=4 * rows * heads * length * width // 2,
            transcendentals=rows * heads * length // 2,
            bytes_accessed=2 * length * width * 2 + 2 * rows * total * 2,
        ),
    )(sref, q, both, both, starts.reshape(rows, 1))


def light_block(carry, inputs, rates):
    state, last_prev = carry
    q_blk, k_blk, v_blk, seg_blk = inputs
    size = q_blk.shape[0]
    seg_f = seg_blk.astype(jnp.float32)
    pos = jnp.arange(size).astype(jnp.float32)
    diff = pos[:, None] - pos[None, :]
    linked = (diff >= 0.0) & (seg_f[:, None] == seg_f[None, :])
    decay = jnp.exp(-rates[:, None, None] * jnp.maximum(diff, 0.0)[None])
    scores = jnp.einsum("thd,shd->hts", q_blk, k_blk, preferred_element_type=jnp.float32)
    weights = jnp.where(linked[None], scores * decay, 0.0).astype(jnp.bfloat16)
    intra = jnp.einsum("hts,shd->thd", weights, v_blk, preferred_element_type=jnp.float32)
    use = (seg_f == last_prev).astype(jnp.float32)
    coef = jnp.exp(-rates[None, :] * (pos[:, None] + 1.0)) * use[:, None]
    q_state = jnp.einsum(
        "thd,hde->the", q_blk.astype(jnp.float32), state, precision=lax.Precision.HIGHEST
    )
    out = intra + coef[:, :, None] * q_state
    last = seg_f[-1]
    k_weight = (
        jnp.exp(-rates[None, :] * (size - 1.0 - pos[:, None]))
        * (seg_f == last).astype(jnp.float32)[:, None]
    )
    k_dec = (k_blk.astype(jnp.float32) * k_weight[:, :, None]).astype(jnp.bfloat16)
    local = jnp.einsum("shd,she->hde", k_dec, v_blk, preferred_element_type=jnp.float32)
    keep = jnp.where(last == last_prev, 1.0, 0.0) * jnp.exp(-rates * size)
    return ((keep[:, None, None] * state + local, last), out)


def body(lin_q, lin_k, lin_v, decay_rates, norm_gain, soft_q, soft_k, soft_v, segment_ids):
    tok = lin_q.shape[0]
    kv_here, lin_q, lin_k, lin_v = lax.optimization_barrier(
        (jnp.concatenate([soft_k, soft_v], axis=1), lin_q, lin_k, lin_v)
    )
    both = lax.all_gather(kv_here, "x", axis=0, tiled=True)
    both = lax.all_gather(both, "z", axis=0, tiled=True)
    heads = decay_rates.shape[0]
    width = lin_q.shape[1] // heads
    blocks = tok // BLOCK
    shape4 = (blocks, BLOCK, heads, width)
    init = (jnp.zeros((heads, width, width), jnp.float32), jnp.float32(-1.0))
    step_fn = lambda c, x: light_block(c, x, decay_rates)
    (state_loc, last_loc), outs = lax.scan(
        step_fn,
        init,
        (
            lin_q.reshape(shape4),
            lin_k.reshape(shape4),
            lin_v.reshape(shape4),
            segment_ids.reshape(blocks, BLOCK),
        ),
    )
    local_out = outs.reshape(tok, heads, width)
    mine = lax.axis_index(SEQ)
    parts = lax.axis_size(SEQ)
    q0 = (mine * tok).astype(jnp.int32)
    seg_i = segment_ids.astype(jnp.float32)
    last_here = seg_i[tok - 1]
    first_here = (q0 + jnp.sum((seg_i < last_here).astype(jnp.int32))).astype(jnp.float32)
    rows_per = heads * width // parts
    chunks = state_loc.reshape(parts, rows_per, width)
    lane = jnp.arange(width)
    info = jnp.where(lane == 0, last_here, jnp.where(lane == 1, first_here, 0.0))
    info = jnp.broadcast_to(info[None, None, :], (parts, 8, width))
    sent = lax.all_to_all(jnp.concatenate([chunks, info], axis=1), SEQ, 0, 0)
    lasts = sent[:, rows_per, 0]
    firsts = sent[:, rows_per, 1]
    idx = jnp.arange(parts)
    last_prev = jnp.where(idx >= 1, jnp.roll(lasts, 1), -1.0)
    rate = decay_rates[(mine * rows_per) // width]
    gap = jnp.maximum(idx[:, None] - 1 - idx[None, :], 0).astype(jnp.float32)
    linked = (idx[None, :] < idx[:, None]) & (lasts[None, :] == last_prev[:, None])
    weight = jnp.where(linked, jnp.exp(-rate * tok * gap), 0.0)
    mixed = jnp.einsum(
        "pj,jrc->prc", weight, sent[:, :rows_per, :], precision=lax.Precision.HIGHEST
    )
    state_in = lax.all_to_all(mixed, SEQ, 0, 0).reshape(heads, width, width)
    last_before = last_prev[mine]
    same_doc = (idx < mine) & (lasts == last_before)
    first_before = jnp.min(jnp.where(same_doc, firsts, jnp.float32(tok * parts)))
    last_in = last_before.reshape(1)
    seg_f = segment_ids.astype(jnp.float32)
    pos = jnp.arange(tok).astype(jnp.float32)
    coef = (
        jnp.exp(-decay_rates[None, :] * (pos[:, None] + 1.0))
        * (seg_f == last_in[0]).astype(jnp.float32)[:, None]
    )
    q_three = lin_q.reshape(tok, heads, width)
    q_state = jnp.einsum(
        "thd,hde->the", q_three.astype(jnp.float32), state_in, precision=lax.Precision.HIGHEST
    )
    raw = (local_out + coef[:, :, None] * q_state).reshape(tok, heads * width)
    sums = jnp.sum(raw * raw, axis=1)
    total_sq = lax.psum(sums, "heads")
    count = lax.axis_size("heads") * heads * width
    lin_out = (raw * lax.rsqrt(total_sq / count + 1e-06)[:, None] * norm_gain[None, :]).astype(
        jnp.bfloat16
    )
    shared_heads = soft_k.shape[1] // width
    group = heads // shared_heads
    below = jnp.sum((seg_i[None, :] < seg_i[:, None]).astype(jnp.int32), axis=1)
    starts = jnp.where(
        seg_i == last_before, first_before.astype(jnp.int32), q0 + below
    )
    pieces = []
    for g in range(shared_heads):
        cols = slice(g * group * width, (g + 1) * group * width)
        pieces.append(
            flash_attention(
                soft_q[:, cols],
                both,
                starts,
                q0,
            )
        )
    soft_out = pieces[0] if shared_heads == 1 else jnp.concatenate(pieces, axis=1)
    return (lin_out, soft_out)


def solution(mesh):
    placed = (
        P(SEQ, "heads"),
        P(SEQ, "heads"),
        P(SEQ, "heads"),
        P("heads"),
        P("heads"),
        P(SEQ, "heads"),
        P(SEQ, "heads"),
        P(SEQ, "heads"),
        P(SEQ),
    )
    devices = mesh.devices
    split = jax.sharding.Mesh(
        devices.reshape(devices.shape[0] // 4, 4, devices.shape[1]), ("z", "x", "heads")
    )
    return jax.shard_map(
        body,
        mesh=split,
        in_specs=placed,
        out_specs=(P(SEQ, "heads"), P(SEQ, "heads")),
        check_vma=False,
    )
```

```python
import math

import jax
import jax.numpy as jnp
from jax import lax
from jax.experimental import pallas as pl
from jax.experimental.pallas import tpu as pltpu
from jax.sharding import PartitionSpec as P

BLOCK = 256
KEY_BLOCK = 1024


def flash_body(sref, q_ref, k_ref, v_ref, st_ref, o_ref, m_ref, l_ref, acc_ref, vx_ref, *, heads, width, scale):
    j = pl.program_id(0)
    lo, hi, flo, fhi, q0 = sref[0], sref[1], sref[2], sref[3], sref[4]
    rows = q_ref.shape[0]
    kb = k_ref.shape[0]

    @pl.when(j == 0)
    def _():
        m_ref[...] = jnp.full(m_ref.shape, -1e30, jnp.float32)
        l_ref[...] = jnp.zeros(l_ref.shape, jnp.float32)
        acc_ref[...] = jnp.zeros(acc_ref.shape, jnp.float32)
        vx_ref[:, width:] = jnp.ones((vx_ref.shape[0], width), vx_ref.dtype)

    def step(masked):
        kt = k_ref[...].T
        vx_ref[:, :width] = v_ref[...]
        vx = vx_ref[...]
        if masked:
            kpos = j * kb + lax.broadcasted_iota(jnp.int32, (rows, kb), 1)
            qpos = q0 + lax.broadcasted_iota(jnp.int32, (rows, kb), 0)
            valid = (kpos <= qpos) & (kpos >= st_ref[...])
        for h in range(heads):
            q = q_ref[:, h * width:(h + 1) * width]
            s = jnp.dot(q, kt, preferred_element_type=jnp.float32) * scale
            if masked:
                s = jnp.where(valid, s, -jnp.inf)
            m_prev = m_ref[h]
            m_new = jnp.maximum(m_prev, jnp.max(s, axis=1, keepdims=True))
            corr = jnp.exp2(m_prev - m_new)
            p = jnp.exp2(s - m_new)
            pv = jnp.dot(p.astype(jnp.bfloat16), vx, preferred_element_type=jnp.float32)
            l_ref[h] = l_ref[h] * corr + pv[:, width:width + 1]
            acc_ref[h] = acc_ref[h] * corr + pv[:, :width]
            m_ref[h] = m_new

    inside = (j >= lo) & (j <= hi)
    full = (j >= flo) & (j <= fhi)

    @pl.when(inside & full)
    def _():
        step(False)

    @pl.when(inside & jnp.logical_not(full))
    def _():
        step(True)

    @pl.when(j == pl.num_programs(0) - 1)
    def _():
        for h in range(heads):
            o_ref[:, h * width:(h + 1) * width] = (acc_ref[h] / l_ref[h]).astype(o_ref.dtype)


def flash_attention(q, both, starts, q0):
    rows, total = q.shape
    length = both.shape[0]
    width = both.shape[1] // 2
    heads = total // width
    kb = min(KEY_BLOCK, length)
    nk = length // kb
    scale = math.log2(math.e) / math.sqrt(width)
    first = starts[0]
    last_start = starts[rows - 1]
    lo = first // kb
    hi = (q0 + rows - 1) // kb
    flo = (last_start + kb - 1) // kb
    fhi = (q0 + 1) // kb - 1
    sref = jnp.stack([lo, hi, flo, fhi, q0]).astype(jnp.int32)

    def k_map(j, s):
        return (jnp.minimum(jnp.maximum(j, s[0]), s[1]), 0)

    def v_map(j, s):
        return (jnp.minimum(jnp.maximum(j, s[0]), s[1]), 1)

    kernel = lambda *refs: flash_body(*refs, heads=heads, width=width, scale=scale)
    return pl.pallas_call(
        kernel,
        out_shape=jax.ShapeDtypeStruct((rows, total), jnp.bfloat16),
        grid_spec=pltpu.PrefetchScalarGridSpec(
            num_scalar_prefetch=1,
            grid=(nk,),
            in_specs=[
                pl.BlockSpec((rows, total), lambda j, s: (0, 0)),
                pl.BlockSpec((kb, width), k_map),
                pl.BlockSpec((kb, width), v_map),
                pl.BlockSpec((rows, 1), lambda j, s: (0, 0)),
            ],
            out_specs=pl.BlockSpec((rows, total), lambda j, s: (0, 0)),
            scratch_shapes=[
                pltpu.VMEM((heads, rows, 1), jnp.float32),
                pltpu.VMEM((heads, rows, 1), jnp.float32),
                pltpu.VMEM((heads, rows, width), jnp.float32),
                pltpu.VMEM((kb, 2 * width), jnp.bfloat16),
            ],
        ),
        compiler_params=pltpu.CompilerParams(dimension_semantics=("arbitrary",)),
        cost_estimate=pl.CostEstimate(
            flops=4 * rows * heads * length * width // 2,
            transcendentals=rows * heads * length // 2,
            bytes_accessed=2 * length * width * 2 + 2 * rows * total * 2,
        ),
    )(sref, q, both, both, starts.reshape(rows, 1))


def light_block(carry, inputs, rates):
    state, last_prev = carry
    q_blk, k_blk, v_blk, seg_blk = inputs
    size = q_blk.shape[0]
    seg_f = seg_blk.astype(jnp.float32)
    pos = jnp.arange(size).astype(jnp.float32)
    diff = pos[:, None] - pos[None, :]
    linked = (diff >= 0.0) & (seg_f[:, None] == seg_f[None, :])
    decay = jnp.exp(-rates[:, None, None] * jnp.maximum(diff, 0.0)[None])
    scores = jnp.einsum("thd,shd->hts", q_blk, k_blk, preferred_element_type=jnp.float32)
    weights = jnp.where(linked[None], scores * decay, 0.0).astype(jnp.bfloat16)
    intra = jnp.einsum("hts,shd->thd", weights, v_blk, preferred_element_type=jnp.float32)
    use = (seg_f == last_prev).astype(jnp.float32)
    coef = jnp.exp(-rates[None, :] * (pos[:, None] + 1.0)) * use[:, None]
    q_state = jnp.einsum(
        "thd,hde->the", q_blk.astype(jnp.float32), state, precision=lax.Precision.HIGHEST
    )
    out = intra + coef[:, :, None] * q_state
    last = seg_f[-1]
    k_weight = (
        jnp.exp(-rates[None, :] * (size - 1.0 - pos[:, None]))
        * (seg_f == last).astype(jnp.float32)[:, None]
    )
    k_dec = (k_blk.astype(jnp.float32) * k_weight[:, :, None]).astype(jnp.bfloat16)
    local = jnp.einsum("shd,she->hde", k_dec, v_blk, preferred_element_type=jnp.float32)
    keep = jnp.where(last == last_prev, 1.0, 0.0) * jnp.exp(-rates * size)
    return ((keep[:, None, None] * state + local, last), out)


def body(lin_q, lin_k, lin_v, decay_rates, norm_gain, soft_q, soft_k, soft_v, segment_ids):
    tok = lin_q.shape[0]
    kv_here, lin_q, lin_k, lin_v = lax.optimization_barrier(
        (jnp.concatenate([soft_k, soft_v], axis=1), lin_q, lin_k, lin_v)
    )
    both = lax.all_gather(kv_here, "seq", axis=0, tiled=True)
    heads = decay_rates.shape[0]
    width = lin_q.shape[1] // heads
    blocks = tok // BLOCK
    shape4 = (blocks, BLOCK, heads, width)
    init = (jnp.zeros((heads, width, width), jnp.float32), jnp.float32(-1.0))
    step_fn = lambda c, x: light_block(c, x, decay_rates)
    (state_loc, last_loc), outs = lax.scan(
        step_fn,
        init,
        (
            lin_q.reshape(shape4),
            lin_k.reshape(shape4),
            lin_v.reshape(shape4),
            segment_ids.reshape(blocks, BLOCK),
        ),
    )
    local_out = outs.reshape(tok, heads, width)
    mine = lax.axis_index("seq")
    parts = lax.axis_size("seq")
    q0 = (mine * tok).astype(jnp.int32)
    seg_i = segment_ids.astype(jnp.float32)
    last_here = seg_i[tok - 1]
    first_here = (q0 + jnp.sum((seg_i < last_here).astype(jnp.int32))).astype(jnp.float32)
    rows_per = heads * width // parts
    chunks = state_loc.reshape(parts, rows_per, width)
    lane = jnp.arange(width)
    info = jnp.where(lane == 0, last_here, jnp.where(lane == 1, first_here, 0.0))
    info = jnp.broadcast_to(info[None, None, :], (parts, 8, width))
    sent = lax.all_to_all(jnp.concatenate([chunks, info], axis=1), "seq", 0, 0)
    lasts = sent[:, rows_per, 0]
    firsts = sent[:, rows_per, 1]
    idx = jnp.arange(parts)
    last_prev = jnp.where(idx >= 1, jnp.roll(lasts, 1), -1.0)
    rate = decay_rates[(mine * rows_per) // width]
    gap = jnp.maximum(idx[:, None] - 1 - idx[None, :], 0).astype(jnp.float32)
    linked = (idx[None, :] < idx[:, None]) & (lasts[None, :] == last_prev[:, None])
    weight = jnp.where(linked, jnp.exp(-rate * tok * gap), 0.0)
    mixed = jnp.einsum(
        "pj,jrc->prc", weight, sent[:, :rows_per, :], precision=lax.Precision.HIGHEST
    )
    state_in = lax.all_to_all(mixed, "seq", 0, 0).reshape(heads, width, width)
    last_before = last_prev[mine]
    same_doc = (idx < mine) & (lasts == last_before)
    first_before = jnp.min(jnp.where(same_doc, firsts, jnp.float32(tok * parts)))
    last_in = last_before.reshape(1)
    seg_f = segment_ids.astype(jnp.float32)
    pos = jnp.arange(tok).astype(jnp.float32)
    coef = (
        jnp.exp(-decay_rates[None, :] * (pos[:, None] + 1.0))
        * (seg_f == last_in[0]).astype(jnp.float32)[:, None]
    )
    q_three = lin_q.reshape(tok, heads, width)
    q_state = jnp.einsum(
        "thd,hde->the", q_three.astype(jnp.float32), state_in, precision=lax.Precision.HIGHEST
    )
    raw = (local_out + coef[:, :, None] * q_state).reshape(tok, heads * width)
    sums = jnp.sum(raw * raw, axis=1)
    total_sq = lax.psum(sums, "heads")
    count = lax.axis_size("heads") * heads * width
    lin_out = (raw * lax.rsqrt(total_sq / count + 1e-06)[:, None] * norm_gain[None, :]).astype(
        jnp.bfloat16
    )
    shared_heads = soft_k.shape[1] // width
    group = heads // shared_heads
    below = jnp.sum((seg_i[None, :] < seg_i[:, None]).astype(jnp.int32), axis=1)
    starts = jnp.where(
        seg_i == last_before, first_before.astype(jnp.int32), q0 + below
    )
    pieces = []
    for g in range(shared_heads):
        cols = slice(g * group * width, (g + 1) * group * width)
        pieces.append(
            flash_attention(
                soft_q[:, cols],
                both,
                starts,
                q0,
            )
        )
    soft_out = pieces[0] if shared_heads == 1 else jnp.concatenate(pieces, axis=1)
    return (lin_out, soft_out)


def solution(mesh):
    placed = (
        P("seq", "heads"),
        P("seq", "heads"),
        P("seq", "heads"),
        P("heads"),
        P("heads"),
        P("seq", "heads"),
        P("seq", "heads"),
        P("seq", "heads"),
        P("seq"),
    )
    return jax.shard_map(
        body,
        mesh=mesh,
        in_specs=placed,
        out_specs=(P("seq", "heads"), P("seq", "heads")),
        check_vma=False,
    )
```

```python
import math

import jax
import jax.numpy as jnp
from jax import lax
from jax.experimental import pallas as pl
from jax.experimental.pallas import tpu as pltpu
from jax.sharding import PartitionSpec as P

BLOCK = 256
KEY_BLOCK = 1024
HEAD_PACK = 2


def flash_body(sref, q_ref, k_ref, v_ref, st_ref, o_ref, qs_ref, m_ref, l_ref, acc_ref, vx_ref, *, heads, width, scale, pack):
    j = pl.program_id(0)
    lo, hi, flo, fhi, q0 = sref[0], sref[1], sref[2], sref[3], sref[4]
    rows = q_ref.shape[0]
    kb = k_ref.shape[0]
    sets = heads // pack

    @pl.when(j == 0)
    def _():
        m_ref[...] = jnp.full(m_ref.shape, -1e30, jnp.float32)
        l_ref[...] = jnp.zeros(l_ref.shape, jnp.float32)
        acc_ref[...] = jnp.zeros(acc_ref.shape, jnp.float32)
        vx_ref[:, width:] = jnp.ones((vx_ref.shape[0], width), vx_ref.dtype)
        for g in range(sets):
            for i in range(pack):
                h = g * pack + i
                qs_ref[g, i * rows:(i + 1) * rows, :] = q_ref[:, h * width:(h + 1) * width]

    def step(masked):
        kt = k_ref[...].T
        vx_ref[:, :width] = v_ref[...]
        vx = vx_ref[...]
        if masked:
            kpos = j * kb + lax.broadcasted_iota(jnp.int32, (pack * rows, kb), 1)
            qpos = q0 + lax.rem(lax.broadcasted_iota(jnp.int32, (pack * rows, kb), 0), rows)
            valid = (kpos <= qpos) & (kpos >= st_ref[...])
        for g in range(sets):
            s = jnp.dot(qs_ref[g], kt, preferred_element_type=jnp.float32) * scale
            if masked:
                s = jnp.where(valid, s, -jnp.inf)
            m_prev = m_ref[g]
            m_new = jnp.maximum(m_prev, jnp.max(s, axis=1, keepdims=True))
            corr = jnp.exp2(m_prev - m_new)
            p = jnp.exp2(s - m_new)
            pv = jnp.dot(p.astype(jnp.bfloat16), vx, preferred_element_type=jnp.float32)
            l_ref[g] = l_ref[g] * corr + pv[:, width:width + 1]
            acc_ref[g] = acc_ref[g] * corr + pv[:, :width]
            m_ref[g] = m_new

    inside = (j >= lo) & (j <= hi)
    full = (j >= flo) & (j <= fhi)

    @pl.when(inside & full)
    def _():
        step(False)

    @pl.when(inside & jnp.logical_not(full))
    def _():
        step(True)

    @pl.when(j == pl.num_programs(0) - 1)
    def _():
        for g in range(sets):
            for i in range(pack):
                h = g * pack + i
                part = slice(i * rows, (i + 1) * rows)
                o_ref[:, h * width:(h + 1) * width] = (
                    acc_ref[g, part, :] / l_ref[g, part, :]
                ).astype(o_ref.dtype)


def flash_attention(q, both, starts, q0):
    rows, total = q.shape
    length = both.shape[0]
    width = both.shape[1] // 2
    heads = total // width
    kb = min(KEY_BLOCK, length)
    nk = length // kb
    scale = math.log2(math.e) / math.sqrt(width)
    first = starts[0]
    last_start = starts[rows - 1]
    lo = first // kb
    hi = (q0 + rows - 1) // kb
    flo = (last_start + kb - 1) // kb
    fhi = (q0 + 1) // kb - 1
    sref = jnp.stack([lo, hi, flo, fhi, q0]).astype(jnp.int32)

    def k_map(j, s):
        return (jnp.minimum(jnp.maximum(j, s[0]), s[1]), 0)

    def v_map(j, s):
        return (jnp.minimum(jnp.maximum(j, s[0]), s[1]), 1)

    pack = HEAD_PACK if heads % HEAD_PACK == 0 else 1
    kernel = lambda *refs: flash_body(*refs, heads=heads, width=width, scale=scale, pack=pack)
    return pl.pallas_call(
        kernel,
        out_shape=jax.ShapeDtypeStruct((rows, total), jnp.bfloat16),
        grid_spec=pltpu.PrefetchScalarGridSpec(
            num_scalar_prefetch=1,
            grid=(nk,),
            in_specs=[
                pl.BlockSpec((rows, total), lambda j, s: (0, 0)),
                pl.BlockSpec((kb, width), k_map),
                pl.BlockSpec((kb, width), v_map),
                pl.BlockSpec((pack * rows, 1), lambda j, s: (0, 0)),
            ],
            out_specs=pl.BlockSpec((rows, total), lambda j, s: (0, 0)),
            scratch_shapes=[
                pltpu.VMEM((heads // pack, pack * rows, width), q.dtype),
                pltpu.VMEM((heads // pack, pack * rows, 1), jnp.float32),
                pltpu.VMEM((heads // pack, pack * rows, 1), jnp.float32),
                pltpu.VMEM((heads // pack, pack * rows, width), jnp.float32),
                pltpu.VMEM((kb, 2 * width), jnp.bfloat16),
            ],
        ),
        compiler_params=pltpu.CompilerParams(dimension_semantics=("arbitrary",)),
        cost_estimate=pl.CostEstimate(
            flops=4 * rows * heads * length * width // 2,
            transcendentals=rows * heads * length // 2,
            bytes_accessed=2 * length * width * 2 + 2 * rows * total * 2,
        ),
    )(sref, q, both, both, jnp.tile(starts, pack).reshape(pack * rows, 1))


def light_block(carry, inputs, rates):
    state, last_prev = carry
    q_blk, k_blk, v_blk, seg_blk = inputs
    size = q_blk.shape[0]
    seg_f = seg_blk.astype(jnp.float32)
    pos = jnp.arange(size).astype(jnp.float32)
    diff = pos[:, None] - pos[None, :]
    linked = (diff >= 0.0) & (seg_f[:, None] == seg_f[None, :])
    decay = jnp.exp(-rates[:, None, None] * jnp.maximum(diff, 0.0)[None])
    scores = jnp.einsum("thd,shd->hts", q_blk, k_blk, preferred_element_type=jnp.float32)
    weights = jnp.where(linked[None], scores * decay, 0.0).astype(jnp.bfloat16)
    intra = jnp.einsum("hts,shd->thd", weights, v_blk, preferred_element_type=jnp.float32)
    use = (seg_f == last_prev).astype(jnp.float32)
    coef = jnp.exp(-rates[None, :] * (pos[:, None] + 1.0)) * use[:, None]
    q_state = jnp.einsum(
        "thd,hde->the", q_blk.astype(jnp.float32), state, precision=lax.Precision.HIGHEST
    )
    out = intra + coef[:, :, None] * q_state
    last = seg_f[-1]
    k_weight = (
        jnp.exp(-rates[None, :] * (size - 1.0 - pos[:, None]))
        * (seg_f == last).astype(jnp.float32)[:, None]
    )
    k_dec = (k_blk.astype(jnp.float32) * k_weight[:, :, None]).astype(jnp.bfloat16)
    local = jnp.einsum("shd,she->hde", k_dec, v_blk, preferred_element_type=jnp.float32)
    keep = jnp.where(last == last_prev, 1.0, 0.0) * jnp.exp(-rates * size)
    return ((keep[:, None, None] * state + local, last), out)


def body(lin_q, lin_k, lin_v, decay_rates, norm_gain, soft_q, soft_k, soft_v, segment_ids):
    tok = lin_q.shape[0]
    kv_here, lin_q, lin_k, lin_v = lax.optimization_barrier(
        (jnp.concatenate([soft_k, soft_v], axis=1), lin_q, lin_k, lin_v)
    )
    both = lax.all_gather(kv_here, "seq", axis=0, tiled=True)
    heads = decay_rates.shape[0]
    width = lin_q.shape[1] // heads
    blocks = tok // BLOCK
    shape4 = (blocks, BLOCK, heads, width)
    init = (jnp.zeros((heads, width, width), jnp.float32), jnp.float32(-1.0))
    step_fn = lambda c, x: light_block(c, x, decay_rates)
    (state_loc, last_loc), outs = lax.scan(
        step_fn,
        init,
        (
            lin_q.reshape(shape4),
            lin_k.reshape(shape4),
            lin_v.reshape(shape4),
            segment_ids.reshape(blocks, BLOCK),
        ),
    )
    local_out = outs.reshape(tok, heads, width)
    mine = lax.axis_index("seq")
    parts = lax.axis_size("seq")
    q0 = (mine * tok).astype(jnp.int32)
    seg_i = segment_ids.astype(jnp.float32)
    last_here = seg_i[tok - 1]
    first_here = (q0 + jnp.sum((seg_i < last_here).astype(jnp.int32))).astype(jnp.float32)
    rows_per = heads * width // parts
    chunks = state_loc.reshape(parts, rows_per, width)
    lane = jnp.arange(width)
    info = jnp.where(lane == 0, last_here, jnp.where(lane == 1, first_here, 0.0))
    info = jnp.broadcast_to(info[None, None, :], (parts, 8, width))
    sent = lax.all_to_all(jnp.concatenate([chunks, info], axis=1), "seq", 0, 0)
    lasts = sent[:, rows_per, 0]
    firsts = sent[:, rows_per, 1]
    idx = jnp.arange(parts)
    last_prev = jnp.where(idx >= 1, jnp.roll(lasts, 1), -1.0)
    rate = decay_rates[(mine * rows_per) // width]
    gap = jnp.maximum(idx[:, None] - 1 - idx[None, :], 0).astype(jnp.float32)
    linked = (idx[None, :] < idx[:, None]) & (lasts[None, :] == last_prev[:, None])
    weight = jnp.where(linked, jnp.exp(-rate * tok * gap), 0.0)
    mixed = jnp.einsum(
        "pj,jrc->prc", weight, sent[:, :rows_per, :], precision=lax.Precision.HIGHEST
    )
    state_in = lax.all_to_all(mixed, "seq", 0, 0).reshape(heads, width, width)
    last_before = last_prev[mine]
    same_doc = (idx < mine) & (lasts == last_before)
    first_before = jnp.min(jnp.where(same_doc, firsts, jnp.float32(tok * parts)))
    last_in = last_before.reshape(1)
    seg_f = segment_ids.astype(jnp.float32)
    pos = jnp.arange(tok).astype(jnp.float32)
    coef = (
        jnp.exp(-decay_rates[None, :] * (pos[:, None] + 1.0))
        * (seg_f == last_in[0]).astype(jnp.float32)[:, None]
    )
    q_three = lin_q.reshape(tok, heads, width)
    q_state = jnp.einsum(
        "thd,hde->the", q_three.astype(jnp.float32), state_in, precision=lax.Precision.HIGHEST
    )
    raw = (local_out + coef[:, :, None] * q_state).reshape(tok, heads * width)
    sums = jnp.sum(raw * raw, axis=1)
    total_sq = lax.psum(sums, "heads")
    count = lax.axis_size("heads") * heads * width
    lin_out = (raw * lax.rsqrt(total_sq / count + 1e-06)[:, None] * norm_gain[None, :]).astype(
        jnp.bfloat16
    )
    shared_heads = soft_k.shape[1] // width
    group = heads // shared_heads
    below = jnp.sum((seg_i[None, :] < seg_i[:, None]).astype(jnp.int32), axis=1)
    starts = jnp.where(
        seg_i == last_before, first_before.astype(jnp.int32), q0 + below
    )
    pieces = []
    for g in range(shared_heads):
        cols = slice(g * group * width, (g + 1) * group * width)
        pieces.append(
            flash_attention(
                soft_q[:, cols],
                both,
                starts,
                q0,
            )
        )
    soft_out = pieces[0] if shared_heads == 1 else jnp.concatenate(pieces, axis=1)
    return (lin_out, soft_out)


def solution(mesh):
    placed = (
        P("seq", "heads"),
        P("seq", "heads"),
        P("seq", "heads"),
        P("heads"),
        P("heads"),
        P("seq", "heads"),
        P("seq", "heads"),
        P("seq", "heads"),
        P("seq"),
    )
    return jax.shard_map(
        body,
        mesh=mesh,
        in_specs=placed,
        out_specs=(P("seq", "heads"), P("seq", "heads")),
        check_vma=False,
    )
```

```python
import math

import jax
import jax.numpy as jnp
from jax import lax
from jax.experimental import pallas as pl
from jax.experimental.pallas import tpu as pltpu
from jax.sharding import PartitionSpec as P

BLOCK = 256
KEY_BLOCK = 1024
SUB_BLOCK = 512


def flash_body(sref, q_ref, k_ref, v_ref, st_ref, o_ref, m_ref, l_ref, acc_ref, vx_ref, *, heads, width, scale):
    j = pl.program_id(0)
    lo, hi, flo, fhi, q0 = sref[0], sref[1], sref[2], sref[3], sref[4]
    rows = q_ref.shape[0]
    kb = k_ref.shape[0]

    @pl.when(j == 0)
    def _():
        m_ref[...] = jnp.full(m_ref.shape, -1e30, jnp.float32)
        l_ref[...] = jnp.zeros(l_ref.shape, jnp.float32)
        acc_ref[...] = jnp.zeros(acc_ref.shape, jnp.float32)
        vx_ref[:, width:] = jnp.ones((vx_ref.shape[0], width), vx_ref.dtype)

    def step(masked):
        kt = k_ref[...].T
        vx_ref[:, :width] = v_ref[...]
        vx = vx_ref[...]
        if masked:
            kpos = j * kb + lax.broadcasted_iota(jnp.int32, (rows, kb), 1)
            qpos = q0 + lax.broadcasted_iota(jnp.int32, (rows, kb), 0)
            valid = (kpos <= qpos) & (kpos >= st_ref[...])
        sub = min(SUB_BLOCK, kb)
        for h in range(heads):
            q = q_ref[:, h * width:(h + 1) * width]
            for c in range(kb // sub):
                cols = slice(c * sub, (c + 1) * sub)
                s = jnp.dot(q, kt[:, cols], preferred_element_type=jnp.float32) * scale
                if masked:
                    s = jnp.where(valid[:, cols], s, -jnp.inf)
                m_prev = m_ref[h]
                m_new = jnp.maximum(m_prev, jnp.max(s, axis=1, keepdims=True))
                corr = jnp.exp2(m_prev - m_new)
                p = jnp.exp2(s - m_new)
                pv = jnp.dot(p.astype(jnp.bfloat16), vx[cols, :], preferred_element_type=jnp.float32)
                l_ref[h] = l_ref[h] * corr + pv[:, width:width + 1]
                acc_ref[h] = acc_ref[h] * corr + pv[:, :width]
                m_ref[h] = m_new

    inside = (j >= lo) & (j <= hi)
    full = (j >= flo) & (j <= fhi)

    @pl.when(inside & full)
    def _():
        step(False)

    @pl.when(inside & jnp.logical_not(full))
    def _():
        step(True)

    @pl.when(j == pl.num_programs(0) - 1)
    def _():
        for h in range(heads):
            o_ref[:, h * width:(h + 1) * width] = (acc_ref[h] / l_ref[h]).astype(o_ref.dtype)


def flash_attention(q, both, starts, q0):
    rows, total = q.shape
    length = both.shape[0]
    width = both.shape[1] // 2
    heads = total // width
    kb = min(KEY_BLOCK, length)
    nk = length // kb
    scale = math.log2(math.e) / math.sqrt(width)
    first = starts[0]
    last_start = starts[rows - 1]
    lo = first // kb
    hi = (q0 + rows - 1) // kb
    flo = (last_start + kb - 1) // kb
    fhi = (q0 + 1) // kb - 1
    sref = jnp.stack([lo, hi, flo, fhi, q0]).astype(jnp.int32)

    def k_map(j, s):
        return (jnp.minimum(jnp.maximum(j, s[0]), s[1]), 0)

    def v_map(j, s):
        return (jnp.minimum(jnp.maximum(j, s[0]), s[1]), 1)

    kernel = lambda *refs: flash_body(*refs, heads=heads, width=width, scale=scale)
    return pl.pallas_call(
        kernel,
        out_shape=jax.ShapeDtypeStruct((rows, total), jnp.bfloat16),
        grid_spec=pltpu.PrefetchScalarGridSpec(
            num_scalar_prefetch=1,
            grid=(nk,),
            in_specs=[
                pl.BlockSpec((rows, total), lambda j, s: (0, 0)),
                pl.BlockSpec((kb, width), k_map),
                pl.BlockSpec((kb, width), v_map),
                pl.BlockSpec((rows, 1), lambda j, s: (0, 0)),
            ],
            out_specs=pl.BlockSpec((rows, total), lambda j, s: (0, 0)),
            scratch_shapes=[
                pltpu.VMEM((heads, rows, 1), jnp.float32),
                pltpu.VMEM((heads, rows, 1), jnp.float32),
                pltpu.VMEM((heads, rows, width), jnp.float32),
                pltpu.VMEM((kb, 2 * width), jnp.bfloat16),
            ],
        ),
        compiler_params=pltpu.CompilerParams(dimension_semantics=("arbitrary",)),
        cost_estimate=pl.CostEstimate(
            flops=4 * rows * heads * length * width // 2,
            transcendentals=rows * heads * length // 2,
            bytes_accessed=2 * length * width * 2 + 2 * rows * total * 2,
        ),
    )(sref, q, both, both, starts.reshape(rows, 1))


def light_block(carry, inputs, rates):
    state, last_prev = carry
    q_blk, k_blk, v_blk, seg_blk = inputs
    size = q_blk.shape[0]
    seg_f = seg_blk.astype(jnp.float32)
    pos = jnp.arange(size).astype(jnp.float32)
    diff = pos[:, None] - pos[None, :]
    linked = (diff >= 0.0) & (seg_f[:, None] == seg_f[None, :])
    decay = jnp.exp(-rates[:, None, None] * jnp.maximum(diff, 0.0)[None])
    scores = jnp.einsum("thd,shd->hts", q_blk, k_blk, preferred_element_type=jnp.float32)
    weights = jnp.where(linked[None], scores * decay, 0.0).astype(jnp.bfloat16)
    intra = jnp.einsum("hts,shd->thd", weights, v_blk, preferred_element_type=jnp.float32)
    use = (seg_f == last_prev).astype(jnp.float32)
    coef = jnp.exp(-rates[None, :] * (pos[:, None] + 1.0)) * use[:, None]
    q_state = jnp.einsum(
        "thd,hde->the", q_blk.astype(jnp.float32), state, precision=lax.Precision.HIGHEST
    )
    out = intra + coef[:, :, None] * q_state
    last = seg_f[-1]
    k_weight = (
        jnp.exp(-rates[None, :] * (size - 1.0 - pos[:, None]))
        * (seg_f == last).astype(jnp.float32)[:, None]
    )
    k_dec = (k_blk.astype(jnp.float32) * k_weight[:, :, None]).astype(jnp.bfloat16)
    local = jnp.einsum("shd,she->hde", k_dec, v_blk, preferred_element_type=jnp.float32)
    keep = jnp.where(last == last_prev, 1.0, 0.0) * jnp.exp(-rates * size)
    return ((keep[:, None, None] * state + local, last), out)


def body(lin_q, lin_k, lin_v, decay_rates, norm_gain, soft_q, soft_k, soft_v, segment_ids):
    tok = lin_q.shape[0]
    kv_here, lin_q, lin_k, lin_v = lax.optimization_barrier(
        (jnp.concatenate([soft_k, soft_v], axis=1), lin_q, lin_k, lin_v)
    )
    both = lax.all_gather(kv_here, "seq", axis=0, tiled=True)
    heads = decay_rates.shape[0]
    width = lin_q.shape[1] // heads
    blocks = tok // BLOCK
    shape4 = (blocks, BLOCK, heads, width)
    init = (jnp.zeros((heads, width, width), jnp.float32), jnp.float32(-1.0))
    step_fn = lambda c, x: light_block(c, x, decay_rates)
    (state_loc, last_loc), outs = lax.scan(
        step_fn,
        init,
        (
            lin_q.reshape(shape4),
            lin_k.reshape(shape4),
            lin_v.reshape(shape4),
            segment_ids.reshape(blocks, BLOCK),
        ),
    )
    local_out = outs.reshape(tok, heads, width)
    mine = lax.axis_index("seq")
    parts = lax.axis_size("seq")
    q0 = (mine * tok).astype(jnp.int32)
    seg_i = segment_ids.astype(jnp.float32)
    last_here = seg_i[tok - 1]
    first_here = (q0 + jnp.sum((seg_i < last_here).astype(jnp.int32))).astype(jnp.float32)
    rows_per = heads * width // parts
    chunks = state_loc.reshape(parts, rows_per, width)
    lane = jnp.arange(width)
    info = jnp.where(lane == 0, last_here, jnp.where(lane == 1, first_here, 0.0))
    info = jnp.broadcast_to(info[None, None, :], (parts, 8, width))
    sent = lax.all_to_all(jnp.concatenate([chunks, info], axis=1), "seq", 0, 0)
    lasts = sent[:, rows_per, 0]
    firsts = sent[:, rows_per, 1]
    idx = jnp.arange(parts)
    last_prev = jnp.where(idx >= 1, jnp.roll(lasts, 1), -1.0)
    rate = decay_rates[(mine * rows_per) // width]
    gap = jnp.maximum(idx[:, None] - 1 - idx[None, :], 0).astype(jnp.float32)
    linked = (idx[None, :] < idx[:, None]) & (lasts[None, :] == last_prev[:, None])
    weight = jnp.where(linked, jnp.exp(-rate * tok * gap), 0.0)
    mixed = jnp.einsum(
        "pj,jrc->prc", weight, sent[:, :rows_per, :], precision=lax.Precision.HIGHEST
    )
    state_in = lax.all_to_all(mixed, "seq", 0, 0).reshape(heads, width, width)
    last_before = last_prev[mine]
    same_doc = (idx < mine) & (lasts == last_before)
    first_before = jnp.min(jnp.where(same_doc, firsts, jnp.float32(tok * parts)))
    last_in = last_before.reshape(1)
    seg_f = segment_ids.astype(jnp.float32)
    pos = jnp.arange(tok).astype(jnp.float32)
    coef = (
        jnp.exp(-decay_rates[None, :] * (pos[:, None] + 1.0))
        * (seg_f == last_in[0]).astype(jnp.float32)[:, None]
    )
    q_three = lin_q.reshape(tok, heads, width)
    q_state = jnp.einsum(
        "thd,hde->the", q_three.astype(jnp.float32), state_in, precision=lax.Precision.HIGHEST
    )
    raw = (local_out + coef[:, :, None] * q_state).reshape(tok, heads * width)
    sums = jnp.sum(raw * raw, axis=1)
    total_sq = lax.psum(sums, "heads")
    count = lax.axis_size("heads") * heads * width
    lin_out = (raw * lax.rsqrt(total_sq / count + 1e-06)[:, None] * norm_gain[None, :]).astype(
        jnp.bfloat16
    )
    shared_heads = soft_k.shape[1] // width
    group = heads // shared_heads
    below = jnp.sum((seg_i[None, :] < seg_i[:, None]).astype(jnp.int32), axis=1)
    starts = jnp.where(
        seg_i == last_before, first_before.astype(jnp.int32), q0 + below
    )
    pieces = []
    for g in range(shared_heads):
        cols = slice(g * group * width, (g + 1) * group * width)
        pieces.append(
            flash_attention(
                soft_q[:, cols],
                both,
                starts,
                q0,
            )
        )
    soft_out = pieces[0] if shared_heads == 1 else jnp.concatenate(pieces, axis=1)
    return (lin_out, soft_out)


def solution(mesh):
    placed = (
        P("seq", "heads"),
        P("seq", "heads"),
        P("seq", "heads"),
        P("heads"),
        P("heads"),
        P("seq", "heads"),
        P("seq", "heads"),
        P("seq", "heads"),
        P("seq"),
    )
    return jax.shard_map(
        body,
        mesh=mesh,
        in_specs=placed,
        out_specs=(P("seq", "heads"), P("seq", "heads")),
        check_vma=False,
    )
```

```python
import math

import jax
import jax.numpy as jnp
from jax import lax
from jax.experimental import pallas as pl
from jax.experimental.pallas import tpu as pltpu
from jax.sharding import PartitionSpec as P

BLOCK = 256
KEY_BLOCK = 1024


def flash_body(sref, q_ref, k_ref, v_ref, st_ref, o_ref, m_ref, l_ref, acc_ref, vx_ref, *, heads, width, scale):
    j = pl.program_id(0)
    lo, hi, flo, fhi, q0 = sref[0], sref[1], sref[2], sref[3], sref[4]
    rows = q_ref.shape[0]
    kb = k_ref.shape[0]

    @pl.when(j == 0)
    def _():
        m_ref[...] = jnp.full(m_ref.shape, -1e30, jnp.float32)
        l_ref[...] = jnp.zeros(l_ref.shape, jnp.float32)
        acc_ref[...] = jnp.zeros(acc_ref.shape, jnp.float32)
        vx_ref[:, width:] = jnp.ones((vx_ref.shape[0], width), vx_ref.dtype)

    def step(masked):
        kt = k_ref[...].T
        vx_ref[:, :width] = v_ref[...]
        vx = vx_ref[...]
        if masked:
            kpos = j * kb + lax.broadcasted_iota(jnp.int32, (rows, kb), 1)
            if masked == "causal":
                valid = kpos <= q0 + lax.broadcasted_iota(jnp.int32, (rows, kb), 0)
            elif masked == "start":
                valid = kpos >= st_ref[...]
            else:
                qpos = q0 + lax.broadcasted_iota(jnp.int32, (rows, kb), 0)
                valid = (kpos <= qpos) & (kpos >= st_ref[...])
        for h in range(heads):
            q = q_ref[:, h * width:(h + 1) * width]
            s = jnp.dot(q, kt, preferred_element_type=jnp.float32) * scale
            if masked:
                s = jnp.where(valid, s, -jnp.inf)
            m_prev = m_ref[h]
            m_new = jnp.maximum(m_prev, jnp.max(s, axis=1, keepdims=True))
            corr = jnp.exp2(m_prev - m_new)
            p = jnp.exp2(s - m_new)
            pv = jnp.dot(p.astype(jnp.bfloat16), vx, preferred_element_type=jnp.float32)
            l_ref[h] = l_ref[h] * corr + pv[:, width:width + 1]
            acc_ref[h] = acc_ref[h] * corr + pv[:, :width]
            m_ref[h] = m_new

    inside = (j >= lo) & (j <= hi)
    full = (j >= flo) & (j <= fhi)

    @pl.when(inside & full)
    def _():
        step(False)

    late = (j + 1) * kb - 1 > q0
    early = j < flo

    @pl.when(inside & jnp.logical_not(full) & late & early)
    def _():
        step("both")

    @pl.when(inside & jnp.logical_not(full) & late & jnp.logical_not(early))
    def _():
        step("causal")

    @pl.when(inside & jnp.logical_not(full) & jnp.logical_not(late))
    def _():
        step("start")

    @pl.when(j == pl.num_programs(0) - 1)
    def _():
        for h in range(heads):
            o_ref[:, h * width:(h + 1) * width] = (acc_ref[h] / l_ref[h]).astype(o_ref.dtype)


def flash_attention(q, both, starts, q0):
    rows, total = q.shape
    length = both.shape[0]
    width = both.shape[1] // 2
    heads = total // width
    kb = min(KEY_BLOCK, length)
    nk = length // kb
    scale = math.log2(math.e) / math.sqrt(width)
    first = starts[0]
    last_start = starts[rows - 1]
    lo = first // kb
    hi = (q0 + rows - 1) // kb
    flo = (last_start + kb - 1) // kb
    fhi = (q0 + 1) // kb - 1
    sref = jnp.stack([lo, hi, flo, fhi, q0]).astype(jnp.int32)

    def k_map(j, s):
        return (jnp.minimum(jnp.maximum(j, s[0]), s[1]), 0)

    def v_map(j, s):
        return (jnp.minimum(jnp.maximum(j, s[0]), s[1]), 1)

    kernel = lambda *refs: flash_body(*refs, heads=heads, width=width, scale=scale)
    return pl.pallas_call(
        kernel,
        out_shape=jax.ShapeDtypeStruct((rows, total), jnp.bfloat16),
        grid_spec=pltpu.PrefetchScalarGridSpec(
            num_scalar_prefetch=1,
            grid=(nk,),
            in_specs=[
                pl.BlockSpec((rows, total), lambda j, s: (0, 0)),
                pl.BlockSpec((kb, width), k_map),
                pl.BlockSpec((kb, width), v_map),
                pl.BlockSpec((rows, 1), lambda j, s: (0, 0)),
            ],
            out_specs=pl.BlockSpec((rows, total), lambda j, s: (0, 0)),
            scratch_shapes=[
                pltpu.VMEM((heads, rows, 1), jnp.float32),
                pltpu.VMEM((heads, rows, 1), jnp.float32),
                pltpu.VMEM((heads, rows, width), jnp.float32),
                pltpu.VMEM((kb, 2 * width), jnp.bfloat16),
            ],
        ),
        compiler_params=pltpu.CompilerParams(dimension_semantics=("arbitrary",)),
        cost_estimate=pl.CostEstimate(
            flops=4 * rows * heads * length * width // 2,
            transcendentals=rows * heads * length // 2,
            bytes_accessed=2 * length * width * 2 + 2 * rows * total * 2,
        ),
    )(sref, q, both, both, starts.reshape(rows, 1))


def light_block(carry, inputs, rates):
    state, last_prev = carry
    q_blk, k_blk, v_blk, seg_blk = inputs
    size = q_blk.shape[0]
    seg_f = seg_blk.astype(jnp.float32)
    pos = jnp.arange(size).astype(jnp.float32)
    diff = pos[:, None] - pos[None, :]
    linked = (diff >= 0.0) & (seg_f[:, None] == seg_f[None, :])
    decay = jnp.exp(-rates[:, None, None] * jnp.maximum(diff, 0.0)[None])
    scores = jnp.einsum("thd,shd->hts", q_blk, k_blk, preferred_element_type=jnp.float32)
    weights = jnp.where(linked[None], scores * decay, 0.0).astype(jnp.bfloat16)
    intra = jnp.einsum("hts,shd->thd", weights, v_blk, preferred_element_type=jnp.float32)
    use = (seg_f == last_prev).astype(jnp.float32)
    coef = jnp.exp(-rates[None, :] * (pos[:, None] + 1.0)) * use[:, None]
    q_state = jnp.einsum(
        "thd,hde->the", q_blk.astype(jnp.float32), state, precision=lax.Precision.HIGHEST
    )
    out = intra + coef[:, :, None] * q_state
    last = seg_f[-1]
    k_weight = (
        jnp.exp(-rates[None, :] * (size - 1.0 - pos[:, None]))
        * (seg_f == last).astype(jnp.float32)[:, None]
    )
    k_dec = (k_blk.astype(jnp.float32) * k_weight[:, :, None]).astype(jnp.bfloat16)
    local = jnp.einsum("shd,she->hde", k_dec, v_blk, preferred_element_type=jnp.float32)
    keep = jnp.where(last == last_prev, 1.0, 0.0) * jnp.exp(-rates * size)
    return ((keep[:, None, None] * state + local, last), out)


def body(lin_q, lin_k, lin_v, decay_rates, norm_gain, soft_q, soft_k, soft_v, segment_ids):
    tok = lin_q.shape[0]
    kv_here, lin_q, lin_k, lin_v = lax.optimization_barrier(
        (jnp.concatenate([soft_k, soft_v], axis=1), lin_q, lin_k, lin_v)
    )
    both = lax.all_gather(kv_here, "seq", axis=0, tiled=True)
    heads = decay_rates.shape[0]
    width = lin_q.shape[1] // heads
    blocks = tok // BLOCK
    shape4 = (blocks, BLOCK, heads, width)
    init = (jnp.zeros((heads, width, width), jnp.float32), jnp.float32(-1.0))
    step_fn = lambda c, x: light_block(c, x, decay_rates)
    (state_loc, last_loc), outs = lax.scan(
        step_fn,
        init,
        (
            lin_q.reshape(shape4),
            lin_k.reshape(shape4),
            lin_v.reshape(shape4),
            segment_ids.reshape(blocks, BLOCK),
        ),
    )
    local_out = outs.reshape(tok, heads, width)
    mine = lax.axis_index("seq")
    parts = lax.axis_size("seq")
    q0 = (mine * tok).astype(jnp.int32)
    seg_i = segment_ids.astype(jnp.float32)
    last_here = seg_i[tok - 1]
    first_here = (q0 + jnp.sum((seg_i < last_here).astype(jnp.int32))).astype(jnp.float32)
    rows_per = heads * width // parts
    chunks = state_loc.reshape(parts, rows_per, width)
    lane = jnp.arange(width)
    info = jnp.where(lane == 0, last_here, jnp.where(lane == 1, first_here, 0.0))
    info = jnp.broadcast_to(info[None, None, :], (parts, 8, width))
    sent = lax.all_to_all(jnp.concatenate([chunks, info], axis=1), "seq", 0, 0)
    lasts = sent[:, rows_per, 0]
    firsts = sent[:, rows_per, 1]
    idx = jnp.arange(parts)
    last_prev = jnp.where(idx >= 1, jnp.roll(lasts, 1), -1.0)
    rate = decay_rates[(mine * rows_per) // width]
    gap = jnp.maximum(idx[:, None] - 1 - idx[None, :], 0).astype(jnp.float32)
    linked = (idx[None, :] < idx[:, None]) & (lasts[None, :] == last_prev[:, None])
    weight = jnp.where(linked, jnp.exp(-rate * tok * gap), 0.0)
    mixed = jnp.einsum(
        "pj,jrc->prc", weight, sent[:, :rows_per, :], precision=lax.Precision.HIGHEST
    )
    state_in = lax.all_to_all(mixed, "seq", 0, 0).reshape(heads, width, width)
    last_before = last_prev[mine]
    same_doc = (idx < mine) & (lasts == last_before)
    first_before = jnp.min(jnp.where(same_doc, firsts, jnp.float32(tok * parts)))
    last_in = last_before.reshape(1)
    seg_f = segment_ids.astype(jnp.float32)
    pos = jnp.arange(tok).astype(jnp.float32)
    coef = (
        jnp.exp(-decay_rates[None, :] * (pos[:, None] + 1.0))
        * (seg_f == last_in[0]).astype(jnp.float32)[:, None]
    )
    q_three = lin_q.reshape(tok, heads, width)
    q_state = jnp.einsum(
        "thd,hde->the", q_three.astype(jnp.float32), state_in, precision=lax.Precision.HIGHEST
    )
    raw = (local_out + coef[:, :, None] * q_state).reshape(tok, heads * width)
    sums = jnp.sum(raw * raw, axis=1)
    total_sq = lax.psum(sums, "heads")
    count = lax.axis_size("heads") * heads * width
    lin_out = (raw * lax.rsqrt(total_sq / count + 1e-06)[:, None] * norm_gain[None, :]).astype(
        jnp.bfloat16
    )
    shared_heads = soft_k.shape[1] // width
    group = heads // shared_heads
    below = jnp.sum((seg_i[None, :] < seg_i[:, None]).astype(jnp.int32), axis=1)
    starts = jnp.where(
        seg_i == last_before, first_before.astype(jnp.int32), q0 + below
    )
    pieces = []
    for g in range(shared_heads):
        cols = slice(g * group * width, (g + 1) * group * width)
        pieces.append(
            flash_attention(
                soft_q[:, cols],
                both,
                starts,
                q0,
            )
        )
    soft_out = pieces[0] if shared_heads == 1 else jnp.concatenate(pieces, axis=1)
    return (lin_out, soft_out)


def solution(mesh):
    placed = (
        P("seq", "heads"),
        P("seq", "heads"),
        P("seq", "heads"),
        P("heads"),
        P("heads"),
        P("seq", "heads"),
        P("seq", "heads"),
        P("seq", "heads"),
        P("seq"),
    )
    return jax.shard_map(
        body,
        mesh=mesh,
        in_specs=placed,
        out_specs=(P("seq", "heads"), P("seq", "heads")),
        check_vma=False,
    )
```

```python
import math

import jax
import jax.numpy as jnp
from jax import lax
from jax.experimental import pallas as pl
from jax.experimental.pallas import tpu as pltpu
from jax.sharding import PartitionSpec as P

BLOCK = 256
KEY_BLOCK = 2048


def flash_body(sref, q_ref, k_ref, v_ref, st_ref, o_ref, m_ref, l_ref, acc_ref, vx_ref, *, heads, width, scale):
    j = pl.program_id(0)
    lo, hi, flo, fhi, q0 = sref[0], sref[1], sref[2], sref[3], sref[4]
    rows = q_ref.shape[0]
    kb = k_ref.shape[0]

    @pl.when(j == 0)
    def _():
        m_ref[...] = jnp.full(m_ref.shape, -1e30, jnp.float32)
        l_ref[...] = jnp.zeros(l_ref.shape, jnp.float32)
        acc_ref[...] = jnp.zeros(acc_ref.shape, jnp.float32)
        vx_ref[:, width:] = jnp.ones((vx_ref.shape[0], width), vx_ref.dtype)

    def step(masked):
        kt = k_ref[...].T
        vx_ref[:, :width] = v_ref[...]
        vx = vx_ref[...]
        if masked:
            kpos = j * kb + lax.broadcasted_iota(jnp.int32, (rows, kb), 1)
            qpos = q0 + lax.broadcasted_iota(jnp.int32, (rows, kb), 0)
            valid = (kpos <= qpos) & (kpos >= st_ref[...])
        for h in range(heads):
            q = q_ref[:, h * width:(h + 1) * width]
            s = jnp.dot(q, kt, preferred_element_type=jnp.float32) * scale
            if masked:
                s = jnp.where(valid, s, -jnp.inf)
            m_prev = m_ref[h]
            m_new = jnp.maximum(m_prev, jnp.max(s, axis=1, keepdims=True))
            corr = jnp.exp2(m_prev - m_new)
            p = jnp.exp2(s - m_new)
            pv = jnp.dot(p.astype(jnp.bfloat16), vx, preferred_element_type=jnp.float32)
            l_ref[h] = l_ref[h] * corr + pv[:, width:width + 1]
            acc_ref[h] = acc_ref[h] * corr + pv[:, :width]
            m_ref[h] = m_new

    inside = (j >= lo) & (j <= hi)
    full = (j >= flo) & (j <= fhi)

    @pl.when(inside & full)
    def _():
        step(False)

    @pl.when(inside & jnp.logical_not(full))
    def _():
        step(True)

    @pl.when(j == pl.num_programs(0) - 1)
    def _():
        for h in range(heads):
            o_ref[:, h * width:(h + 1) * width] = (acc_ref[h] / l_ref[h]).astype(o_ref.dtype)


def flash_attention(q, both, starts, q0):
    rows, total = q.shape
    length = both.shape[0]
    width = both.shape[1] // 2
    heads = total // width
    kb = min(KEY_BLOCK, length)
    nk = length // kb
    scale = math.log2(math.e) / math.sqrt(width)
    first = starts[0]
    last_start = starts[rows - 1]
    lo = first // kb
    hi = (q0 + rows - 1) // kb
    flo = (last_start + kb - 1) // kb
    fhi = (q0 + 1) // kb - 1
    sref = jnp.stack([lo, hi, flo, fhi, q0]).astype(jnp.int32)

    def k_map(j, s):
        return (jnp.minimum(jnp.maximum(j, s[0]), s[1]), 0)

    def v_map(j, s):
        return (jnp.minimum(jnp.maximum(j, s[0]), s[1]), 1)

    kernel = lambda *refs: flash_body(*refs, heads=heads, width=width, scale=scale)
    return pl.pallas_call(
        kernel,
        out_shape=jax.ShapeDtypeStruct((rows, total), jnp.bfloat16),
        grid_spec=pltpu.PrefetchScalarGridSpec(
            num_scalar_prefetch=1,
            grid=(nk,),
            in_specs=[
                pl.BlockSpec((rows, total), lambda j, s: (0, 0)),
                pl.BlockSpec((kb, width), k_map),
                pl.BlockSpec((kb, width), v_map),
                pl.BlockSpec((rows, 1), lambda j, s: (0, 0)),
            ],
            out_specs=pl.BlockSpec((rows, total), lambda j, s: (0, 0)),
            scratch_shapes=[
                pltpu.VMEM((heads, rows, 1), jnp.float32),
                pltpu.VMEM((heads, rows, 1), jnp.float32),
                pltpu.VMEM((heads, rows, width), jnp.float32),
                pltpu.VMEM((kb, 2 * width), jnp.bfloat16),
            ],
        ),
        compiler_params=pltpu.CompilerParams(dimension_semantics=("arbitrary",)),
        cost_estimate=pl.CostEstimate(
            flops=4 * rows * heads * length * width // 2,
            transcendentals=rows * heads * length // 2,
            bytes_accessed=2 * length * width * 2 + 2 * rows * total * 2,
        ),
    )(sref, q, both, both, starts.reshape(rows, 1))


def light_block(carry, inputs, rates):
    state, last_prev = carry
    q_blk, k_blk, v_blk, seg_blk = inputs
    size = q_blk.shape[0]
    seg_f = seg_blk.astype(jnp.float32)
    pos = jnp.arange(size).astype(jnp.float32)
    diff = pos[:, None] - pos[None, :]
    linked = (diff >= 0.0) & (seg_f[:, None] == seg_f[None, :])
    decay = jnp.exp(-rates[:, None, None] * jnp.maximum(diff, 0.0)[None])
    scores = jnp.einsum("thd,shd->hts", q_blk, k_blk, preferred_element_type=jnp.float32)
    weights = jnp.where(linked[None], scores * decay, 0.0).astype(jnp.bfloat16)
    intra = jnp.einsum("hts,shd->thd", weights, v_blk, preferred_element_type=jnp.float32)
    use = (seg_f == last_prev).astype(jnp.float32)
    coef = jnp.exp(-rates[None, :] * (pos[:, None] + 1.0)) * use[:, None]
    q_state = jnp.einsum(
        "thd,hde->the", q_blk.astype(jnp.float32), state, precision=lax.Precision.HIGHEST
    )
    out = intra + coef[:, :, None] * q_state
    last = seg_f[-1]
    k_weight = (
        jnp.exp(-rates[None, :] * (size - 1.0 - pos[:, None]))
        * (seg_f == last).astype(jnp.float32)[:, None]
    )
    k_dec = (k_blk.astype(jnp.float32) * k_weight[:, :, None]).astype(jnp.bfloat16)
    local = jnp.einsum("shd,she->hde", k_dec, v_blk, preferred_element_type=jnp.float32)
    keep = jnp.where(last == last_prev, 1.0, 0.0) * jnp.exp(-rates * size)
    return ((keep[:, None, None] * state + local, last), out)


def body(lin_q, lin_k, lin_v, decay_rates, norm_gain, soft_q, soft_k, soft_v, segment_ids):
    tok = lin_q.shape[0]
    kv_here, lin_q, lin_k, lin_v = lax.optimization_barrier(
        (jnp.concatenate([soft_k, soft_v], axis=1), lin_q, lin_k, lin_v)
    )
    both = lax.all_gather(kv_here, "seq", axis=0, tiled=True)
    heads = decay_rates.shape[0]
    width = lin_q.shape[1] // heads
    blocks = tok // BLOCK
    shape4 = (blocks, BLOCK, heads, width)
    init = (jnp.zeros((heads, width, width), jnp.float32), jnp.float32(-1.0))
    step_fn = lambda c, x: light_block(c, x, decay_rates)
    (state_loc, last_loc), outs = lax.scan(
        step_fn,
        init,
        (
            lin_q.reshape(shape4),
            lin_k.reshape(shape4),
            lin_v.reshape(shape4),
            segment_ids.reshape(blocks, BLOCK),
        ),
    )
    local_out = outs.reshape(tok, heads, width)
    mine = lax.axis_index("seq")
    parts = lax.axis_size("seq")
    q0 = (mine * tok).astype(jnp.int32)
    seg_i = segment_ids.astype(jnp.float32)
    last_here = seg_i[tok - 1]
    first_here = (q0 + jnp.sum((seg_i < last_here).astype(jnp.int32))).astype(jnp.float32)
    rows_per = heads * width // parts
    chunks = state_loc.reshape(parts, rows_per, width)
    lane = jnp.arange(width)
    info = jnp.where(lane == 0, last_here, jnp.where(lane == 1, first_here, 0.0))
    info = jnp.broadcast_to(info[None, None, :], (parts, 8, width))
    sent = lax.all_to_all(jnp.concatenate([chunks, info], axis=1), "seq", 0, 0)
    lasts = sent[:, rows_per, 0]
    firsts = sent[:, rows_per, 1]
    idx = jnp.arange(parts)
    last_prev = jnp.where(idx >= 1, jnp.roll(lasts, 1), -1.0)
    rate = decay_rates[(mine * rows_per) // width]
    gap = jnp.maximum(idx[:, None] - 1 - idx[None, :], 0).astype(jnp.float32)
    linked = (idx[None, :] < idx[:, None]) & (lasts[None, :] == last_prev[:, None])
    weight = jnp.where(linked, jnp.exp(-rate * tok * gap), 0.0)
    mixed = jnp.einsum(
        "pj,jrc->prc", weight, sent[:, :rows_per, :], precision=lax.Precision.HIGHEST
    )
    state_in = lax.all_to_all(mixed, "seq", 0, 0).reshape(heads, width, width)
    last_before = last_prev[mine]
    same_doc = (idx < mine) & (lasts == last_before)
    first_before = jnp.min(jnp.where(same_doc, firsts, jnp.float32(tok * parts)))
    last_in = last_before.reshape(1)
    seg_f = segment_ids.astype(jnp.float32)
    pos = jnp.arange(tok).astype(jnp.float32)
    coef = (
        jnp.exp(-decay_rates[None, :] * (pos[:, None] + 1.0))
        * (seg_f == last_in[0]).astype(jnp.float32)[:, None]
    )
    q_three = lin_q.reshape(tok, heads, width)
    q_state = jnp.einsum(
        "thd,hde->the", q_three.astype(jnp.float32), state_in, precision=lax.Precision.HIGHEST
    )
    raw = (local_out + coef[:, :, None] * q_state).reshape(tok, heads * width)
    sums = jnp.sum(raw * raw, axis=1)
    total_sq = lax.psum(sums, "heads")
    count = lax.axis_size("heads") * heads * width
    lin_out = (raw * lax.rsqrt(total_sq / count + 1e-06)[:, None] * norm_gain[None, :]).astype(
        jnp.bfloat16
    )
    shared_heads = soft_k.shape[1] // width
    group = heads // shared_heads
    below = jnp.sum((seg_i[None, :] < seg_i[:, None]).astype(jnp.int32), axis=1)
    starts = jnp.where(
        seg_i == last_before, first_before.astype(jnp.int32), q0 + below
    )
    pieces = []
    for g in range(shared_heads):
        cols = slice(g * group * width, (g + 1) * group * width)
        pieces.append(
            flash_attention(
                soft_q[:, cols],
                both,
                starts,
                q0,
            )
        )
    soft_out = pieces[0] if shared_heads == 1 else jnp.concatenate(pieces, axis=1)
    return (lin_out, soft_out)


def solution(mesh):
    placed = (
        P("seq", "heads"),
        P("seq", "heads"),
        P("seq", "heads"),
        P("heads"),
        P("heads"),
        P("seq", "heads"),
        P("seq", "heads"),
        P("seq", "heads"),
        P("seq"),
    )
    return jax.shard_map(
        body,
        mesh=mesh,
        in_specs=placed,
        out_specs=(P("seq", "heads"), P("seq", "heads")),
        check_vma=False,
    )
```

```python
import math

import jax
import jax.numpy as jnp
from jax import lax
from jax.experimental import pallas as pl
from jax.experimental.pallas import tpu as pltpu
from jax.sharding import PartitionSpec as P

BLOCK = 256
KEY_BLOCK = 4096


def flash_body(sref, q_ref, k_ref, v_ref, st_ref, o_ref, m_ref, l_ref, acc_ref, vx_ref, *, heads, width, scale):
    j = pl.program_id(0)
    lo, hi, flo, fhi, q0 = sref[0], sref[1], sref[2], sref[3], sref[4]
    rows = q_ref.shape[0]
    kb = k_ref.shape[0]

    @pl.when(j == 0)
    def _():
        m_ref[...] = jnp.full(m_ref.shape, -1e30, jnp.float32)
        l_ref[...] = jnp.zeros(l_ref.shape, jnp.float32)
        acc_ref[...] = jnp.zeros(acc_ref.shape, jnp.float32)
        vx_ref[:, width:] = jnp.ones((vx_ref.shape[0], width), vx_ref.dtype)

    def step(masked):
        kt = k_ref[...].T
        vx_ref[:, :width] = v_ref[...]
        vx = vx_ref[...]
        if masked:
            kpos = j * kb + lax.broadcasted_iota(jnp.int32, (rows, kb), 1)
            qpos = q0 + lax.broadcasted_iota(jnp.int32, (rows, kb), 0)
            valid = (kpos <= qpos) & (kpos >= st_ref[...])
        for h in range(heads):
            q = q_ref[:, h * width:(h + 1) * width]
            s = jnp.dot(q, kt, preferred_element_type=jnp.float32) * scale
            if masked:
                s = jnp.where(valid, s, -jnp.inf)
            m_prev = m_ref[h]
            m_new = jnp.maximum(m_prev, jnp.max(s, axis=1, keepdims=True))
            corr = jnp.exp2(m_prev - m_new)
            p = jnp.exp2(s - m_new)
            pv = jnp.dot(p.astype(jnp.bfloat16), vx, preferred_element_type=jnp.float32)
            l_ref[h] = l_ref[h] * corr + pv[:, width:width + 1]
            acc_ref[h] = acc_ref[h] * corr + pv[:, :width]
            m_ref[h] = m_new

    inside = (j >= lo) & (j <= hi)
    full = (j >= flo) & (j <= fhi)

    @pl.when(inside & full)
    def _():
        step(False)

    @pl.when(inside & jnp.logical_not(full))
    def _():
        step(True)

    @pl.when(j == pl.num_programs(0) - 1)
    def _():
        for h in range(heads):
            o_ref[:, h * width:(h + 1) * width] = (acc_ref[h] / l_ref[h]).astype(o_ref.dtype)


def flash_attention(q, both, starts, q0):
    rows, total = q.shape
    length = both.shape[0]
    width = both.shape[1] // 2
    heads = total // width
    kb = min(KEY_BLOCK, length)
    nk = length // kb
    scale = math.log2(math.e) / math.sqrt(width)
    first = starts[0]
    last_start = starts[rows - 1]
    lo = first // kb
    hi = (q0 + rows - 1) // kb
    flo = (last_start + kb - 1) // kb
    fhi = (q0 + 1) // kb - 1
    sref = jnp.stack([lo, hi, flo, fhi, q0]).astype(jnp.int32)

    def k_map(j, s):
        return (jnp.minimum(jnp.maximum(j, s[0]), s[1]), 0)

    def v_map(j, s):
        return (jnp.minimum(jnp.maximum(j, s[0]), s[1]), 1)

    kernel = lambda *refs: flash_body(*refs, heads=heads, width=width, scale=scale)
    return pl.pallas_call(
        kernel,
        out_shape=jax.ShapeDtypeStruct((rows, total), jnp.bfloat16),
        grid_spec=pltpu.PrefetchScalarGridSpec(
            num_scalar_prefetch=1,
            grid=(nk,),
            in_specs=[
                pl.BlockSpec((rows, total), lambda j, s: (0, 0)),
                pl.BlockSpec((kb, width), k_map),
                pl.BlockSpec((kb, width), v_map),
                pl.BlockSpec((rows, 1), lambda j, s: (0, 0)),
            ],
            out_specs=pl.BlockSpec((rows, total), lambda j, s: (0, 0)),
            scratch_shapes=[
                pltpu.VMEM((heads, rows, 1), jnp.float32),
                pltpu.VMEM((heads, rows, 1), jnp.float32),
                pltpu.VMEM((heads, rows, width), jnp.float32),
                pltpu.VMEM((kb, 2 * width), jnp.bfloat16),
            ],
        ),
        compiler_params=pltpu.CompilerParams(dimension_semantics=("arbitrary",)),
        cost_estimate=pl.CostEstimate(
            flops=4 * rows * heads * length * width // 2,
            transcendentals=rows * heads * length // 2,
            bytes_accessed=2 * length * width * 2 + 2 * rows * total * 2,
        ),
    )(sref, q, both, both, starts.reshape(rows, 1))


def light_block(carry, inputs, rates):
    state, last_prev = carry
    q_blk, k_blk, v_blk, seg_blk = inputs
    size = q_blk.shape[0]
    seg_f = seg_blk.astype(jnp.float32)
    pos = jnp.arange(size).astype(jnp.float32)
    diff = pos[:, None] - pos[None, :]
    linked = (diff >= 0.0) & (seg_f[:, None] == seg_f[None, :])
    decay = jnp.exp(-rates[:, None, None] * jnp.maximum(diff, 0.0)[None])
    scores = jnp.einsum("thd,shd->hts", q_blk, k_blk, preferred_element_type=jnp.float32)
    weights = jnp.where(linked[None], scores * decay, 0.0).astype(jnp.bfloat16)
    intra = jnp.einsum("hts,shd->thd", weights, v_blk, preferred_element_type=jnp.float32)
    use = (seg_f == last_prev).astype(jnp.float32)
    coef = jnp.exp(-rates[None, :] * (pos[:, None] + 1.0)) * use[:, None]
    q_state = jnp.einsum(
        "thd,hde->the", q_blk.astype(jnp.float32), state, precision=lax.Precision.HIGHEST
    )
    out = intra + coef[:, :, None] * q_state
    last = seg_f[-1]
    k_weight = (
        jnp.exp(-rates[None, :] * (size - 1.0 - pos[:, None]))
        * (seg_f == last).astype(jnp.float32)[:, None]
    )
    k_dec = (k_blk.astype(jnp.float32) * k_weight[:, :, None]).astype(jnp.bfloat16)
    local = jnp.einsum("shd,she->hde", k_dec, v_blk, preferred_element_type=jnp.float32)
    keep = jnp.where(last == last_prev, 1.0, 0.0) * jnp.exp(-rates * size)
    return ((keep[:, None, None] * state + local, last), out)


def body(lin_q, lin_k, lin_v, decay_rates, norm_gain, soft_q, soft_k, soft_v, segment_ids):
    tok = lin_q.shape[0]
    kv_here, lin_q, lin_k, lin_v = lax.optimization_barrier(
        (jnp.concatenate([soft_k, soft_v], axis=1), lin_q, lin_k, lin_v)
    )
    both = lax.all_gather(kv_here, "seq", axis=0, tiled=True)
    heads = decay_rates.shape[0]
    width = lin_q.shape[1] // heads
    blocks = tok // BLOCK
    shape4 = (blocks, BLOCK, heads, width)
    init = (jnp.zeros((heads, width, width), jnp.float32), jnp.float32(-1.0))
    step_fn = lambda c, x: light_block(c, x, decay_rates)
    (state_loc, last_loc), outs = lax.scan(
        step_fn,
        init,
        (
            lin_q.reshape(shape4),
            lin_k.reshape(shape4),
            lin_v.reshape(shape4),
            segment_ids.reshape(blocks, BLOCK),
        ),
    )
    local_out = outs.reshape(tok, heads, width)
    mine = lax.axis_index("seq")
    parts = lax.axis_size("seq")
    q0 = (mine * tok).astype(jnp.int32)
    seg_i = segment_ids.astype(jnp.float32)
    last_here = seg_i[tok - 1]
    first_here = (q0 + jnp.sum((seg_i < last_here).astype(jnp.int32))).astype(jnp.float32)
    rows_per = heads * width // parts
    chunks = state_loc.reshape(parts, rows_per, width)
    lane = jnp.arange(width)
    info = jnp.where(lane == 0, last_here, jnp.where(lane == 1, first_here, 0.0))
    info = jnp.broadcast_to(info[None, None, :], (parts, 8, width))
    sent = lax.all_to_all(jnp.concatenate([chunks, info], axis=1), "seq", 0, 0)
    lasts = sent[:, rows_per, 0]
    firsts = sent[:, rows_per, 1]
    idx = jnp.arange(parts)
    last_prev = jnp.where(idx >= 1, jnp.roll(lasts, 1), -1.0)
    rate = decay_rates[(mine * rows_per) // width]
    gap = jnp.maximum(idx[:, None] - 1 - idx[None, :], 0).astype(jnp.float32)
    linked = (idx[None, :] < idx[:, None]) & (lasts[None, :] == last_prev[:, None])
    weight = jnp.where(linked, jnp.exp(-rate * tok * gap), 0.0)
    mixed = jnp.einsum(
        "pj,jrc->prc", weight, sent[:, :rows_per, :], precision=lax.Precision.HIGHEST
    )
    state_in = lax.all_to_all(mixed, "seq", 0, 0).reshape(heads, width, width)
    last_before = last_prev[mine]
    same_doc = (idx < mine) & (lasts == last_before)
    first_before = jnp.min(jnp.where(same_doc, firsts, jnp.float32(tok * parts)))
    last_in = last_before.reshape(1)
    seg_f = segment_ids.astype(jnp.float32)
    pos = jnp.arange(tok).astype(jnp.float32)
    coef = (
        jnp.exp(-decay_rates[None, :] * (pos[:, None] + 1.0))
        * (seg_f == last_in[0]).astype(jnp.float32)[:, None]
    )
    q_three = lin_q.reshape(tok, heads, width)
    q_state = jnp.einsum(
        "thd,hde->the", q_three.astype(jnp.float32), state_in, precision=lax.Precision.HIGHEST
    )
    raw = (local_out + coef[:, :, None] * q_state).reshape(tok, heads * width)
    sums = jnp.sum(raw * raw, axis=1)
    total_sq = lax.psum(sums, "heads")
    count = lax.axis_size("heads") * heads * width
    lin_out = (raw * lax.rsqrt(total_sq / count + 1e-06)[:, None] * norm_gain[None, :]).astype(
        jnp.bfloat16
    )
    shared_heads = soft_k.shape[1] // width
    group = heads // shared_heads
    below = jnp.sum((seg_i[None, :] < seg_i[:, None]).astype(jnp.int32), axis=1)
    starts = jnp.where(
        seg_i == last_before, first_before.astype(jnp.int32), q0 + below
    )
    pieces = []
    for g in range(shared_heads):
        cols = slice(g * group * width, (g + 1) * group * width)
        pieces.append(
            flash_attention(
                soft_q[:, cols],
                both,
                starts,
                q0,
            )
        )
    soft_out = pieces[0] if shared_heads == 1 else jnp.concatenate(pieces, axis=1)
    return (lin_out, soft_out)


def solution(mesh):
    placed = (
        P("seq", "heads"),
        P("seq", "heads"),
        P("seq", "heads"),
        P("heads"),
        P("heads"),
        P("seq", "heads"),
        P("seq", "heads"),
        P("seq", "heads"),
        P("seq"),
    )
    return jax.shard_map(
        body,
        mesh=mesh,
        in_specs=placed,
        out_specs=(P("seq", "heads"), P("seq", "heads")),
        check_vma=False,
    )
```
